32 devices in a mesh: leaf: 16 (over z, y, x), chip: 2 (over core).
Axes of the slice: x: 2, y: 2, z: 4, core: 2. Of those that a mesh axis runs over, the one named last changes fastest.
Arguments:
- points: bfloat16 [524288, 64], P(('leaf', 'chip')), may hold values from -14 to 14
- direction: float32 [524288, 16], P(('leaf', 'chip')), may hold values from -6 to 6
- ridge: float32 [16], replicated, may hold values from 0.3 to 3
- leaf_basis: bfloat16 [2048, 256, 128], P(('leaf', 'chip')), may hold values from -0.375 to 0.375
- local_basis: bfloat16 [2016, 256, 128], P(('leaf', 'chip')), may hold values from -1 to 1
- top_basis: bfloat16 [31, 256, 128], replicated, may hold values from -1 to 1
- leaf_pick: int32 [2048, 128], P(('leaf', 'chip')), may hold values from 0 to 255, as said below
- local_pick: int32 [2016, 128], P(('leaf', 'chip')), may hold values from 0 to 255, as said below
- top_pick: int32 [31, 128], replicated, may hold values from 0 to 255, as said below
- near_list: int32 [2048, 10], P(('leaf', 'chip')), may hold values from 0 to 2047, as said below
Outputs:
- product: float32 [524288, 16], P(('leaf', 'chip'))
The draws below stay inside these ranges and needn't reach their ends.
Inputs may be any that keep to these rules, and one draw needn't show every extreme that they name: `leaf_pick`: each row names 128 different points of a leaf. `local_pick`: each row names 128 different rows of the children's stacked skeletons. `top_pick`: each row names 128 different rows of the children's stacked skeletons. `near_list`: the first entry of leaf i's list is i; every entry is a leaf of the same device subtree or of the subtree numbered one lower or one higher (subtrees numbered by leaf index times 32 / 16 plus chip index).
All inputs are finite; a program needn't handle non-finite values.
Results may differ from the reference program's by a relative error of at most 0.0065.
Values may be sent and summed in bfloat16 or wider, within the bound.
No kernel may reach another device: no remote copies, remote signals or barrier semaphores. Data moves between devices by JAX's collectives and lax.ppermute only.
A program may use at most 128 MiB of HBM per device.

```python
import math
import jax
import jax.numpy as jnp
from jax import lax

LEAF = 256
RANK = 128
DIM = 64
RHS = 16
NEAR = 10
LEAF_DEV = 64
SUBTREES = 32
LEAVES = 2048
POINTS = 524288


def order_rows(key, rows, width):
    row_keys = jax.random.split(key, rows)
    return jax.vmap(lambda k: jax.random.permutation(k, width))(row_keys).astype(jnp.int32)


def pick_rows(key, rows, width):
    return order_rows(key, rows, width)[:, :RANK]


def interp_rows(order_key, noise_key, rows):
    orders = order_rows(order_key, rows, 2 * RANK)
    slot_of = jnp.argsort(orders, axis=1).astype(jnp.int32)
    columns = jnp.arange(RANK, dtype=jnp.int32)
    identity_part = (slot_of[:, :, None] == columns[None, None, :]).astype(jnp.float32)
    free_rows = (slot_of[:, :, None] >= RANK).astype(jnp.float32)
    spread = 0.643 / math.sqrt(RANK)
    shape = (rows, 2 * RANK, RANK)
    noise_part = jnp.clip(jax.random.normal(noise_key, shape, jnp.float32) * spread, -3.0 * spread, 3.0 * spread)
    return identity_part + free_rows * noise_part


def draw_points(key, part):
    order_key, centre_key, noise_key = jax.random.split(jax.random.fold_in(key, 15), 3)
    ranks = jax.random.permutation(order_key, DIM).astype(jnp.float32)
    scales = 0.1 * jnp.exp(ranks * (math.log(30.0) / max(DIM - 1, 1)))
    shape = (POINTS, DIM)
    centre = jnp.clip(jax.random.normal(centre_key, (DIM,), jnp.float32) * 1.5, -4.5, 4.5)
    noise = jnp.clip(jax.random.normal(noise_key, shape, jnp.float32), -3.0, 3.0)
    return (centre[None, :] + noise * scales[None, :]).astype(jnp.bfloat16)


def draw_leaf_pick(key, part):
    return pick_rows(jax.random.fold_in(key, 11), LEAVES, LEAF)


def draw_local_pick(key, part):
    return pick_rows(jax.random.fold_in(key, 12), SUBTREES * (LEAF_DEV - 1), 2 * RANK)


def draw_top_pick(key, part):
    return pick_rows(jax.random.fold_in(key, 13), SUBTREES - 1, 2 * RANK)


def draw_local_basis(key, part):
    return interp_rows(jax.random.fold_in(key, 12), jax.random.fold_in(key, 22), SUBTREES * (LEAF_DEV - 1)).astype(jnp.bfloat16)


def draw_top_basis(key, part):
    return interp_rows(jax.random.fold_in(key, 13), jax.random.fold_in(key, 23), SUBTREES - 1).astype(jnp.bfloat16)


def draw_near_list(key, part):
    first, second = jax.random.split(jax.random.fold_in(key, 14))
    rows = jnp.arange(LEAVES, dtype=jnp.int32)
    owner = rows // LEAF_DEV
    offset = jax.random.randint(first, (LEAVES, NEAR - 1), -1, 2).astype(jnp.int32)
    target = jnp.clip(owner[:, None] + offset, 0, SUBTREES - 1)
    inside = jax.random.randint(second, (LEAVES, NEAR - 1), 0, LEAF_DEV).astype(jnp.int32)
    return jnp.concatenate([rows[:, None], target * LEAF_DEV + inside], 1).astype(jnp.int32)


def levels(stream_key, shape, cuts, low, largest):
    gain = 1.0
    for position, blocks in cuts:
        draws = jax.random.uniform(jax.random.fold_in(jax.random.fold_in(stream_key, 6), position), (blocks,), jnp.float32, low / len(cuts), largest / len(cuts))
        gain = gain * jnp.repeat(jnp.exp(draws), shape[position] // blocks).reshape((-1,) + (1,) * (len(shape) - 1 - position))
    return gain


def scatter_about(key, extent, scale, bound, pieces=(), kind=jnp.bfloat16):
    level = levels(key, extent, pieces, -0.22, 0.18) if pieces else 1.0
    values = jax.random.normal(key, extent, jnp.float32) * scale * level
    return jnp.minimum(jnp.maximum(values, -bound), bound).astype(kind)


def setup_inputs(seed: int = 0) -> dict:
    keys = jax.random.split(jax.random.key(seed), 11)
    points = draw_points(jax.random.fold_in(keys[10], 71), 0)
    direction = scatter_about(keys[1], (POINTS, RHS), 1.0, 6.0, ((0, 32),), jnp.float32)
    ridge = jnp.clip(jnp.exp(jax.random.uniform(keys[2], (RHS,), jnp.float32, math.log(0.3), math.log(3.0))), 0.3, 3.0)
    leaf_basis = scatter_about(keys[3], (LEAVES, LEAF, RANK), LEAF ** -0.5, 0.375, ((0, 32),))
    local_basis = draw_local_basis(jax.random.fold_in(keys[10], 71), 0)
    top_basis = draw_top_basis(jax.random.fold_in(keys[10], 71), 0)
    leaf_pick = draw_leaf_pick(jax.random.fold_in(keys[10], 71), 0)
    local_pick = draw_local_pick(jax.random.fold_in(keys[10], 71), 0)
    top_pick = draw_top_pick(jax.random.fold_in(keys[10], 71), 0)
    near_list = draw_near_list(jax.random.fold_in(keys[10], 71), 0)
    return {"points": points, "direction": direction, "ridge": ridge, "leaf_basis": leaf_basis, "local_basis": local_basis, "top_basis": top_basis, "leaf_pick": leaf_pick, "local_pick": local_pick, "top_pick": top_pick, "near_list": near_list}


inverse_width = 1.0 / 32.0


def kernel_tile(left, right_points):
    a = left.astype(jnp.float32)
    batch_points = right_points.astype(jnp.float32)
    cross_product = jnp.einsum('...pd,...qd->...pq', a, batch_points)
    left_square_norm = jnp.sum(a * a, -1)
    right_square_norm = jnp.sum(batch_points * batch_points, -1)
    return jnp.exp((2.0 * cross_product - left_square_norm[..., :, None] - right_square_norm[..., None, :]) * inverse_width).astype(jnp.bfloat16)


def level_tables(depth, top_depth, top_table, local_table):
    if depth < top_depth:
        return top_table[2 ** depth - 1:2 ** (depth + 1) - 1]
    inner = depth - top_depth
    reshaped_input = local_table.reshape((SUBTREES, LEAF_DEV - 1) + local_table.shape[1:])
    part = reshaped_input[:, 2 ** inner - 1:2 ** (inner + 1) - 1]
    return part.reshape((-1,) + local_table.shape[1:])


def reference(points, direction, ridge, leaf_basis, local_basis, top_basis, leaf_pick, local_pick, top_pick, near_list):
    coords = points.reshape(LEAVES, LEAF, DIM)
    weights = direction.astype(jnp.bfloat16).reshape(LEAVES, LEAF, RHS)

    def near_block(inputs):
        own, ids = inputs
        nbr = coords[ids]
        nbw = weights[ids].astype(jnp.float32)
        tiles = kernel_tile(own[:, None], nbr).astype(jnp.float32)
        return jnp.einsum('bjpq,bjqr->bpr', tiles, nbw)

    near = lax.map(near_block, (coords.reshape(SUBTREES, LEAF_DEV, LEAF, DIM), near_list.reshape(SUBTREES, LEAF_DEV, NEAR)))
    near = near.reshape(LEAVES, LEAF, RHS)

    total_depth = LEAVES.bit_length() - 1
    top_depth = SUBTREES.bit_length() - 1
    coeff = jnp.einsum('lpk,lpr->lkr', leaf_basis.astype(jnp.float32), weights.astype(jnp.float32)).astype(jnp.bfloat16)
    skel = jnp.take_along_axis(coords, leaf_pick[:, :, None], axis=1)
    terms = {}
    for depth in range(total_depth, 0, -1):
        count = coeff.shape[0]
        tiles = kernel_tile(skel[0::2], skel[1::2]).astype(jnp.float32)
        left_term = jnp.einsum('npq,nqr->npr', tiles, coeff[1::2].astype(jnp.float32))
        right_term = jnp.einsum('npq,npr->nqr', tiles, coeff[0::2].astype(jnp.float32))
        terms[depth] = jnp.stack([left_term, right_term], 1).reshape(count, RANK, RHS)
        basis = level_tables(depth - 1, top_depth, top_basis, local_basis)
        pick = level_tables(depth - 1, top_depth, top_pick, local_pick)
        stacked = coeff.reshape(count // 2, 2 * RANK, RHS).astype(jnp.float32)
        coeff = jnp.einsum('npk,npr->nkr', basis.astype(jnp.float32), stacked).astype(jnp.bfloat16)
        skel = jnp.take_along_axis(skel.reshape(count // 2, 2 * RANK, DIM), pick[:, :, None], axis=1)
    value = jnp.zeros((1, RANK, RHS), jnp.bfloat16)
    for depth in range(1, total_depth + 1):
        basis = level_tables(depth - 1, top_depth, top_basis, local_basis)
        down = jnp.einsum('npk,nkr->npr', basis.astype(jnp.float32), value.astype(jnp.float32))
        down = down.reshape(-1, RANK, RHS)
        value = (terms[depth] + down).astype(jnp.bfloat16)
    far = jnp.einsum('lpk,lkr->lpr', leaf_basis.astype(jnp.float32), value.astype(jnp.float32))
    result = ridge[None, :] * direction + near.reshape(POINTS, RHS) + far.reshape(POINTS, RHS)
    return result
```

```python
import functools
import math

import jax
import jax.numpy as jnp
from jax import lax
from jax.experimental import pallas as pl
from jax.experimental.pallas import tpu as pltpu
from jax.sharding import PartitionSpec as P

f32 = jnp.float32
bf16 = jnp.bfloat16
AXES = ("leaf", "chip")
SCALE = math.log2(math.e) / 32.0
FEAT = 128
GROUP = 8


def dot(a, b, ca=1, cb=0):
    return lax.dot_general(a, b, (((ca,), (cb,)), ((), ())), preferred_element_type=f32)


def square_rows(xf):
    n = jnp.sum(xf * xf, axis=0, keepdims=True)
    hi = n.astype(bf16).astype(f32)
    rest = n - hi
    mid = rest.astype(bf16).astype(f32)
    low = rest - mid
    row = lax.broadcasted_iota(jnp.int32, (16, xf.shape[1]), 0)
    zero = jnp.zeros((), f32)
    neg = jnp.where(row == 0, -hi, jnp.where(row == 1, -mid, jnp.where(row == 2, -low, zero)))
    ones = jnp.where(row < 3, jnp.ones((), f32), zero)
    return neg.astype(bf16), ones.astype(bf16)


def feature_pair(x):
    dim, width = x.shape
    xf = x.astype(f32)
    neg, ones = square_rows(xf)
    pad = jnp.zeros((FEAT - dim - 32, width), bf16)
    left = jnp.concatenate([(xf + xf).astype(bf16), ones, neg, pad], 0)
    right = jnp.concatenate([x, neg, ones, pad], 0)
    return left, right


def swap_form(left, dim):
    half = (left[:dim].astype(f32) * 0.5).astype(bf16)
    return jnp.concatenate([half, left[dim + 16 : dim + 32], left[dim : dim + 16], left[dim + 32 :]], 0)


def selector(pick_row, width):
    rows = lax.broadcasted_iota(jnp.int32, (width, pick_row.shape[1]), 0)
    return jnp.where(rows == pick_row, jnp.ones((), f32), jnp.zeros((), f32)).astype(bf16)


def gauss(right_rows, left_cols):
    s = dot(right_rows, left_cols)
    return jnp.exp2(s * SCALE).astype(bf16)


def grouped(count, group, fn):
    group = min(group, count)

    def body(t, carry):
        for u in range(group):
            fn(t * group + u)
        return carry

    if count == group:
        body(0, 0)
    else:
        lax.fori_loop(0, count // group, body, 0)


def lanes(start, width):
    if isinstance(start, int):
        return pl.ds(start * width, width)
    return pl.ds(pl.multiple_of(start * width, width), width)


def up_kernel(dims, xt, wt, leaf_pick, local_pick, leaf_hbm, local_hbm, at, b, terms, root, lb, nb, coeff, skel, sems):
    count, leaf, rank, dim, cols = dims
    get_leaf = pltpu.make_async_copy(leaf_hbm, lb, sems.at[0])
    get_local = pltpu.make_async_copy(local_hbm, nb, sems.at[1])
    get_leaf.start()
    get_local.start()

    def prepare(l):
        left, right = feature_pair(xt[:, lanes(l, leaf)])
        at[l] = left
        b[l] = right.T

    grouped(count, 4, prepare)
    get_leaf.wait()
    base = count - 1

    def leaf_step(l):
        c = dot(wt[:, lanes(l, leaf)], lb[l])
        coeff[:, lanes(base + l, rank)] = c.astype(bf16)
        sel = selector(leaf_pick[pl.ds(l, 1), :], leaf)
        skel[:, lanes(base + l, rank)] = dot(at[l], sel).astype(bf16)

    grouped(count, 4, leaf_step)
    get_local.wait()
    depth = count.bit_length() - 1
    for d in range(depth, 0, -1):
        off = 2**d - 1
        up = 2 ** (d - 1) - 1

        def pair_step(m):
            both = pl.ds((off + 2 * m) * rank, 2 * rank)
            if not isinstance(m, int):
                both = pl.ds(pl.multiple_of((off + 2 * m) * rank, rank), 2 * rank)
            c2 = coeff[:, both]
            s2 = skel[:, both]
            left, right = s2[:, :rank], s2[:, rank:]
            c = dot(c2, nb[up + m])
            sel = selector(local_pick[pl.ds(up + m, 1), :], 2 * rank)
            s = dot(s2, sel)
            coeff[:, lanes(up + m, rank)] = c.astype(bf16)
            skel[:, lanes(up + m, rank)] = s.astype(bf16)
            g = gauss(swap_form(right, dim).T, left)
            term_left = dot(c2[:, rank:], g)
            term_right = dot(c2[:, :rank], g, 1, 1)
            terms[:, lanes(2**d - 2 + 2 * m, rank)] = term_left
            terms[:, lanes(2**d - 1 + 2 * m, rank)] = term_right

        grouped(2 ** (d - 1), 4, pair_step)
    root[:cols, :] = coeff[:, :rank]
    root[cols:, :] = skel[:dim, :rank]


def upward(xt, wt, leaf_pick, local_pick, leaf_basis, local_basis):
    count, leaf, rank = leaf_basis.shape
    dim, cols = xt.shape[0], wt.shape[0]
    vm = pl.BlockSpec(memory_space=pltpu.VMEM)
    hbm = pl.BlockSpec(memory_space=pl.ANY)
    return pl.pallas_call(
        functools.partial(up_kernel, (count, leaf, rank, dim, cols)),
        in_specs=[vm, vm, vm, vm, hbm, hbm],
        out_specs=[vm] * 4,
        out_shape=[
            jax.ShapeDtypeStruct((count, FEAT, leaf), bf16),
            jax.ShapeDtypeStruct((count, leaf, FEAT), bf16),
            jax.ShapeDtypeStruct((cols, (2 * count - 2) * rank), f32),
            jax.ShapeDtypeStruct((cols + dim, rank), bf16),
        ],
        scratch_shapes=[
            pltpu.VMEM(leaf_basis.shape, bf16),
            pltpu.VMEM(local_basis.shape, bf16),
            pltpu.VMEM((cols, (2 * count - 1) * rank), bf16),
            pltpu.VMEM((FEAT, (2 * count - 1) * rank), bf16),
            pltpu.SemaphoreType.DMA((2,)),
        ],
        compiler_params=pltpu.CompilerParams(vmem_limit_bytes=48 << 20),
        name="upward",
    )(xt, wt, leaf_pick, local_pick, leaf_basis, local_basis)


def near_pairs(count, entries, lst, pair, at, b, w, acc, tiles):
    h = GROUP
    for u in range(h):
        pair[u] = count * count

    def scan(i, pos):
        for e in range(entries):
            pair[pos + e] = i * count + lst[e, i]
        return pos + lst[entries, i]

    end = lax.fori_loop(0, count, scan, h)
    for u in range(3 * h):
        pair[end + u] = count * count
    total = end - h
    tiles[...] = jnp.zeros_like(tiles)
    acc[...] = jnp.zeros_like(acc)

    def first(k, slot):
        code = pair[k]
        i = code // count
        v = code - i * count
        tiles[slot] = gauss(b[v], at[jnp.where(i < count, i, 0)])

    def second(k, slot):
        code = pair[k]
        i = code // count
        v = code - i * count
        leaf = b.shape[1]
        return i, dot(w[:, lanes(v, leaf)], tiles[slot])

    def body(t, carry):
        for phase in range(2):
            k = (2 * t + phase) * h
            got = []
            for u in range(h):
                first(k + h + u, (1 - phase) * h + u)
                got.append(second(k + u, phase * h + u))
            for i, o in got:
                acc[i] += o
        return carry

    phases = (total + h - 1) // h + 1
    lax.fori_loop(0, (phases + 1) // 2, body, 0)


def near_scratch(count, entries, leaf, cols):
    return [
        pltpu.SMEM((count * entries + entries + 4 * GROUP,), jnp.int32),
        pltpu.VMEM((count + 1, cols, leaf), f32),
        pltpu.VMEM((2 * GROUP, leaf, leaf), bf16),
    ]


def near_own_kernel(count, entries, lst, at, b, w, out, pair, acc, tiles):
    near_pairs(count, entries, lst, pair, at, b, w, acc, tiles)
    leaf = b.shape[1]
    grouped(count, 4, lambda l: out.__setitem__((slice(None), lanes(l, leaf)), acc[l]))


def near_back_kernel(count, entries, lst, xlow, b, w, out, pair, acc, tiles, at):
    leaf = b.shape[1]

    def prepare(l):
        at[l] = feature_pair(xlow[:, lanes(l, leaf)])[0]

    grouped(count, 4, prepare)
    near_pairs(count, entries, lst, pair, at, b, w, acc, tiles)
    grouped(count, 4, lambda l: out.__setitem__((slice(None), lanes(l, leaf)), acc[l].astype(bf16)))


def near_low_kernel(count, entries, lst, at, xlow, w, add1, add2, out, pair, acc, tiles, b):
    leaf = at.shape[2]

    def prepare(l):
        b[l] = feature_pair(xlow[:, lanes(l, leaf)])[1].T

    grouped(count, 4, prepare)
    near_pairs(count, entries, lst, pair, at, b, w, acc, tiles)

    def finish(l):
        s = lanes(l, leaf)
        out[:, s] = acc[l] + add1[:, s] + add2[:, s]

    grouped(count, 4, finish)


def near_call(kernel, lst, operands, count, entries, leaf, cols, dtype, extra, name):
    vm = pl.BlockSpec(memory_space=pltpu.VMEM)
    return pl.pallas_call(
        functools.partial(kernel, count, entries),
        grid_spec=pltpu.PrefetchScalarGridSpec(
            num_scalar_prefetch=1,
            grid=(1,),
            in_specs=[vm] * len(operands),
            out_specs=vm,
            scratch_shapes=near_scratch(count, entries, leaf, cols) + extra,
        ),
        out_shape=jax.ShapeDtypeStruct((cols, count * leaf), dtype),
        compiler_params=pltpu.CompilerParams(vmem_limit_bytes=40 << 20),
        name=name,
    )(lst, *operands)


def down_kernel(dims, pos_ref, gathered, top_pick, ridge, dt, terms, top_hbm, local_hbm, leaf_hbm, out,
                tb, nb, lb, tcoeff, tskel, value, sems):
    count, leaf, rank, dim, cols, subtrees = dims
    get_top = pltpu.make_async_copy(top_hbm, tb, sems.at[0])
    get_local = pltpu.make_async_copy(local_hbm, nb, sems.at[1])
    get_leaf = pltpu.make_async_copy(leaf_hbm, lb, sems.at[2])
    get_top.start()
    get_local.start()
    get_leaf.start()
    pos = pos_ref[0]
    depth = subtrees.bit_length() - 1
    for s in range(subtrees):
        tcoeff[:, lanes(subtrees - 1 + s, rank)] = gathered[s, :cols]
        tskel[:, lanes(subtrees - 1 + s, rank)] = gathered[s, cols:]
    get_top.wait()
    for d in range(depth - 1, 0, -1):
        off = 2 ** (d + 1) - 1
        up = 2**d - 1

        def climb(m):
            start = (off + 2 * m) * rank
            if not isinstance(m, int):
                start = pl.multiple_of(start, rank)
            both = pl.ds(start, 2 * rank)
            c = dot(tcoeff[:, both], tb[up + m])
            sel = selector(top_pick[pl.ds(up + m, 1), :], 2 * rank)
            s = dot(tskel[:, both], sel)
            tcoeff[:, lanes(up + m, rank)] = c.astype(bf16)
            tskel[:, lanes(up + m, rank)] = s.astype(bf16)

        grouped(2**d, 4, climb)
    top_terms = {}
    for d in range(depth, 0, -1):
        mine = pos >> (depth - d)
        other = mine ^ 1
        half = lambda v: (v.astype(f32) * 0.5).astype(bf16)
        own_left = feature_pair(half(tskel[:, lanes(2**d - 1 + mine, rank)]))[0]
        sib_right = feature_pair(half(tskel[:, lanes(2**d - 1 + other, rank)]))[1]
        g = gauss(sib_right.T, own_left)
        top_terms[d] = dot(tcoeff[:, lanes(2**d - 1 + other, rank)], g)
    v = jnp.zeros((cols, rank), bf16)
    for d in range(1, depth + 1):
        parent = pos >> (depth - d + 1)
        down = dot(v, tb[2 ** (d - 1) - 1 + parent], 1, 1)
        right = ((pos >> (depth - d)) & 1) == 1
        v = (top_terms[d] + jnp.where(right, down[:, rank:], down[:, :rank])).astype(bf16)
    value[:, lanes(0, rank)] = v
    get_local.wait()
    local_depth = count.bit_length() - 1
    for d in range(1, local_depth + 1):
        up = 2 ** (d - 1) - 1

        def descend(m):
            down = dot(value[:, lanes(up + m, rank)], nb[up + m], 1, 1)
            start_t, start_v = (2**d - 2 + 2 * m) * rank, (2**d - 1 + 2 * m) * rank
            if not isinstance(m, int):
                start_t, start_v = pl.multiple_of(start_t, rank), pl.multiple_of(start_v, rank)
            value[:, pl.ds(start_v, 2 * rank)] = (terms[:, pl.ds(start_t, 2 * rank)] + down).astype(bf16)

        grouped(2 ** (d - 1), 4, descend)
    get_leaf.wait()
    scale = ridge[...]

    def finish(l):
        s = lanes(l, leaf)
        far = dot(value[:, lanes(count - 1 + l, rank)], lb[l], 1, 1)
        out[:, s] = scale * dt[:, s] + far

    grouped(count, 4, finish)


def downward(pos, gathered, top_pick, ridge, dt, terms, top_basis, local_basis, leaf_basis, dim):
    count, leaf, rank = leaf_basis.shape
    cols = dt.shape[0]
    subtrees = gathered.shape[0]
    vm = pl.BlockSpec(memory_space=pltpu.VMEM)
    hbm = pl.BlockSpec(memory_space=pl.ANY)
    return pl.pallas_call(
        functools.partial(down_kernel, (count, leaf, rank, dim, cols, subtrees)),
        grid_spec=pltpu.PrefetchScalarGridSpec(
            num_scalar_prefetch=1,
            grid=(1,),
            in_specs=[vm] * 5 + [hbm] * 3,
            out_specs=vm,
            scratch_shapes=[
                pltpu.VMEM(top_basis.shape, bf16),
                pltpu.VMEM(local_basis.shape, bf16),
                pltpu.VMEM(leaf_basis.shape, bf16),
                pltpu.VMEM((cols, (2 * subtrees - 1) * rank), bf16),
                pltpu.VMEM((dim, (2 * subtrees - 1) * rank), bf16),
                pltpu.VMEM((cols, (2 * count - 1) * rank), bf16),
                pltpu.SemaphoreType.DMA((3,)),
            ],
        ),
        out_shape=jax.ShapeDtypeStruct(dt.shape, f32),
        compiler_params=pltpu.CompilerParams(vmem_limit_bytes=48 << 20),
        name="downward",
    )(pos, gathered, top_pick, ridge, dt, terms, top_basis, local_basis, leaf_basis)


def class_list(ids, low, count):
    entries = ids.shape[0]
    local = ids - low
    inside = (local >= 0) & (local < count)
    ones = inside.astype(jnp.int32)
    row = [jnp.zeros_like(ones[0])]
    for e in range(entries):
        row.append(row[-1] + ones[e])
    out = []
    for k in range(entries):
        acc = jnp.zeros_like(ones[0])
        for e in range(k, entries):
            acc = acc + jnp.where(inside[e] & (row[e] == k), local[e], 0)
        out.append(acc)
    out.append(row[-1])
    return jnp.stack(out, 0)


def shards(points, direction, ridge, leaf_basis, local_basis, top_basis, leaf_pick, local_pick, top_pick, near_list):
    count, leaf, rank = leaf_basis.shape
    dim, cols = points.shape[1], direction.shape[1]
    entries = near_list.shape[1]
    chips = lax.axis_size("chip")
    subtrees = lax.axis_size("leaf") * chips
    pos = lax.axis_index("leaf") * chips + lax.axis_index("chip")
    upper = [(i, i + 1) for i in range(subtrees - 1)]
    lower = [(i + 1, i) for i in range(subtrees - 1)]

    xt, dt, ids = points.T, direction.T, near_list.T
    x_low = lax.ppermute(xt, AXES, upper)
    wt = dt.astype(bf16)
    list_up = class_list(ids, (pos + 1) * count, count)
    extra = jnp.pad(list_up.astype(bf16), ((0, cols - entries - 1), (0, 128 - count)))
    w_low_all = lax.ppermute(jnp.concatenate([wt, extra], 1), AXES, upper)
    list_own = class_list(ids, pos * count, count)
    list_low = class_list(ids, (pos - 1) * count, count)

    at, b, terms, root = upward(xt, wt, leaf_pick, local_pick, leaf_basis, local_basis)
    spread = jnp.broadcast_to(root[None], (subtrees,) + root.shape)
    gathered = lax.all_to_all(spread, AXES, 0, 0)
    call = functools.partial(near_call, count=count, entries=entries, leaf=leaf, cols=cols)
    near = call(near_own_kernel, list_own, (at, b, wt), dtype=f32, extra=[], name="near_own")

    w_low = w_low_all[:, : count * leaf]
    list_back = w_low_all[: entries + 1, count * leaf : count * leaf + count].astype(jnp.int32)
    back = call(
        near_back_kernel, list_back, (x_low, b, wt), dtype=bf16,
        extra=[pltpu.VMEM((count, FEAT, leaf), bf16)], name="near_back",
    )
    returned = lax.ppermute(back, AXES, lower)
    part = downward(
        pos[None], gathered, top_pick, ridge[:, None], dt, terms, top_basis, local_basis, leaf_basis, dim
    )
    out = call(
        near_low_kernel, list_low, (at, x_low, w_low, near, part), dtype=f32,
        extra=[pltpu.VMEM((count, leaf, FEAT), bf16)], name="near_low",
    )
    return (out + returned.astype(f32)).T


def solution(mesh):
    split = P(AXES, None)
    split3 = P(AXES, None, None)
    return jax.shard_map(
        shards,
        mesh=mesh,
        in_specs=(split, split, P(), split3, split3, P(), split, split, P(), split),
        out_specs=split,
        check_vma=False,
    )
```

```python
import functools
import math

import jax
import jax.numpy as jnp
from jax import lax
from jax.experimental import pallas as pl
from jax.experimental.pallas import tpu as pltpu
from jax.sharding import PartitionSpec as P

f32 = jnp.float32
bf16 = jnp.bfloat16
AXES = ("leaf", "chip")
SCALE = math.log2(math.e) / 32.0
FEAT = 128
GROUP = 8


def dot(a, b, ca=1, cb=0):
    return lax.dot_general(a, b, (((ca,), (cb,)), ((), ())), preferred_element_type=f32)


def square_rows(xf):
    n = jnp.sum(xf * xf, axis=0, keepdims=True)
    hi = n.astype(bf16).astype(f32)
    rest = n - hi
    mid = rest.astype(bf16).astype(f32)
    low = rest - mid
    row = lax.broadcasted_iota(jnp.int32, (16, xf.shape[1]), 0)
    zero = jnp.zeros((), f32)
    neg = jnp.where(row == 0, -hi, jnp.where(row == 1, -mid, jnp.where(row == 2, -low, zero)))
    ones = jnp.where(row < 3, jnp.ones((), f32), zero)
    return neg.astype(bf16), ones.astype(bf16)


def feature_pair(x):
    dim, width = x.shape
    xf = x.astype(f32)
    neg, ones = square_rows(xf)
    pad = jnp.zeros((FEAT - dim - 32, width), bf16)
    left = jnp.concatenate([(xf + xf).astype(bf16), ones, neg, pad], 0)
    right = jnp.concatenate([x, neg, ones, pad], 0)
    return left, right


def swap_form(left, dim):
    half = (left[:dim].astype(f32) * 0.5).astype(bf16)
    return jnp.concatenate([half, left[dim + 16 : dim + 32], left[dim : dim + 16], left[dim + 32 :]], 0)


def selector(pick_row, width):
    rows = lax.broadcasted_iota(jnp.int32, (width, pick_row.shape[1]), 0)
    return jnp.where(rows == pick_row, jnp.ones((), f32), jnp.zeros((), f32)).astype(bf16)


def gauss(right_rows, left_cols):
    s = dot(right_rows, left_cols)
    return jnp.exp2(s * SCALE).astype(bf16)


def grouped(count, group, compute, store):
    group = min(group, count)

    def body(t, carry):
        got = [compute(t * group + u) for u in range(group)]
        for u in range(group):
            store(t * group + u, got[u])
        return carry

    if count == group:
        body(0, 0)
    else:
        lax.fori_loop(0, count // group, body, 0)


def lanes(start, width, number=1):
    if isinstance(start, int):
        return pl.ds(start * width, number * width)
    return pl.ds(pl.multiple_of(start * width, width), number * width)


def up_kernel(dims, xt, wt, leaf_pick, local_pick, leaf_hbm, local_hbm, at, b, terms, root, lb, nb, coeff, skel, sems):
    count, leaf, rank, dim, cols = dims
    get_leaf = pltpu.make_async_copy(leaf_hbm, lb, sems.at[0])
    get_local = pltpu.make_async_copy(local_hbm, nb, sems.at[1])
    get_leaf.start()
    get_local.start()

    def prepare(l):
        left, right = feature_pair(xt[:, lanes(l, leaf)])
        return left, right.T

    def keep(l, got):
        at[l], b[l] = got

    grouped(count, 4, prepare, keep)
    get_leaf.wait()
    base = count - 1

    def leaf_step(l):
        c = dot(wt[:, lanes(l, leaf)], lb[l])
        sel = selector(leaf_pick[pl.ds(l, 1), :], leaf)
        return c.astype(bf16), dot(at[l], sel).astype(bf16)

    def leaf_keep(l, got):
        coeff[:, lanes(base + l, rank)], skel[:, lanes(base + l, rank)] = got

    grouped(count, 8, leaf_step, leaf_keep)
    get_local.wait()
    depth = count.bit_length() - 1
    for d in range(depth, 0, -1):
        off = 2**d - 1
        up = 2 ** (d - 1) - 1

        def pair_step(m):
            both = lanes(off + 2 * m, rank, 2)
            c2 = coeff[:, both]
            s2 = skel[:, both]
            left, right = s2[:, :rank], s2[:, rank:]
            c = dot(c2, nb[up + m])
            sel = selector(local_pick[pl.ds(up + m, 1), :], 2 * rank)
            s = dot(s2, sel)
            g = gauss(swap_form(right, dim).T, left)
            term_left = dot(c2[:, rank:], g)
            term_right = dot(c2[:, :rank], g, 1, 1)
            return c.astype(bf16), s.astype(bf16), term_left, term_right

        def pair_keep(m, got):
            coeff[:, lanes(up + m, rank)] = got[0]
            skel[:, lanes(up + m, rank)] = got[1]
            terms[:, lanes(2**d - 2 + 2 * m, rank)] = got[2]
            terms[:, lanes(2**d - 1 + 2 * m, rank)] = got[3]

        grouped(2 ** (d - 1), 8, pair_step, pair_keep)
    root[:cols, :] = coeff[:, :rank]
    root[cols:, :] = skel[:dim, :rank]


def upward(xt, wt, leaf_pick, local_pick, leaf_basis, local_basis):
    count, leaf, rank = leaf_basis.shape
    dim, cols = xt.shape[0], wt.shape[0]
    vm = pl.BlockSpec(memory_space=pltpu.VMEM)
    hbm = pl.BlockSpec(memory_space=pl.ANY)
    return pl.pallas_call(
        functools.partial(up_kernel, (count, leaf, rank, dim, cols)),
        in_specs=[vm, vm, vm, vm, hbm, hbm],
        out_specs=[vm] * 4,
        out_shape=[
            jax.ShapeDtypeStruct((count, FEAT, leaf), bf16),
            jax.ShapeDtypeStruct((count, leaf, FEAT), bf16),
            jax.ShapeDtypeStruct((cols, (2 * count - 2) * rank), f32),
            jax.ShapeDtypeStruct((cols + dim, rank), bf16),
        ],
        scratch_shapes=[
            pltpu.VMEM(leaf_basis.shape, bf16),
            pltpu.VMEM(local_basis.shape, bf16),
            pltpu.VMEM((cols, (2 * count - 1) * rank), bf16),
            pltpu.VMEM((FEAT, (2 * count - 1) * rank), bf16),
            pltpu.SemaphoreType.DMA((2,)),
        ],
        compiler_params=pltpu.CompilerParams(vmem_limit_bytes=32 << 20),
        name="upward",
    )(xt, wt, leaf_pick, local_pick, leaf_basis, local_basis)


def near_pairs(count, entries, lst, pair, at, b, w, acc, tiles):
    h = GROUP
    for u in range(h):
        pair[u] = count * count

    def scan(i, pos):
        for e in range(entries):
            pair[pos + e] = i * count + lst[e, i]
        return pos + lst[entries, i]

    end = lax.fori_loop(0, count, scan, h)
    for u in range(3 * h):
        pair[end + u] = count * count
    total = end - h
    tiles[...] = jnp.zeros_like(tiles)
    acc[...] = jnp.zeros_like(acc)

    def first(k, slot):
        code = pair[k]
        i = code // count
        v = code - i * count
        tiles[slot] = gauss(b[v], at[jnp.where(i < count, i, 0)])

    def second(k, slot):
        code = pair[k]
        i = code // count
        v = code - i * count
        leaf = b.shape[1]
        return i, dot(w[:, lanes(v, leaf)], tiles[slot])

    def body(t, carry):
        for phase in range(2):
            k = (2 * t + phase) * h
            got = []
            for u in range(h):
                first(k + h + u, (1 - phase) * h + u)
                got.append(second(k + u, phase * h + u))
            for i, o in got:
                acc[i] += o
        return carry

    phases = (total + h - 1) // h + 1
    lax.fori_loop(0, (phases + 1) // 2, body, 0)


def near_scratch(count, entries, leaf, cols):
    return [
        pltpu.SMEM((count * entries + entries + 4 * GROUP,), jnp.int32),
        pltpu.VMEM((count + 1, cols, leaf), f32),
        pltpu.VMEM((2 * GROUP, leaf, leaf), bf16),
    ]


def write_out(out, acc, count, leaf, *more):
    def compute(l):
        return functools.reduce(lambda x, y: x + y[:, lanes(l, leaf)], more, acc[l])

    def store(l, got):
        out[:, lanes(l, leaf)] = got.astype(out.dtype)

    grouped(count, 4, compute, store)


def near_own_kernel(count, entries, lst, at, b, w, out, pair, acc, tiles):
    near_pairs(count, entries, lst, pair, at, b, w, acc, tiles)
    leaf = b.shape[1]
    write_out(out, acc, count, leaf)


def near_back_kernel(count, entries, lst, xlow, b, w, out, pair, acc, tiles, at):
    leaf = b.shape[1]

    def keep(l, got):
        at[l] = got

    grouped(count, 4, lambda l: feature_pair(xlow[:, lanes(l, leaf)])[0], keep)
    near_pairs(count, entries, lst, pair, at, b, w, acc, tiles)
    write_out(out, acc, count, leaf)


def near_low_kernel(count, entries, lst, at, xlow, w, add1, add2, out, pair, acc, tiles, b):
    leaf = at.shape[2]

    def keep(l, got):
        b[l] = got

    grouped(count, 4, lambda l: feature_pair(xlow[:, lanes(l, leaf)])[1].T, keep)
    near_pairs(count, entries, lst, pair, at, b, w, acc, tiles)
    write_out(out, acc, count, leaf, add1, add2)


def near_call(kernel, lst, operands, count, entries, leaf, cols, dtype, extra, name):
    vm = pl.BlockSpec(memory_space=pltpu.VMEM)
    return pl.pallas_call(
        functools.partial(kernel, count, entries),
        grid_spec=pltpu.PrefetchScalarGridSpec(
            num_scalar_prefetch=1,
            grid=(1,),
            in_specs=[vm] * len(operands),
            out_specs=vm,
            scratch_shapes=near_scratch(count, entries, leaf, cols) + extra,
        ),
        out_shape=jax.ShapeDtypeStruct((cols, count * leaf), dtype),
        compiler_params=pltpu.CompilerParams(vmem_limit_bytes=24 << 20),
        name=name,
    )(lst, *operands)


def down_kernel(dims, pos_ref, gathered, top_pick, ridge, dt, terms, top_hbm, local_hbm, leaf_hbm, out,
                tb, nb, lb, tcoeff, tskel, value, sems):
    count, leaf, rank, dim, cols, subtrees = dims
    get_top = pltpu.make_async_copy(top_hbm, tb, sems.at[0])
    get_local = pltpu.make_async_copy(local_hbm, nb, sems.at[1])
    get_leaf = pltpu.make_async_copy(leaf_hbm, lb, sems.at[2])
    get_top.start()
    get_local.start()
    get_leaf.start()
    pos = pos_ref[0]
    depth = subtrees.bit_length() - 1
    for s in range(subtrees):
        tcoeff[:, lanes(subtrees - 1 + s, rank)] = gathered[s, :cols]
        tskel[:, lanes(subtrees - 1 + s, rank)] = gathered[s, cols:]
    get_top.wait()
    for d in range(depth - 1, 0, -1):
        off = 2 ** (d + 1) - 1
        up = 2**d - 1

        def climb(m):
            both = lanes(off + 2 * m, rank, 2)
            c = dot(tcoeff[:, both], tb[up + m])
            sel = selector(top_pick[pl.ds(up + m, 1), :], 2 * rank)
            s = dot(tskel[:, both], sel)
            return c.astype(bf16), s.astype(bf16)

        def climb_keep(m, got):
            tcoeff[:, lanes(up + m, rank)], tskel[:, lanes(up + m, rank)] = got

        grouped(2**d, 8, climb, climb_keep)
    top_terms = {}
    for d in range(depth, 0, -1):
        mine = pos >> (depth - d)
        other = mine ^ 1
        half = lambda v: (v.astype(f32) * 0.5).astype(bf16)
        own_left = feature_pair(half(tskel[:, lanes(2**d - 1 + mine, rank)]))[0]
        sib_right = feature_pair(half(tskel[:, lanes(2**d - 1 + other, rank)]))[1]
        g = gauss(sib_right.T, own_left)
        top_terms[d] = dot(tcoeff[:, lanes(2**d - 1 + other, rank)], g)
    v = jnp.zeros((cols, rank), bf16)
    for d in range(1, depth + 1):
        parent = pos >> (depth - d + 1)
        down = dot(v, tb[2 ** (d - 1) - 1 + parent], 1, 1)
        right = ((pos >> (depth - d)) & 1) == 1
        v = (top_terms[d] + jnp.where(right, down[:, rank:], down[:, :rank])).astype(bf16)
    value[:, lanes(0, rank)] = v
    get_local.wait()
    local_depth = count.bit_length() - 1
    for d in range(1, local_depth + 1):
        up = 2 ** (d - 1) - 1

        def descend(m):
            down = dot(value[:, lanes(up + m, rank)], nb[up + m], 1, 1)
            return (terms[:, lanes(2**d - 2 + 2 * m, rank, 2)] + down).astype(bf16)

        def descend_keep(m, got):
            value[:, lanes(2**d - 1 + 2 * m, rank, 2)] = got

        grouped(2 ** (d - 1), 8, descend, descend_keep)
    get_leaf.wait()
    scale = ridge[...]

    def finish(l):
        far = dot(value[:, lanes(count - 1 + l, rank)], lb[l], 1, 1)
        return scale * dt[:, lanes(l, leaf)] + far

    def finish_keep(l, got):
        out[:, lanes(l, leaf)] = got

    grouped(count, 8, finish, finish_keep)


def downward(pos, gathered, top_pick, ridge, dt, terms, top_basis, local_basis, leaf_basis, dim):
    count, leaf, rank = leaf_basis.shape
    cols = dt.shape[0]
    subtrees = gathered.shape[0]
    vm = pl.BlockSpec(memory_space=pltpu.VMEM)
    hbm = pl.BlockSpec(memory_space=pl.ANY)
    return pl.pallas_call(
        functools.partial(down_kernel, (count, leaf, rank, dim, cols, subtrees)),
        grid_spec=pltpu.PrefetchScalarGridSpec(
            num_scalar_prefetch=1,
            grid=(1,),
            in_specs=[vm] * 5 + [hbm] * 3,
            out_specs=vm,
            scratch_shapes=[
                pltpu.VMEM(top_basis.shape, bf16),
                pltpu.VMEM(local_basis.shape, bf16),
                pltpu.VMEM(leaf_basis.shape, bf16),
                pltpu.VMEM((cols, (2 * subtrees - 1) * rank), bf16),
                pltpu.VMEM((dim, (2 * subtrees - 1) * rank), bf16),
                pltpu.VMEM((cols, (2 * count - 1) * rank), bf16),
                pltpu.SemaphoreType.DMA((3,)),
            ],
        ),
        out_shape=jax.ShapeDtypeStruct(dt.shape, f32),
        compiler_params=pltpu.CompilerParams(vmem_limit_bytes=24 << 20),
        name="downward",
    )(pos, gathered, top_pick, ridge, dt, terms, top_basis, local_basis, leaf_basis)


def class_list(ids, low, count):
    entries = ids.shape[0]
    local = ids - low
    inside = (local >= 0) & (local < count)
    ones = inside.astype(jnp.int32)
    row = [jnp.zeros_like(ones[0])]
    for e in range(entries):
        row.append(row[-1] + ones[e])
    out = []
    for k in range(entries):
        acc = jnp.zeros_like(ones[0])
        for e in range(k, entries):
            acc = acc + jnp.where(inside[e] & (row[e] == k), local[e], 0)
        out.append(acc)
    out.append(row[-1])
    return jnp.stack(out, 0)


def shards(points, direction, ridge, leaf_basis, local_basis, top_basis, leaf_pick, local_pick, top_pick, near_list):
    count, leaf, rank = leaf_basis.shape
    dim, cols = points.shape[1], direction.shape[1]
    entries = near_list.shape[1]
    chips = lax.axis_size("chip")
    subtrees = lax.axis_size("leaf") * chips
    pos = lax.axis_index("leaf") * chips + lax.axis_index("chip")
    upper = [(i, i + 1) for i in range(subtrees - 1)]
    lower = [(i + 1, i) for i in range(subtrees - 1)]

    xt, dt, ids = points.T, direction.T, near_list.T
    x_low = lax.ppermute(xt, AXES, upper)
    wt = dt.astype(bf16)
    list_up = class_list(ids, (pos + 1) * count, count)
    extra = jnp.pad(list_up.astype(bf16), ((0, cols - entries - 1), (0, 128 - count)))
    w_low_all = lax.ppermute(jnp.concatenate([wt, extra], 1), AXES, upper)
    list_own = class_list(ids, pos * count, count)
    list_low = class_list(ids, (pos - 1) * count, count)

    at, b, terms, root = upward(xt, wt, leaf_pick, local_pick, leaf_basis, local_basis)
    spread = jnp.broadcast_to(root[None], (subtrees,) + root.shape)
    gathered = lax.all_to_all(spread, AXES, 0, 0)
    call = functools.partial(near_call, count=count, entries=entries, leaf=leaf, cols=cols)
    near = call(near_own_kernel, list_own, (at, b, wt), dtype=f32, extra=[], name="near_own")

    w_low = w_low_all[:, : count * leaf]
    list_back = w_low_all[: entries + 1, count * leaf : count * leaf + count].astype(jnp.int32)
    back = call(
        near_back_kernel, list_back, (x_low, b, wt), dtype=bf16,
        extra=[pltpu.VMEM((count, FEAT, leaf), bf16)], name="near_back",
    )
    returned = lax.ppermute(back, AXES, lower)
    part = downward(
        pos[None], gathered, top_pick, ridge[:, None], dt, terms, top_basis, local_basis, leaf_basis, dim
    )
    out = call(
        near_low_kernel, list_low, (at, x_low, w_low, near, part), dtype=f32,
        extra=[pltpu.VMEM((count, leaf, FEAT), bf16)], name="near_low",
    )
    return (out + returned.astype(f32)).T


def solution(mesh):
    split = P(AXES, None)
    split3 = P(AXES, None, None)
    return jax.shard_map(
        shards,
        mesh=mesh,
        in_specs=(split, split, P(), split3, split3, P(), split, split, P(), split),
        out_specs=split,
        check_vma=False,
    )
```

```python
import functools
import math

import jax
import jax.numpy as jnp
from jax import lax
from jax.experimental import pallas as pl
from jax.experimental.pallas import tpu as pltpu
from jax.sharding import PartitionSpec as P

f32 = jnp.float32
bf16 = jnp.bfloat16
AXES = ("leaf", "chip")
SCALE = math.log2(math.e) / 32.0
FEAT = 128
GROUP = 16


def dot(a, b, ca=1, cb=0):
    return lax.dot_general(a, b, (((ca,), (cb,)), ((), ())), preferred_element_type=f32)


def copy(src, dst, sem):
    c = pltpu.make_async_copy(src, dst, sem)
    c.start()
    return c


VM = pl.BlockSpec(memory_space=pltpu.VMEM)
HBM = pl.BlockSpec(memory_space=pltpu.HBM)
ANY = pl.BlockSpec(memory_space=pl.ANY)


def square_rows(xf):
    n = jnp.sum(xf * xf, axis=0, keepdims=True)
    hi = n.astype(bf16).astype(f32)
    rest = n - hi
    mid = rest.astype(bf16).astype(f32)
    low = rest - mid
    row = lax.broadcasted_iota(jnp.int32, (16, xf.shape[1]), 0)
    zero = jnp.zeros((), f32)
    neg = jnp.where(row == 0, -hi, jnp.where(row == 1, -mid, jnp.where(row == 2, -low, zero)))
    ones = jnp.where(row < 3, jnp.ones((), f32), zero)
    return neg.astype(bf16), ones.astype(bf16)


def feature_pair(x):
    dim, width = x.shape
    xf = x.astype(f32)
    neg, ones = square_rows(xf)
    pad = jnp.zeros((FEAT - dim - 32, width), bf16)
    left = jnp.concatenate([(xf + xf).astype(bf16), ones, neg, pad], 0)
    right = jnp.concatenate([x, neg, ones, pad], 0)
    return left, right


def swap_form(left, dim):
    half = (left[:dim].astype(f32) * 0.5).astype(bf16)
    return jnp.concatenate([half, left[dim + 16 : dim + 32], left[dim : dim + 16], left[dim + 32 :]], 0)


def selector(pick_row, width):
    rows = lax.broadcasted_iota(jnp.int32, (width, pick_row.shape[1]), 0)
    return jnp.where(rows == pick_row, jnp.ones((), f32), jnp.zeros((), f32)).astype(bf16)


def gauss(right_rows, left_cols):
    s = dot(right_rows, left_cols)
    return jnp.exp2(s * SCALE).astype(bf16)


def grouped(count, group, compute, store, start=0):
    group = min(group, count)

    def body(t, carry):
        got = [compute(start + t * group + u) for u in range(group)]
        for u in range(group):
            store(start + t * group + u, got[u])
        return carry

    if count == group:
        body(0, 0)
    else:
        lax.fori_loop(0, count // group, body, 0)


def lanes(start, width, number=1):
    if isinstance(start, int):
        return pl.ds(start * width, number * width)
    return pl.ds(pl.multiple_of(start * width, width), number * width)


CHUNKS = 4
PAIRS = 8


def up_kernel(dims, x_hbm, d_hbm, ext, leaf_pick, local_pick, leaf_hbm, local_hbm,
              at_hbm, b_hbm, w_hbm, terms_hbm, spread,
              xt, dt, at, b, wt, terms, lb, nb, coeff, skel, tiles, xs, ls, ms, os):
    count, leaf, rank, dim, cols = dims
    part = count // CHUNKS
    seg = lambda c: pl.ds(c * part * leaf, part * leaf)
    own = lambda c: pl.ds(c * part, part)
    get_x = [copy(x_hbm.at[:, seg(c)], xt.at[:, seg(c)], xs.at[c]) for c in range(CHUNKS)]
    get_d = copy(d_hbm, dt, ms.at[0])
    get_leaf = [copy(leaf_hbm.at[own(c)], lb.at[own(c)], ls.at[c]) for c in range(CHUNKS)]
    get_local = copy(local_hbm, nb, ms.at[1])

    def prepare(l):
        left, right = feature_pair(xt[:, lanes(l, leaf)])
        return left, right.T

    def keep(l, got):
        at[l], b[l] = got

    puts = []
    for c in range(CHUNKS):
        get_x[c].wait()
        grouped(part, 8, prepare, keep, c * part)
        puts.append(copy(at.at[own(c)], at_hbm.at[own(c)], os.at[0, c]))
        puts.append(copy(b.at[own(c)], b_hbm.at[own(c)], os.at[1, c]))
    get_d.wait()
    for c in range(CHUNKS):
        wt[:, seg(c)] = dt[:, seg(c)].astype(bf16)
    wt[:, pl.ds(count * leaf, 128)] = ext[...]
    puts.append(copy(wt, w_hbm, ms.at[2]))
    base = count - 1

    def leaf_step(l):
        c = dot(wt[:, lanes(l, leaf)], lb[l])
        sel = selector(leaf_pick[pl.ds(l, 1), :], leaf)
        return c.astype(bf16), dot(at[l], sel).astype(bf16)

    def leaf_keep(l, got):
        coeff[:, lanes(base + l, rank)], skel[:, lanes(base + l, rank)] = got

    for c in range(CHUNKS):
        get_leaf[c].wait()
        grouped(part, 8, leaf_step, leaf_keep, c * part)
    get_local.wait()
    depth = count.bit_length() - 1
    for d in range(depth, 0, -1):
        up = 2 ** (d - 1) - 1

        def climb(j):
            both = lanes(2 * j + 1, rank, 2)
            sel = selector(local_pick[pl.ds(j, 1), :], 2 * rank)
            return dot(coeff[:, both], nb[j]).astype(bf16), dot(skel[:, both], sel).astype(bf16)

        def climb_keep(j, got):
            coeff[:, lanes(j, rank)], skel[:, lanes(j, rank)] = got

        grouped(2 ** (d - 1), 8, climb, climb_keep, up)
    root_c, root_s = coeff[:, :rank], skel[:dim, :rank]
    for s in range(spread.shape[0]):
        spread[s, :cols, :] = root_c
        spread[s, cols:, :] = root_s

    last = count - 2

    def index(j):
        return min(j, last) if isinstance(j, int) else jnp.minimum(j, last)

    def first(j, slot):
        both = skel[:, lanes(2 * index(j) + 1, rank, 2)]
        tiles[slot] = gauss(swap_form(both[:, rank:], dim).T, both[:, :rank])

    def second(j, slot):
        c2 = coeff[:, lanes(2 * index(j) + 1, rank, 2)]
        g = tiles[slot]
        return jnp.concatenate([dot(c2[:, rank:], g), dot(c2[:, :rank], g, 1, 1)], 1)

    for u in range(PAIRS):
        first(u, u)

    def body(t, carry):
        for phase in range(2):
            k = (2 * t + phase) * PAIRS
            got = []
            for u in range(PAIRS):
                first(k + PAIRS + u, (1 - phase) * PAIRS + u)
                got.append(second(k + u, phase * PAIRS + u))
            for u in range(PAIRS):
                terms[:, lanes(2 * index(k + u), rank, 2)] = got[u]
        return carry

    lax.fori_loop(0, count // (2 * PAIRS), body, 0)
    puts.append(copy(terms, terms_hbm, ms.at[3]))
    for p in puts:
        p.wait()


def upward(xt, dt, ext, leaf_pick, local_pick, leaf_basis, local_basis, subtrees):
    count, leaf, rank = leaf_basis.shape
    dim, cols = xt.shape[0], dt.shape[0]
    width = count * leaf + 128
    return pl.pallas_call(
        functools.partial(up_kernel, (count, leaf, rank, dim, cols)),
        in_specs=[HBM, HBM, VM, VM, VM, HBM, HBM],
        out_specs=[HBM] * 4 + [VM],
        out_shape=[
            jax.ShapeDtypeStruct((count, FEAT, leaf), bf16),
            jax.ShapeDtypeStruct((count, leaf, FEAT), bf16),
            jax.ShapeDtypeStruct((cols, width), bf16),
            jax.ShapeDtypeStruct((cols, (2 * count - 2) * rank), f32),
            jax.ShapeDtypeStruct((subtrees, cols + dim, rank), bf16),
        ],
        scratch_shapes=[
            pltpu.VMEM(xt.shape, bf16),
            pltpu.VMEM(dt.shape, f32),
            pltpu.VMEM((count, FEAT, leaf), bf16),
            pltpu.VMEM((count, leaf, FEAT), bf16),
            pltpu.VMEM((cols, width), bf16),
            pltpu.VMEM((cols, (2 * count - 2) * rank), f32),
            pltpu.VMEM(leaf_basis.shape, bf16),
            pltpu.VMEM(local_basis.shape, bf16),
            pltpu.VMEM((cols, (2 * count - 1) * rank), bf16),
            pltpu.VMEM((FEAT, (2 * count - 1) * rank), bf16),
            pltpu.VMEM((2 * PAIRS, rank, rank), bf16),
            pltpu.SemaphoreType.DMA((CHUNKS,)),
            pltpu.SemaphoreType.DMA((CHUNKS,)),
            pltpu.SemaphoreType.DMA((4,)),
            pltpu.SemaphoreType.DMA((2, CHUNKS)),
        ],
        compiler_params=pltpu.CompilerParams(vmem_limit_bytes=60 << 20),
        name="upward",
    )(xt, dt, ext, leaf_pick, local_pick, leaf_basis, local_basis)


def scan_list(count, entries, lst, pair):
    def scan(i, pos):
        for e in range(entries):
            pair[pos + e] = i * count + lst[e, i]
        return pos + lst[entries, i]

    total = lax.fori_loop(0, count, scan, 0)
    for u in range(3 * GROUP):
        pair[total + u] = count * count
    return total


def near_pairs(count, total, pair, at, b, w, acc, tiles):
    h = GROUP
    leaf = b.shape[1]

    def first(k, slot):
        code = pair[k]
        i = code // count
        v = code - i * count
        tiles[slot] = gauss(b[v], at[jnp.where(i < count, i, 0)])

    def second(k, slot):
        code = pair[k]
        i = code // count
        v = code - i * count
        return i, dot(w[:, lanes(v, leaf)], tiles[slot])

    for u in range(h):
        first(u, u)

    def body(t, carry):
        for phase in range(2):
            k = (2 * t + phase) * h
            got = []
            for u in range(h):
                first(k + h + u, (1 - phase) * h + u)
                got.append(second(k + u, phase * h + u))
            for i, o in got:
                acc[i] += o
        return carry

    blocks = (total + h - 1) // h
    lax.fori_loop(0, (blocks + 1) // 2, body, 0)


def write_out(out, acc, count, leaf):
    def store(l, got):
        out[:, lanes(l, leaf)] = got.astype(out.dtype)

    grouped(count, 8, lambda l: acc[l], store)


def near_own_kernel(count, entries, lst, at_hbm, b_hbm, w_hbm, out, pair, acc, tiles, at, b, w, sems):
    gets = [copy(at_hbm, at, sems.at[0]), copy(b_hbm, b, sems.at[1]), copy(w_hbm, w, sems.at[2])]
    total = scan_list(count, entries, lst, pair)
    acc[...] = jnp.zeros_like(acc)
    for g in gets:
        g.wait()
    near_pairs(count, total, pair, at, b, w, acc, tiles)
    write_out(out, acc, count, b.shape[1])


def near_back_kernel(count, entries, lst, x_hbm, b_hbm, w_hbm, after, out, pair, acc, tiles, at, b, w, x, sems):
    leaf = b.shape[1]
    get_x = copy(x_hbm, x, sems.at[0])
    gets = [copy(b_hbm, b, sems.at[1]), copy(w_hbm, w, sems.at[2])]
    total = scan_list(count, entries, lst, pair)
    acc[...] = jnp.zeros_like(acc)

    def keep(l, got):
        at[l] = got

    get_x.wait()
    grouped(count, 8, lambda l: feature_pair(x[:, lanes(l, leaf)])[0], keep)
    for g in gets:
        g.wait()
    near_pairs(count, total, pair, at, b, w, acc, tiles)
    write_out(out, acc, count, leaf)


def near_low_kernel(count, entries, lst, x_hbm, at_hbm, w_hbm, after, out, pair, acc, tiles, at, b, w, x, sems):
    leaf = b.shape[1]
    get_x = copy(x_hbm, x, sems.at[0])
    gets = [copy(at_hbm, at, sems.at[1]), copy(w_hbm, w, sems.at[2])]
    total = scan_list(count, entries, lst, pair)
    acc[...] = jnp.zeros_like(acc)

    def keep(l, got):
        b[l] = got

    get_x.wait()
    grouped(count, 8, lambda l: feature_pair(x[:, lanes(l, leaf)])[1].T, keep)
    for g in gets:
        g.wait()
    near_pairs(count, total, pair, at, b, w, acc, tiles)
    write_out(out, acc, count, leaf)


def near_call(kernel, lst, operands, count, entries, leaf, dim, cols, dtype, own, name):
    return pl.pallas_call(
        functools.partial(kernel, count, entries),
        grid_spec=pltpu.PrefetchScalarGridSpec(
            num_scalar_prefetch=1,
            grid=(1,),
            in_specs=[HBM] * 3 if own else [ANY, HBM, ANY, HBM],
            out_specs=VM,
            scratch_shapes=[
                pltpu.SMEM((count * entries + entries + 4 * GROUP,), jnp.int32),
                pltpu.VMEM((count + 1, cols, leaf), f32),
                pltpu.VMEM((2 * GROUP, leaf, leaf), bf16),
                pltpu.VMEM((count, FEAT, leaf), bf16),
                pltpu.VMEM((count, leaf, FEAT), bf16),
                pltpu.VMEM((cols, count * leaf + 128), bf16),
            ]
            + ([] if own else [pltpu.VMEM((dim, count * leaf), bf16)])
            + [pltpu.SemaphoreType.DMA((3,))],
        ),
        out_shape=jax.ShapeDtypeStruct((cols, count * leaf), dtype),
        compiler_params=pltpu.CompilerParams(vmem_limit_bytes=60 << 20),
        name=name,
    )(lst, *operands)


def down_kernel(dims, pos_ref, gathered, top_pick, ridge, top_hbm, terms_hbm, local_hbm, leaf_hbm, d_hbm, n1_hbm,
                n2_hbm, n3_hbm, out, tb, terms, nb, lb, dt, n1, n2, n3, tcoeff, tskel, value, sems):
    count, leaf, rank, dim, cols, subtrees = dims
    pairs = ((top_hbm, tb), (terms_hbm, terms), (local_hbm, nb), (leaf_hbm, lb), (d_hbm, dt), (n1_hbm, n1),
             (n2_hbm, n2), (n3_hbm, n3))
    gets = [copy(src, dst, sems.at[k]) for k, (src, dst) in enumerate(pairs)]
    pos = pos_ref[0]
    depth = subtrees.bit_length() - 1
    for s in range(subtrees):
        tcoeff[:, lanes(subtrees - 1 + s, rank)] = gathered[s, :cols]
        tskel[:, lanes(subtrees - 1 + s, rank)] = gathered[s, cols:]
    gets[0].wait()
    for d in range(depth - 1, 0, -1):

        def climb(j):
            both = lanes(2 * j + 1, rank, 2)
            sel = selector(top_pick[pl.ds(j, 1), :], 2 * rank)
            return dot(tcoeff[:, both], tb[j]).astype(bf16), dot(tskel[:, both], sel).astype(bf16)

        def climb_keep(j, got):
            tcoeff[:, lanes(j, rank)], tskel[:, lanes(j, rank)] = got

        grouped(2**d, 8, climb, climb_keep, 2**d - 1)

    def half(v):
        return (v.astype(f32) * 0.5).astype(bf16)

    top_terms = {}
    for d in range(depth, 0, -1):
        mine = pos >> (depth - d)
        other = mine ^ 1
        own_left = feature_pair(half(tskel[:, lanes(2**d - 1 + mine, rank)]))[0]
        sib_right = feature_pair(half(tskel[:, lanes(2**d - 1 + other, rank)]))[1]
        g = gauss(sib_right.T, own_left)
        top_terms[d] = dot(tcoeff[:, lanes(2**d - 1 + other, rank)], g)
    v = jnp.zeros((cols, rank), bf16)
    for d in range(1, depth + 1):
        parent = pos >> (depth - d + 1)
        down = dot(v, tb[2 ** (d - 1) - 1 + parent], 1, 1)
        right = ((pos >> (depth - d)) & 1) == 1
        v = (top_terms[d] + jnp.where(right, down[:, rank:], down[:, :rank])).astype(bf16)
    value[:, lanes(0, rank)] = v
    gets[1].wait()
    gets[2].wait()
    local_depth = count.bit_length() - 1
    for d in range(1, local_depth + 1):

        def descend(j):
            down = dot(value[:, lanes(j, rank)], nb[j], 1, 1)
            return (terms[:, lanes(2 * j, rank, 2)] + down).astype(bf16)

        def descend_keep(j, got):
            value[:, lanes(2 * j + 1, rank, 2)] = got

        grouped(2 ** (d - 1), 8, descend, descend_keep, 2 ** (d - 1) - 1)
    for g in gets[3:]:
        g.wait()
    scale = ridge[...]

    def finish(l):
        far = dot(value[:, lanes(count - 1 + l, rank)], lb[l], 1, 1)
        s = lanes(l, leaf)
        return scale * dt[:, s] + far + (n1[:, s] + n2[:, s] + n3[:, s].astype(f32))

    def finish_keep(l, got):
        out[:, lanes(l, leaf)] = got

    grouped(count, 8, finish, finish_keep)


def downward(pos, gathered, top_pick, ridge, top_basis, terms, local_basis, leaf_basis, dt, n1, n2, n3, dim):
    count, leaf, rank = leaf_basis.shape
    cols = dt.shape[0]
    subtrees = gathered.shape[0]
    big = (top_basis, terms, local_basis, leaf_basis, dt, n1, n2, n3)
    return pl.pallas_call(
        functools.partial(down_kernel, (count, leaf, rank, dim, cols, subtrees)),
        grid_spec=pltpu.PrefetchScalarGridSpec(
            num_scalar_prefetch=1,
            grid=(1,),
            in_specs=[VM] * 3 + [HBM] * 7 + [ANY],
            out_specs=VM,
            scratch_shapes=[pltpu.VMEM(a.shape, a.dtype) for a in big]
            + [
                pltpu.VMEM((cols, (2 * subtrees - 1) * rank), bf16),
                pltpu.VMEM((dim, (2 * subtrees - 1) * rank), bf16),
                pltpu.VMEM((cols, (2 * count - 1) * rank), bf16),
                pltpu.SemaphoreType.DMA((8,)),
            ],
        ),
        out_shape=jax.ShapeDtypeStruct(dt.shape, f32),
        compiler_params=pltpu.CompilerParams(vmem_limit_bytes=60 << 20),
        name="downward",
    )(pos, gathered, top_pick, ridge, *big)


def class_list(ids, low, count):
    entries = ids.shape[0]
    local = ids - low
    inside = (local >= 0) & (local < count)
    ones = inside.astype(jnp.int32)
    row = [jnp.zeros_like(ones[0])]
    for e in range(entries):
        row.append(row[-1] + ones[e])
    out = []
    for k in range(entries):
        acc = jnp.zeros_like(ones[0])
        for e in range(k, entries):
            acc = acc + jnp.where(inside[e] & (row[e] == k), local[e], 0)
        out.append(acc)
    out.append(row[-1])
    return jnp.stack(out, 0)


def shards(points, direction, ridge, leaf_basis, local_basis, top_basis, leaf_pick, local_pick, top_pick, near_list):
    count, leaf, rank = leaf_basis.shape
    dim, cols = points.shape[1], direction.shape[1]
    entries = near_list.shape[1]
    chips = lax.axis_size("chip")
    subtrees = lax.axis_size("leaf") * chips
    pos = lax.axis_index("leaf") * chips + lax.axis_index("chip")
    upper = [(i, i + 1) for i in range(subtrees - 1)]
    lower = [(i + 1, i) for i in range(subtrees - 1)]

    xt, dt, ids = points.T, direction.T, near_list.T
    x_low = lax.ppermute(xt, AXES, upper)
    list_up = class_list(ids, (pos + 1) * count, count)
    ext = jnp.pad(list_up.astype(bf16), ((0, cols - entries - 1), (0, 128 - count)))
    list_own = class_list(ids, pos * count, count)
    list_low = class_list(ids, (pos - 1) * count, count)

    at, b, w, terms, spread = upward(xt, dt, ext, leaf_pick, local_pick, leaf_basis, local_basis, subtrees)
    w_low = lax.ppermute(w, AXES, upper)
    gathered = lax.all_to_all(spread, AXES, 0, 0)
    call = functools.partial(near_call, count=count, entries=entries, leaf=leaf, dim=dim, cols=cols)
    n_own = call(near_own_kernel, list_own, (at, b, w), dtype=f32, own=True, name="near_own")
    list_back = w_low[: entries + 1, count * leaf : count * leaf + count].astype(jnp.int32)
    back = call(near_back_kernel, list_back, (x_low, b, w, n_own), dtype=bf16, own=False, name="near_back")
    returned = lax.ppermute(back, AXES, lower)
    n_low = call(near_low_kernel, list_low, (x_low, at, w_low, back), dtype=f32, own=False, name="near_low")
    out = downward(
        pos[None], gathered, top_pick, ridge[:, None], top_basis, terms, local_basis, leaf_basis, dt,
        n_own, n_low, returned, dim,
    )
    return out.T


def solution(mesh):
    split = P(AXES, None)
    split3 = P(AXES, None, None)
    return jax.shard_map(
        shards,
        mesh=mesh,
        in_specs=(split, split, P(), split3, split3, P(), split, split, P(), split),
        out_specs=split,
        check_vma=False,
    )
```

```python
import functools
import math

import jax
import jax.numpy as jnp
from jax import lax
from jax.experimental import pallas as pl
from jax.experimental.pallas import tpu as pltpu
from jax.sharding import PartitionSpec as P

f32 = jnp.float32
bf16 = jnp.bfloat16
AXES = ("leaf", "chip")
SCALE = math.log2(math.e) / 32.0
FEAT = 128
GROUP = 16


def dot(a, b, ca=1, cb=0):
    return lax.dot_general(a, b, (((ca,), (cb,)), ((), ())), preferred_element_type=f32)


def copy(src, dst, sem):
    c = pltpu.make_async_copy(src, dst, sem)
    c.start()
    return c


VM = pl.BlockSpec(memory_space=pltpu.VMEM)
HBM = pl.BlockSpec(memory_space=pltpu.HBM)
ANY = pl.BlockSpec(memory_space=pl.ANY)


def square_rows(xf):
    n = jnp.sum(xf * xf, axis=0, keepdims=True)
    hi = n.astype(bf16).astype(f32)
    rest = n - hi
    mid = rest.astype(bf16).astype(f32)
    low = rest - mid
    row = lax.broadcasted_iota(jnp.int32, (16, xf.shape[1]), 0)
    zero = jnp.zeros((), f32)
    neg = jnp.where(row == 0, -hi, jnp.where(row == 1, -mid, jnp.where(row == 2, -low, zero)))
    ones = jnp.where(row < 3, jnp.ones((), f32), zero)
    return neg.astype(bf16), ones.astype(bf16)


def feature_pair(x):
    dim, width = x.shape
    xf = x.astype(f32)
    neg, ones = square_rows(xf)
    pad = jnp.zeros((FEAT - dim - 32, width), bf16)
    left = jnp.concatenate([(xf + xf).astype(bf16), ones, neg, pad], 0)
    right = jnp.concatenate([x, neg, ones, pad], 0)
    return left, right


def swap_form(left, dim):
    half = (left[:dim].astype(f32) * 0.5).astype(bf16)
    return jnp.concatenate([half, left[dim + 16 : dim + 32], left[dim : dim + 16], left[dim + 32 :]], 0)


def selector(pick_row, width):
    rows = lax.broadcasted_iota(jnp.int32, (width, pick_row.shape[1]), 0)
    return jnp.where(rows == pick_row, jnp.ones((), f32), jnp.zeros((), f32)).astype(bf16)


def gauss(right_rows, left_cols):
    s = dot(right_rows, left_cols)
    return jnp.exp2(s * SCALE).astype(bf16)


def grouped(count, group, compute, store, start=0):
    group = min(group, count)

    def body(t, carry):
        got = [compute(start + t * group + u) for u in range(group)]
        for u in range(group):
            store(start + t * group + u, got[u])
        return carry

    if count == group:
        body(0, 0)
    else:
        lax.fori_loop(0, count // group, body, 0)


def lanes(start, width, number=1):
    if isinstance(start, int):
        return pl.ds(start * width, number * width)
    return pl.ds(pl.multiple_of(start * width, width), number * width)


CHUNKS = 4
PAIRS = 8


def class_list(ids, low, count):
    entries = ids.shape[0]
    local = ids - low
    inside = (local >= 0) & (local < count)
    ones = inside.astype(jnp.int32)
    rank = [jnp.zeros_like(ones[0:1])]
    for e in range(entries):
        rank.append(rank[-1] + ones[e : e + 1])
    row = lax.broadcasted_iota(jnp.int32, (16, ids.shape[1]), 0)
    out = jnp.where(row == entries, rank[-1], 0)
    for e in range(entries):
        here = (row == rank[e]) & (ones[e : e + 1] == 1)
        out = out + jnp.where(here, local[e : e + 1], 0)
    return out


def up_kernel(dims, pos_ref, x_hbm, d_hbm, ids, leaf_pick, local_pick, leaf_hbm, local_hbm,
              w_hbm, terms_hbm, spread, list_own, list_low,
              xt, dt, at, wt, terms, lb, nb, coeff, skel, tiles, xs, ls, ms):
    count, leaf, rank, dim, cols = dims
    part = count // CHUNKS
    seg = lambda c: pl.ds(c * part * leaf, part * leaf)
    own = lambda c: pl.ds(c * part, part)
    get_x = [copy(x_hbm.at[:, seg(c)], xt.at[:, seg(c)], xs.at[c]) for c in range(CHUNKS)]
    get_d = copy(d_hbm, dt, ms.at[0])
    get_leaf = [copy(leaf_hbm.at[own(c)], lb.at[own(c)], ls.at[c]) for c in range(CHUNKS)]
    get_local = copy(local_hbm, nb, ms.at[1])
    pos = pos_ref[0]
    table = ids[...]
    list_own[...] = class_list(table, pos * count, count)
    list_low[...] = class_list(table, (pos - 1) * count, count)
    wt[:, pl.ds(count * leaf, 128)] = jnp.zeros((cols, 128), bf16)
    wt[:, pl.ds(count * leaf, count)] = class_list(table, (pos + 1) * count, count).astype(f32).astype(bf16)

    def keep(l, got):
        at[l] = got

    for c in range(CHUNKS):
        get_x[c].wait()
        grouped(part, 8, lambda l: feature_pair(xt[:, lanes(l, leaf)])[0], keep, c * part)
    get_d.wait()
    for c in range(CHUNKS):
        wt[:, seg(c)] = dt[:, seg(c)].astype(bf16)
    puts = [copy(wt, w_hbm, ms.at[2])]
    base = count - 1

    def leaf_step(l):
        c = dot(wt[:, lanes(l, leaf)], lb[l])
        sel = selector(leaf_pick[pl.ds(l, 1), :], leaf)
        return c.astype(bf16), dot(at[l], sel).astype(bf16)

    def leaf_keep(l, got):
        coeff[:, lanes(base + l, rank)], skel[:, lanes(base + l, rank)] = got

    for c in range(CHUNKS):
        get_leaf[c].wait()
        grouped(part, 8, leaf_step, leaf_keep, c * part)
    get_local.wait()
    depth = count.bit_length() - 1
    for d in range(depth, 0, -1):
        up = 2 ** (d - 1) - 1

        def climb(j):
            both = lanes(2 * j + 1, rank, 2)
            sel = selector(local_pick[pl.ds(j, 1), :], 2 * rank)
            return dot(coeff[:, both], nb[j]).astype(bf16), dot(skel[:, both], sel).astype(bf16)

        def climb_keep(j, got):
            coeff[:, lanes(j, rank)], skel[:, lanes(j, rank)] = got

        grouped(2 ** (d - 1), 8, climb, climb_keep, up)
    root_c, root_s = coeff[:, :rank], skel[:dim, :rank]
    for s in range(spread.shape[0]):
        spread[s, :cols, :] = root_c
        spread[s, cols:, :] = root_s

    last = count - 2

    def index(j):
        return min(j, last) if isinstance(j, int) else jnp.minimum(j, last)

    def first(j, slot):
        both = skel[:, lanes(2 * index(j) + 1, rank, 2)]
        tiles[slot] = gauss(swap_form(both[:, rank:], dim).T, both[:, :rank])

    def second(j, slot):
        c2 = coeff[:, lanes(2 * index(j) + 1, rank, 2)]
        g = tiles[slot]
        return jnp.concatenate([dot(c2[:, rank:], g), dot(c2[:, :rank], g, 1, 1)], 1)

    for u in range(PAIRS):
        first(u, u)

    def body(t, carry):
        for phase in range(2):
            k = (2 * t + phase) * PAIRS
            got = []
            for u in range(PAIRS):
                first(k + PAIRS + u, (1 - phase) * PAIRS + u)
                got.append(second(k + u, phase * PAIRS + u))
            for u in range(PAIRS):
                terms[:, lanes(2 * index(k + u), rank, 2)] = got[u]
        return carry

    lax.fori_loop(0, count // (2 * PAIRS), body, 0)
    puts.append(copy(terms, terms_hbm, ms.at[3]))
    for p in puts:
        p.wait()


def upward(pos, xt, dt, ids, leaf_pick, local_pick, leaf_basis, local_basis, subtrees):
    count, leaf, rank = leaf_basis.shape
    dim, cols = xt.shape[0], dt.shape[0]
    width = count * leaf + 128
    return pl.pallas_call(
        functools.partial(up_kernel, (count, leaf, rank, dim, cols)),
        grid_spec=pltpu.PrefetchScalarGridSpec(
            num_scalar_prefetch=1,
            grid=(1,),
            in_specs=[HBM, HBM, VM, VM, VM, HBM, HBM],
            out_specs=[HBM, HBM, VM, VM, VM],
            scratch_shapes=[
                pltpu.VMEM(xt.shape, bf16),
                pltpu.VMEM(dt.shape, f32),
                pltpu.VMEM((count, FEAT, leaf), bf16),
                pltpu.VMEM((cols, width), bf16),
                pltpu.VMEM((cols, (2 * count - 2) * rank), f32),
                pltpu.VMEM(leaf_basis.shape, bf16),
                pltpu.VMEM(local_basis.shape, bf16),
                pltpu.VMEM((cols, (2 * count - 1) * rank), bf16),
                pltpu.VMEM((FEAT, (2 * count - 1) * rank), bf16),
                pltpu.VMEM((2 * PAIRS, rank, rank), bf16),
                pltpu.SemaphoreType.DMA((CHUNKS,)),
                pltpu.SemaphoreType.DMA((CHUNKS,)),
                pltpu.SemaphoreType.DMA((4,)),
            ],
        ),
        out_shape=[
            jax.ShapeDtypeStruct((cols, width), bf16),
            jax.ShapeDtypeStruct((cols, (2 * count - 2) * rank), f32),
            jax.ShapeDtypeStruct((subtrees, cols + dim, rank), bf16),
            jax.ShapeDtypeStruct((16, count), jnp.int32),
            jax.ShapeDtypeStruct((16, count), jnp.int32),
        ],
        compiler_params=pltpu.CompilerParams(vmem_limit_bytes=60 << 20),
        name="upward",
    )(pos, xt, dt, ids, leaf_pick, local_pick, leaf_basis, local_basis)


def scan_list(count, entries, lst, pair):
    def scan(i, pos):
        for e in range(entries):
            pair[pos + e] = i * count + lst[e, i]
        return pos + lst[entries, i]

    total = lax.fori_loop(0, count, scan, 0)
    for u in range(3 * GROUP):
        pair[total + u] = count * count
    return total


def near_pairs(count, total, pair, at, b, w, acc, tiles):
    h = GROUP
    leaf = b.shape[1]
    shift = count.bit_length() - 1

    def first(k, slot):
        code = pair[k]
        tiles[slot] = gauss(b[code & (count - 1)], at[(code >> shift) & (count - 1)])

    def second(k, slot):
        code = pair[k]
        return code >> shift, dot(w[:, lanes(code & (count - 1), leaf)], tiles[slot])

    for u in range(h):
        first(u, u)

    def body(t, carry):
        for phase in range(2):
            k = (2 * t + phase) * h
            got = []
            for u in range(h):
                first(k + h + u, (1 - phase) * h + u)
                got.append(second(k + u, phase * h + u))
            for i, o in got:
                acc[i] += o
        return carry

    blocks = (total + h - 1) // h
    lax.fori_loop(0, (blocks + 1) // 2, body, 0)


def near_scratch(count, entries, leaf, dim, cols):
    return [
        pltpu.SMEM((count * entries + entries + 4 * GROUP,), jnp.int32),
        pltpu.VMEM((2 * GROUP, leaf, leaf), bf16),
        pltpu.VMEM((count, FEAT, leaf), bf16),
        pltpu.VMEM((count, leaf, FEAT), bf16),
        pltpu.VMEM((cols, count * leaf + 128), bf16),
        pltpu.VMEM((dim, count * leaf), bf16),
    ]


def near_own_kernel(entries, lst, x_hbm, w_hbm, acc, pair, tiles, at, b, w, x, xs, sems):
    count, _, leaf = at.shape
    part = count // CHUNKS
    seg = lambda c: pl.ds(c * part * leaf, part * leaf)
    get_x = [copy(x_hbm.at[:, seg(c)], x.at[:, seg(c)], xs.at[c]) for c in range(CHUNKS)]
    get_w = copy(w_hbm, w, sems.at[0])
    total = scan_list(count, entries, lst, pair)
    acc[...] = jnp.zeros_like(acc)

    def prepare(l):
        left, right = feature_pair(x[:, lanes(l, leaf)])
        return left, right.T

    def keep(l, got):
        at[l], b[l] = got

    for c in range(CHUNKS):
        get_x[c].wait()
        grouped(part, 8, prepare, keep, c * part)
    get_w.wait()
    near_pairs(count, total, pair, at, b, w, acc, tiles)


def near_own(lst, x, w, count, entries, leaf):
    dim, cols = x.shape[0], w.shape[0]
    return pl.pallas_call(
        functools.partial(near_own_kernel, entries),
        grid_spec=pltpu.PrefetchScalarGridSpec(
            num_scalar_prefetch=1,
            grid=(1,),
            in_specs=[HBM] * 2,
            out_specs=VM,
            scratch_shapes=near_scratch(count, entries, leaf, dim, cols)
            + [pltpu.SemaphoreType.DMA((CHUNKS,)), pltpu.SemaphoreType.DMA((1,))],
        ),
        out_shape=jax.ShapeDtypeStruct((count + 1, cols, leaf), f32),
        compiler_params=pltpu.CompilerParams(vmem_limit_bytes=60 << 20),
        name="near_own",
    )(lst, x, w)


def two_sided(count, leaf, target_hbm, source_hbm, x, y, at, b, xs):
    part = count // CHUNKS
    seg = lambda c: pl.ds(c * part * leaf, part * leaf)
    gets = []
    for c in range(CHUNKS):
        gets.append(copy(source_hbm.at[:, seg(c)], y.at[:, seg(c)], xs.at[1, c]))
        gets.append(copy(target_hbm.at[:, seg(c)], x.at[:, seg(c)], xs.at[0, c]))

    def finish():
        def prepare(l):
            return feature_pair(x[:, lanes(l, leaf)])[0], feature_pair(y[:, lanes(l, leaf)])[1].T

        def keep(l, got):
            at[l], b[l] = got

        for c in range(CHUNKS):
            gets[2 * c].wait()
            gets[2 * c + 1].wait()
            grouped(part, 8, prepare, keep, c * part)

    return finish


def near_back_kernel(entries, low_hbm, x_hbm, wlow_hbm, w_hbm, after, out,
                     pair, tiles, at, b, w, x, y, acc, lf, lv, lst, xs, sems):
    count, _, leaf = at.shape
    get_list = copy(wlow_hbm.at[:, pl.ds(count * leaf, 128)], lf, sems.at[0])
    finish = two_sided(count, leaf, low_hbm, x_hbm, x, y, at, b, xs)
    get_w = copy(w_hbm, w, sems.at[1])
    get_list.wait()
    lv[...] = lf[...].astype(f32).astype(jnp.int32)
    put_list = copy(lv, lst, sems.at[2])
    acc[...] = jnp.zeros_like(acc)
    put_list.wait()
    total = scan_list(count, entries, lst, pair)
    finish()
    get_w.wait()
    near_pairs(count, total, pair, at, b, w, acc, tiles)

    def store(l, got):
        out[:, lanes(l, leaf)] = got.astype(out.dtype)

    grouped(count, 8, lambda l: acc[l], store)


def near_back(x_low, x, w_low, w, after, count, entries, leaf):
    dim, cols = x.shape[0], w.shape[0]
    return pl.pallas_call(
        functools.partial(near_back_kernel, entries),
        grid=(1,),
        in_specs=[ANY, HBM, ANY, HBM, HBM],
        out_specs=VM,
        scratch_shapes=near_scratch(count, entries, leaf, dim, cols)
        + [
            pltpu.VMEM((dim, count * leaf), bf16),
            pltpu.VMEM((count + 1, cols, leaf), f32),
            pltpu.VMEM((cols, 128), bf16),
            pltpu.VMEM((cols, 128), jnp.int32),
            pltpu.SMEM((cols, 128), jnp.int32),
            pltpu.SemaphoreType.DMA((2, CHUNKS)),
            pltpu.SemaphoreType.DMA((3,)),
        ],
        out_shape=jax.ShapeDtypeStruct((cols, count * leaf), bf16),
        compiler_params=pltpu.CompilerParams(vmem_limit_bytes=57 << 20),
        name="near_back",
    )(x_low, x, w_low, w, after)


def down_kernel(dims, pos_ref, lst, ridge, gathered, top_pick, low_hbm, x_hbm, wlow_hbm, own_hbm,
                top_hbm, terms_hbm, local_hbm, leaf_hbm, d_hbm, after, out,
                pair, tiles, at, b, w, x, y, acc, tb, terms, nb, lb, dt, tcoeff, tskel, value, xs, sems):
    count, leaf, rank, dim, cols, subtrees, entries = dims
    finish_features = two_sided(count, leaf, x_hbm, low_hbm, x, y, at, b, xs)
    get_w = copy(wlow_hbm, w, sems.at[0])
    get_acc = copy(own_hbm, acc, sems.at[1])
    pairs = ((top_hbm, tb), (terms_hbm, terms), (local_hbm, nb), (leaf_hbm, lb), (d_hbm, dt))
    gets = [copy(src, dst, sems.at[k + 2]) for k, (src, dst) in enumerate(pairs)]
    total = scan_list(count, entries, lst, pair)
    finish_features()
    get_w.wait()
    get_acc.wait()
    near_pairs(count, total, pair, at, b, w, acc, tiles)

    pos = pos_ref[0]
    depth = subtrees.bit_length() - 1
    for s in range(subtrees):
        tcoeff[:, lanes(subtrees - 1 + s, rank)] = gathered[s, :cols]
        tskel[:, lanes(subtrees - 1 + s, rank)] = gathered[s, cols:]
    for g in gets:
        g.wait()
    for d in range(depth - 1, 0, -1):

        def climb(j):
            both = lanes(2 * j + 1, rank, 2)
            sel = selector(top_pick[pl.ds(j, 1), :], 2 * rank)
            return dot(tcoeff[:, both], tb[j]).astype(bf16), dot(tskel[:, both], sel).astype(bf16)

        def climb_keep(j, got):
            tcoeff[:, lanes(j, rank)], tskel[:, lanes(j, rank)] = got

        grouped(2**d, 8, climb, climb_keep, 2**d - 1)

    def half(v):
        return (v.astype(f32) * 0.5).astype(bf16)

    top_terms = {}
    for d in range(depth, 0, -1):
        mine = pos >> (depth - d)
        other = mine ^ 1
        own_left = feature_pair(half(tskel[:, lanes(2**d - 1 + mine, rank)]))[0]
        sib_right = feature_pair(half(tskel[:, lanes(2**d - 1 + other, rank)]))[1]
        g = gauss(sib_right.T, own_left)
        top_terms[d] = dot(tcoeff[:, lanes(2**d - 1 + other, rank)], g)
    v = jnp.zeros((cols, rank), bf16)
    for d in range(1, depth + 1):
        parent = pos >> (depth - d + 1)
        down = dot(v, tb[2 ** (d - 1) - 1 + parent], 1, 1)
        right = ((pos >> (depth - d)) & 1) == 1
        v = (top_terms[d] + jnp.where(right, down[:, rank:], down[:, :rank])).astype(bf16)
    value[:, lanes(0, rank)] = v
    local_depth = count.bit_length() - 1
    for d in range(1, local_depth + 1):

        def descend(j):
            down = dot(value[:, lanes(j, rank)], nb[j], 1, 1)
            return (terms[:, lanes(2 * j, rank, 2)] + down).astype(bf16)

        def descend_keep(j, got):
            value[:, lanes(2 * j + 1, rank, 2)] = got

        grouped(2 ** (d - 1), 8, descend, descend_keep, 2 ** (d - 1) - 1)
    row = lax.broadcasted_iota(jnp.int32, (cols, leaf), 0)
    scale = jnp.zeros((cols, leaf), f32)
    for r in range(cols):
        scale = jnp.where(row == r, ridge[r], scale)

    def finish(l):
        far = dot(value[:, lanes(count - 1 + l, rank)], lb[l], 1, 1)
        return scale * dt[:, lanes(l, leaf)] + far + acc[l]

    def finish_keep(l, got):
        out[:, lanes(l, leaf)] = got

    grouped(count, 8, finish, finish_keep)


def downward(pos, lst, ridge, gathered, top_pick, x_low, x, w_low, n_own, top_basis, terms, local_basis, leaf_basis,
             dt, after, entries):
    count, leaf, rank = leaf_basis.shape
    dim, cols = x.shape[0], dt.shape[0]
    subtrees = gathered.shape[0]
    big = (top_basis, terms, local_basis, leaf_basis, dt)
    return pl.pallas_call(
        functools.partial(down_kernel, (count, leaf, rank, dim, cols, subtrees, entries)),
        grid_spec=pltpu.PrefetchScalarGridSpec(
            num_scalar_prefetch=3,
            grid=(1,),
            in_specs=[VM] * 2 + [ANY, HBM, ANY] + [HBM] * 7,
            out_specs=VM,
            scratch_shapes=near_scratch(count, entries, leaf, dim, cols)
            + [pltpu.VMEM((dim, count * leaf), bf16), pltpu.VMEM((count + 1, cols, leaf), f32)]
            + [pltpu.VMEM(a.shape, a.dtype) for a in big]
            + [
                pltpu.VMEM((cols, (2 * subtrees - 1) * rank), bf16),
                pltpu.VMEM((dim, (2 * subtrees - 1) * rank), bf16),
                pltpu.VMEM((cols, (2 * count - 1) * rank), bf16),
                pltpu.SemaphoreType.DMA((2, CHUNKS)),
                pltpu.SemaphoreType.DMA((7,)),
            ],
        ),
        out_shape=jax.ShapeDtypeStruct(dt.shape, f32),
        compiler_params=pltpu.CompilerParams(vmem_limit_bytes=57 << 20),
        name="downward",
    )(pos, lst, ridge, gathered, top_pick, x_low, x, w_low, n_own, *big, after)


def shards(points, direction, ridge, leaf_basis, local_basis, top_basis, leaf_pick, local_pick, top_pick, near_list):
    count, leaf, rank = leaf_basis.shape
    entries = near_list.shape[1]
    chips = lax.axis_size("chip")
    subtrees = lax.axis_size("leaf") * chips
    pos = (lax.axis_index("leaf") * chips + lax.axis_index("chip"))[None]
    upper = [(i, i + 1) for i in range(subtrees - 1)]
    lower = [(i + 1, i) for i in range(subtrees - 1)]

    xt, dt, ids = points.T, direction.T, near_list.T
    x_low = lax.ppermute(xt, AXES, upper)
    w, terms, spread, list_own, list_low = upward(
        pos, xt, dt, ids, leaf_pick, local_pick, leaf_basis, local_basis, subtrees
    )
    gathered = lax.all_to_all(spread, AXES, 0, 0)
    w_low = lax.ppermute(w, AXES, upper)
    n_own = near_own(list_own, xt, w, count, entries, leaf)
    back = near_back(x_low, xt, w_low, w, n_own, count, entries, leaf)
    returned = lax.ppermute(back, AXES, lower)
    out = downward(
        pos, list_low, ridge, gathered, top_pick, x_low, xt, w_low, n_own, top_basis, terms, local_basis, leaf_basis,
        dt, back, entries,
    )
    return (out + returned.astype(f32)).T


def solution(mesh):
    split = P(AXES, None)
    split3 = P(AXES, None, None)
    return jax.shard_map(
        shards,
        mesh=mesh,
        in_specs=(split, split, P(), split3, split3, P(), split, split, P(), split),
        out_specs=split,
        check_vma=False,
    )
```

```python
import functools
import math

import jax
import jax.numpy as jnp
from jax import lax
from jax.experimental import pallas as pl
from jax.experimental.pallas import tpu as pltpu
from jax.sharding import PartitionSpec as P

f32 = jnp.float32
bf16 = jnp.bfloat16
AXES = ("leaf", "chip")
SCALE = math.log2(math.e) / 32.0
FEAT = 128
GROUP = 16


def dot(a, b, ca=1, cb=0):
    return lax.dot_general(a, b, (((ca,), (cb,)), ((), ())), preferred_element_type=f32)


def copy(src, dst, sem):
    c = pltpu.make_async_copy(src, dst, sem)
    c.start()
    return c


VM = pl.BlockSpec(memory_space=pltpu.VMEM)
HBM = pl.BlockSpec(memory_space=pltpu.HBM)
ANY = pl.BlockSpec(memory_space=pl.ANY)


def square_rows(xf):
    n = jnp.sum(xf * xf, axis=0, keepdims=True)
    hi = n.astype(bf16).astype(f32)
    rest = n - hi
    mid = rest.astype(bf16).astype(f32)
    low = rest - mid
    row = lax.broadcasted_iota(jnp.int32, (16, xf.shape[1]), 0)
    zero = jnp.zeros((), f32)
    neg = jnp.where(row == 0, -hi, jnp.where(row == 1, -mid, jnp.where(row == 2, -low, zero)))
    ones = jnp.where(row < 3, jnp.ones((), f32), zero)
    return neg.astype(bf16), ones.astype(bf16)


def feature_pair(x):
    dim, width = x.shape
    xf = x.astype(f32)
    neg, ones = square_rows(xf)
    pad = jnp.zeros((FEAT - dim - 32, width), bf16)
    left = jnp.concatenate([(xf + xf).astype(bf16), ones, neg, pad], 0)
    right = jnp.concatenate([x, neg, ones, pad], 0)
    return left, right


def swap_form(left, dim):
    half = (left[:dim].astype(f32) * 0.5).astype(bf16)
    return jnp.concatenate([half, left[dim + 16 : dim + 32], left[dim : dim + 16], left[dim + 32 :]], 0)


def selector(pick_row, width):
    rows = lax.broadcasted_iota(jnp.int32, (width, pick_row.shape[1]), 0)
    return jnp.where(rows == pick_row, jnp.ones((), f32), jnp.zeros((), f32)).astype(bf16)


def gauss(right_rows, left_cols):
    s = dot(right_rows, left_cols)
    return jnp.exp2(s * SCALE).astype(bf16)


def grouped(count, group, compute, store, start=0, also=None, carry=0):
    group = min(group, count)

    def body(t, carry):
        got = [compute(start + t * group + u) for u in range(group)]
        for u in range(group):
            store(start + t * group + u, got[u])
            if also is not None:
                carry = also(start + t * group + u, carry)
        return carry

    if count == group:
        return body(0, carry)
    return lax.fori_loop(0, count // group, body, carry)


def lanes(start, width, number=1):
    if isinstance(start, int):
        return pl.ds(start * width, number * width)
    return pl.ds(pl.multiple_of(start * width, width), number * width)


CHUNKS = 4
PAIRS = 16


def class_list(ids, low, count):
    entries = ids.shape[0]
    local = ids - low
    inside = (local >= 0) & (local < count)
    ones = inside.astype(jnp.int32)
    rank = [jnp.zeros_like(ones[0:1])]
    for e in range(entries):
        rank.append(rank[-1] + ones[e : e + 1])
    row = lax.broadcasted_iota(jnp.int32, (16, ids.shape[1]), 0)
    out = jnp.where(row == entries, rank[-1], 0)
    for e in range(entries):
        here = (row == rank[e]) & (ones[e : e + 1] == 1)
        out = out + jnp.where(here, local[e : e + 1], 0)
    return out


def up_kernel(dims, pos_ref, x_hbm, d_hbm, ids, leaf_pick, local_pick, leaf_hbm, local_hbm,
              w_hbm, terms_hbm, spread, list_low, acc,
              pair, big, at, b, wt, xt, dt, terms, lb, nb, coeff, skel, tiles, lv, lst, xs, ls, ms):
    count, leaf, rank, dim, cols = dims
    entries = ids.shape[0]
    part = count // CHUNKS
    seg = lambda c: pl.ds(c * part * leaf, part * leaf)
    own = lambda c: pl.ds(c * part, part)
    get_x = [copy(x_hbm.at[:, seg(c)], xt.at[:, seg(c)], xs.at[c]) for c in range(CHUNKS)]
    get_d = copy(d_hbm, dt, ms.at[0])
    pos = pos_ref[0]
    table = ids[...]
    put_list = put_class(table, pos * count, count, lv, lst, ms.at[4])
    list_low[...] = class_list(table, (pos - 1) * count, count)
    acc[...] = jnp.zeros_like(acc)

    def prepare(l):
        left, right = feature_pair(xt[:, lanes(l, leaf)])
        return left, right.T

    def keep(l, got):
        at[l], b[l] = got

    total = 0
    for c in range(CHUNKS):
        get_x[c].wait()
        if c == 0:
            put_list.wait()
        if c == 1:
            get_leaf = [copy(leaf_hbm.at[own(k)], lb.at[own(k)], ls.at[k]) for k in range(CHUNKS)]
            get_local = copy(local_hbm, nb, ms.at[1])
        total = grouped(part, 8, prepare, keep, c * part, scan_leaf(count, entries, lst, pair), total)
    end_list(count, pair, total)
    get_d.wait()
    for c in range(CHUNKS):
        wt[:, seg(c)] = dt[:, seg(c)].astype(bf16)
    puts = [copy(wt, w_hbm, ms.at[2])]
    base = count - 1

    def leaf_step(l):
        c = dot(wt[:, lanes(l, leaf)], lb[l])
        sel = selector(leaf_pick[pl.ds(l, 1), :], leaf)
        return c.astype(bf16), dot(at[l], sel).astype(bf16)

    def leaf_keep(l, got):
        coeff[:, lanes(base + l, rank)], skel[:, lanes(base + l, rank)] = got

    for c in range(CHUNKS):
        get_leaf[c].wait()
        grouped(part, 8, leaf_step, leaf_keep, c * part)
    get_local.wait()
    depth = count.bit_length() - 1
    for d in range(depth, 0, -1):
        up = 2 ** (d - 1) - 1

        def climb(j):
            both = lanes(2 * j + 1, rank, 2)
            sel = selector(local_pick[pl.ds(j, 1), :], 2 * rank)
            return dot(coeff[:, both], nb[j]).astype(bf16), dot(skel[:, both], sel).astype(bf16)

        def climb_keep(j, got):
            coeff[:, lanes(j, rank)], skel[:, lanes(j, rank)] = got

        grouped(2 ** (d - 1), 16, climb, climb_keep, up)
    root_c, root_s = coeff[:, :rank], skel[:dim, :rank]
    for s in range(spread.shape[0]):
        spread[s, :cols, :] = root_c
        spread[s, cols:, :] = root_s

    last = count - 2

    def index(j):
        return min(j, last) if isinstance(j, int) else jnp.minimum(j, last)

    def first(j, slot):
        both = skel[:, lanes(2 * index(j) + 1, rank, 2)]
        tiles[slot] = gauss(swap_form(both[:, rank:], dim).T, both[:, :rank])

    def second(j, slot):
        c2 = coeff[:, lanes(2 * index(j) + 1, rank, 2)]
        g = tiles[slot]
        return jnp.concatenate([dot(c2[:, rank:], g), dot(c2[:, :rank], g, 1, 1)], 1)

    for u in range(PAIRS):
        first(u, u)

    def body(t, carry):
        for phase in range(2):
            k = (2 * t + phase) * PAIRS
            got = []
            for u in range(PAIRS):
                first(k + PAIRS + u, (1 - phase) * PAIRS + u)
                got.append(second(k + u, phase * PAIRS + u))
            for u in range(PAIRS):
                terms[:, lanes(2 * index(k + u), rank, 2)] = got[u]
        return carry

    lax.fori_loop(0, count // (2 * PAIRS), body, 0)
    puts.append(copy(terms, terms_hbm, ms.at[3]))
    near_pairs(count, total, pair, at, b, wt, acc, big)
    for p in puts:
        p.wait()


def put_class(table, low, count, lv, lst, sem):
    lv[...] = jnp.zeros_like(lv)
    lv[:, :count] = class_list(table, low, count)
    return copy(lv, lst, sem)


def upward(pos, xt, dt, ids, leaf_pick, local_pick, leaf_basis, local_basis, subtrees):
    count, leaf, rank = leaf_basis.shape
    dim, cols = xt.shape[0], dt.shape[0]
    entries = ids.shape[0]
    return pl.pallas_call(
        functools.partial(up_kernel, (count, leaf, rank, dim, cols)),
        grid_spec=pltpu.PrefetchScalarGridSpec(
            num_scalar_prefetch=1,
            grid=(1,),
            in_specs=[HBM, HBM, VM, VM, VM, HBM, HBM],
            out_specs=[HBM, HBM, VM, VM, VM],
            scratch_shapes=near_scratch(count, entries, leaf, dim, cols)
            + [
                pltpu.VMEM(dt.shape, f32),
                pltpu.VMEM((cols, (2 * count - 2) * rank), f32),
                pltpu.VMEM(leaf_basis.shape, bf16),
                pltpu.VMEM(local_basis.shape, bf16),
                pltpu.VMEM((cols, (2 * count - 1) * rank), bf16),
                pltpu.VMEM((FEAT, (2 * count - 1) * rank), bf16),
                pltpu.VMEM((2 * PAIRS, rank, rank), bf16),
                pltpu.VMEM((16, 128), jnp.int32),
                pltpu.SMEM((16, 128), jnp.int32),
                pltpu.SemaphoreType.DMA((CHUNKS,)),
                pltpu.SemaphoreType.DMA((CHUNKS,)),
                pltpu.SemaphoreType.DMA((5,)),
            ],
        ),
        out_shape=[
            jax.ShapeDtypeStruct((cols, count * leaf), bf16),
            jax.ShapeDtypeStruct((cols, (2 * count - 2) * rank), f32),
            jax.ShapeDtypeStruct((subtrees, cols + dim, rank), bf16),
            jax.ShapeDtypeStruct((16, count), jnp.int32),
            jax.ShapeDtypeStruct((count + 1, cols, leaf), f32),
        ],
        compiler_params=pltpu.CompilerParams(vmem_limit_bytes=60 << 20),
        name="upward",
    )(pos, xt, dt, ids, leaf_pick, local_pick, leaf_basis, local_basis)


def scan_leaf(count, entries, lst, pair):
    def scan(i, pos):
        for e in range(entries):
            pair[pos + e] = i * count + lst[e, i]
        return pos + lst[entries, i]

    return scan


def end_list(count, pair, total):
    for u in range(3 * GROUP):
        pair[total + u] = count * count


def near_pairs(count, total, pair, at, b, w, acc, tiles):
    h = GROUP
    leaf = b.shape[1]
    shift = count.bit_length() - 1

    def first(k, slot):
        code = pair[k]
        tiles[slot] = gauss(b[code & (count - 1)], at[(code >> shift) & (count - 1)])

    def second(k, slot):
        code = pair[k]
        return code >> shift, dot(w[:, lanes(code & (count - 1), leaf)], tiles[slot])

    for u in range(h):
        first(u, u)

    def body(t, carry):
        for phase in range(2):
            k = (2 * t + phase) * h
            got = []
            for u in range(h):
                first(k + h + u, (1 - phase) * h + u)
                got.append(second(k + u, phase * h + u))
            for i, o in got:
                acc[i] += o
        return carry

    blocks = (total + h - 1) // h
    lax.fori_loop(0, (blocks + 1) // 2, body, 0)


def near_scratch(count, entries, leaf, dim, cols):
    return [
        pltpu.SMEM((count * entries + entries + 4 * GROUP,), jnp.int32),
        pltpu.VMEM((2 * GROUP, leaf, leaf), bf16),
        pltpu.VMEM((count, FEAT, leaf), bf16),
        pltpu.VMEM((count, leaf, FEAT), bf16),
        pltpu.VMEM((cols, count * leaf), bf16),
        pltpu.VMEM((dim, count * leaf), bf16),
    ]


def two_sided(count, leaf, target_hbm, source_hbm, x, y, at, b, xs):
    part = count // CHUNKS
    seg = lambda c: pl.ds(c * part * leaf, part * leaf)
    gets = []
    for c in range(CHUNKS):
        gets.append(copy(source_hbm.at[:, seg(c)], y.at[:, seg(c)], xs.at[1, c]))
        gets.append(copy(target_hbm.at[:, seg(c)], x.at[:, seg(c)], xs.at[0, c]))

    def finish(also):
        def prepare(l):
            return feature_pair(x[:, lanes(l, leaf)])[0], feature_pair(y[:, lanes(l, leaf)])[1].T

        def keep(l, got):
            at[l], b[l] = got

        total = 0
        for c in range(CHUNKS):
            gets[2 * c].wait()
            gets[2 * c + 1].wait()
            total = grouped(part, 8, prepare, keep, c * part, also, total)
        return total

    return finish


def near_back_kernel(pos_ref, ids, low_hbm, x_hbm, w_hbm, out,
                     pair, tiles, at, b, w, x, y, acc, lv, lst, xs, sems):
    count, _, leaf = at.shape
    entries = ids.shape[0]
    finish = two_sided(count, leaf, low_hbm, x_hbm, x, y, at, b, xs)
    get_w = copy(w_hbm, w, sems.at[0])
    pos = pos_ref[0]
    low = jnp.where(pos == 0, -(1 << 24), pos * count)
    put_list = put_class(ids[...], low, count, lv, lst, sems.at[1])
    acc[...] = jnp.zeros_like(acc)
    put_list.wait()
    total = finish(scan_leaf(count, entries, lst, pair))
    end_list(count, pair, total)
    get_w.wait()
    near_pairs(count, total, pair, at, b, w, acc, tiles)

    def store(l, got):
        out[:, lanes(l, leaf)] = got.astype(out.dtype)

    grouped(count, 8, lambda l: acc[l], store)


def near_back(pos, ids_low, x_low, x, w, count, leaf):
    dim, cols = x.shape[0], w.shape[0]
    entries = ids_low.shape[0]
    return pl.pallas_call(
        near_back_kernel,
        grid_spec=pltpu.PrefetchScalarGridSpec(
            num_scalar_prefetch=1,
            grid=(1,),
            in_specs=[VM, ANY, HBM, HBM],
            out_specs=VM,
            scratch_shapes=near_scratch(count, entries, leaf, dim, cols)
            + [
                pltpu.VMEM((dim, count * leaf), bf16),
                pltpu.VMEM((count + 1, cols, leaf), f32),
                pltpu.VMEM((16, 128), jnp.int32),
                pltpu.SMEM((16, 128), jnp.int32),
                pltpu.SemaphoreType.DMA((2, CHUNKS)),
                pltpu.SemaphoreType.DMA((2,)),
            ],
        ),
        out_shape=jax.ShapeDtypeStruct((cols, count * leaf), bf16),
        compiler_params=pltpu.CompilerParams(vmem_limit_bytes=52 << 20),
        name="near_back",
    )(pos, ids_low, x_low, x, w)


def down_kernel(dims, pos_ref, lst, ridge, gathered, top_pick, low_hbm, x_hbm, wlow_hbm, own_hbm,
                top_hbm, terms_hbm, local_hbm, leaf_hbm, d_hbm, after, out,
                pair, tiles, at, b, w, x, y, acc, tb, terms, nb, lb, dt, tcoeff, tskel, value, xs, sems):
    count, leaf, rank, dim, cols, subtrees, entries = dims
    finish_features = two_sided(count, leaf, x_hbm, low_hbm, x, y, at, b, xs)
    get_w = copy(wlow_hbm, w, sems.at[0])
    get_acc = copy(own_hbm, acc, sems.at[1])
    pairs = ((top_hbm, tb), (terms_hbm, terms), (local_hbm, nb), (leaf_hbm, lb), (d_hbm, dt))
    total = finish_features(scan_leaf(count, entries, lst, pair))
    end_list(count, pair, total)
    gets = [copy(src, dst, sems.at[k + 2]) for k, (src, dst) in enumerate(pairs)]
    get_w.wait()
    get_acc.wait()
    near_pairs(count, total, pair, at, b, w, acc, tiles)

    pos = pos_ref[0]
    depth = subtrees.bit_length() - 1
    for s in range(subtrees):
        tcoeff[:, lanes(subtrees - 1 + s, rank)] = gathered[s, :cols]
        tskel[:, lanes(subtrees - 1 + s, rank)] = gathered[s, cols:]
    for g in gets:
        g.wait()
    for d in range(depth - 1, 0, -1):

        def climb(j):
            both = lanes(2 * j + 1, rank, 2)
            sel = selector(top_pick[pl.ds(j, 1), :], 2 * rank)
            return dot(tcoeff[:, both], tb[j]).astype(bf16), dot(tskel[:, both], sel).astype(bf16)

        def climb_keep(j, got):
            tcoeff[:, lanes(j, rank)], tskel[:, lanes(j, rank)] = got

        grouped(2**d, 8, climb, climb_keep, 2**d - 1)

    def half(v):
        return (v.astype(f32) * 0.5).astype(bf16)

    top_terms = {}
    for d in range(depth, 0, -1):
        mine = pos >> (depth - d)
        other = mine ^ 1
        own_left = feature_pair(half(tskel[:, lanes(2**d - 1 + mine, rank)]))[0]
        sib_right = feature_pair(half(tskel[:, lanes(2**d - 1 + other, rank)]))[1]
        g = gauss(sib_right.T, own_left)
        top_terms[d] = dot(tcoeff[:, lanes(2**d - 1 + other, rank)], g)
    v = jnp.zeros((cols, rank), bf16)
    for d in range(1, depth + 1):
        parent = pos >> (depth - d + 1)
        down = dot(v, tb[2 ** (d - 1) - 1 + parent], 1, 1)
        right = ((pos >> (depth - d)) & 1) == 1
        v = (top_terms[d] + jnp.where(right, down[:, rank:], down[:, :rank])).astype(bf16)
    value[:, lanes(0, rank)] = v
    local_depth = count.bit_length() - 1
    for d in range(1, local_depth + 1):

        def descend(j):
            down = dot(value[:, lanes(j, rank)], nb[j], 1, 1)
            return (terms[:, lanes(2 * j, rank, 2)] + down).astype(bf16)

        def descend_keep(j, got):
            value[:, lanes(2 * j + 1, rank, 2)] = got

        grouped(2 ** (d - 1), 8, descend, descend_keep, 2 ** (d - 1) - 1)
    row = lax.broadcasted_iota(jnp.int32, (cols, leaf), 0)
    scale = jnp.zeros((cols, leaf), f32)
    for r in range(cols):
        scale = jnp.where(row == r, ridge[r], scale)

    def finish(l):
        far = dot(value[:, lanes(count - 1 + l, rank)], lb[l], 1, 1)
        return scale * dt[:, lanes(l, leaf)] + far + acc[l]

    def finish_keep(l, got):
        out[:, lanes(l, leaf)] = got

    grouped(count, 8, finish, finish_keep)


def downward(pos, lst, ridge, gathered, top_pick, x_low, x, w_low, n_own, top_basis, terms, local_basis, leaf_basis,
             dt, after, entries):
    count, leaf, rank = leaf_basis.shape
    dim, cols = x.shape[0], dt.shape[0]
    subtrees = gathered.shape[0]
    big = (top_basis, terms, local_basis, leaf_basis, dt)
    return pl.pallas_call(
        functools.partial(down_kernel, (count, leaf, rank, dim, cols, subtrees, entries)),
        grid_spec=pltpu.PrefetchScalarGridSpec(
            num_scalar_prefetch=3,
            grid=(1,),
            in_specs=[VM] * 2 + [ANY, HBM, ANY] + [HBM] * 7,
            out_specs=VM,
            scratch_shapes=near_scratch(count, entries, leaf, dim, cols)
            + [pltpu.VMEM((dim, count * leaf), bf16), pltpu.VMEM((count + 1, cols, leaf), f32)]
            + [pltpu.VMEM(a.shape, a.dtype) for a in big]
            + [
                pltpu.VMEM((cols, (2 * subtrees - 1) * rank), bf16),
                pltpu.VMEM((dim, (2 * subtrees - 1) * rank), bf16),
                pltpu.VMEM((cols, (2 * count - 1) * rank), bf16),
                pltpu.SemaphoreType.DMA((2, CHUNKS)),
                pltpu.SemaphoreType.DMA((7,)),
            ],
        ),
        out_shape=jax.ShapeDtypeStruct(dt.shape, f32),
        compiler_params=pltpu.CompilerParams(vmem_limit_bytes=52 << 20),
        name="downward",
    )(pos, lst, ridge, gathered, top_pick, x_low, x, w_low, n_own, *big, after)


def shards(points, direction, ridge, leaf_basis, local_basis, top_basis, leaf_pick, local_pick, top_pick, near_list):
    count, leaf, rank = leaf_basis.shape
    entries = near_list.shape[1]
    chips = lax.axis_size("chip")
    subtrees = lax.axis_size("leaf") * chips
    pos = (lax.axis_index("leaf") * chips + lax.axis_index("chip"))[None]
    upper = [(i, i + 1) for i in range(subtrees - 1)]
    lower = [(i + 1, i) for i in range(subtrees - 1)]

    xt, dt, ids = points.T, direction.T, near_list.T
    x_low = lax.ppermute(xt, AXES, upper)
    ids_low = lax.ppermute(ids, AXES, upper)
    w, terms, spread, list_low, n_own = upward(
        pos, xt, dt, ids, leaf_pick, local_pick, leaf_basis, local_basis, subtrees
    )
    gathered = lax.all_to_all(spread, AXES, 0, 0)
    w_low = lax.ppermute(w, AXES, upper)
    back = near_back(pos, ids_low, x_low, xt, w, count, leaf)
    returned = lax.ppermute(back, AXES, lower)
    out = downward(
        pos, list_low, ridge, gathered, top_pick, x_low, xt, w_low, n_own, top_basis, terms, local_basis, leaf_basis,
        dt, back, entries,
    )
    return (out + returned.astype(f32)).T


def solution(mesh):
    split = P(AXES, None)
    split3 = P(AXES, None, None)
    return jax.shard_map(
        shards,
        mesh=mesh,
        in_specs=(split, split, P(), split3, split3, P(), split, split, P(), split),
        out_specs=split,
        check_vma=False,
    )
```

```python
import functools
import math

import jax
import jax.numpy as jnp
from jax import lax
from jax.experimental import pallas as pl
from jax.experimental.pallas import tpu as pltpu
from jax.sharding import PartitionSpec as P

f32 = jnp.float32
bf16 = jnp.bfloat16
AXES = ("leaf", "chip")
SCALE = math.log2(math.e) / 32.0
FEAT = 128
GROUP = 16


def dot(a, b, ca=1, cb=0):
    return lax.dot_general(a, b, (((ca,), (cb,)), ((), ())), preferred_element_type=f32)


def copy(src, dst, sem):
    c = pltpu.make_async_copy(src, dst, sem)
    c.start()
    return c


VM = pl.BlockSpec(memory_space=pltpu.VMEM)
HBM = pl.BlockSpec(memory_space=pltpu.HBM)
ANY = pl.BlockSpec(memory_space=pl.ANY)


def square_rows(xf):
    n = jnp.sum(xf * xf, axis=0, keepdims=True)
    hi = n.astype(bf16).astype(f32)
    rest = n - hi
    mid = rest.astype(bf16).astype(f32)
    low = rest - mid
    row = lax.broadcasted_iota(jnp.int32, (16, xf.shape[1]), 0)
    zero = jnp.zeros((), f32)
    neg = jnp.where(row == 0, -hi, jnp.where(row == 1, -mid, jnp.where(row == 2, -low, zero)))
    ones = jnp.where(row < 3, jnp.ones((), f32), zero)
    return neg.astype(bf16), ones.astype(bf16)


def feature_pair(x):
    dim, width = x.shape
    xf = x.astype(f32)
    neg, ones = square_rows(xf)
    pad = jnp.zeros((FEAT - dim - 32, width), bf16)
    left = jnp.concatenate([(xf + xf).astype(bf16), ones, neg, pad], 0)
    right = jnp.concatenate([x, neg, ones, pad], 0)
    return left, right


def swap_form(left, dim):
    half = (left[:dim].astype(f32) * 0.5).astype(bf16)
    return jnp.concatenate([half, left[dim + 16 : dim + 32], left[dim : dim + 16], left[dim + 32 :]], 0)


def selector(pick_row, width):
    rows = lax.broadcasted_iota(jnp.int32, (width, pick_row.shape[1]), 0)
    return jnp.where(rows == pick_row, jnp.ones((), f32), jnp.zeros((), f32)).astype(bf16)


def gauss(right_rows, left_cols):
    s = dot(right_rows, left_cols)
    return jnp.exp2(s * SCALE).astype(bf16)


def grouped(count, group, compute, store, start=0, also=None, carry=0):
    group = min(group, count)

    def body(t, carry):
        got = [compute(start + t * group + u) for u in range(group)]
        for u in range(group):
            store(start + t * group + u, got[u])
            if also is not None:
                carry = also(start + t * group + u, carry)
        return carry

    if count == group:
        return body(0, carry)
    return lax.fori_loop(0, count // group, body, carry)


def lanes(start, width, number=1):
    if isinstance(start, int):
        return pl.ds(start * width, number * width)
    return pl.ds(pl.multiple_of(start * width, width), number * width)


CHUNKS = 4
PAIRS = 16


def class_list(ids, low, count):
    entries = ids.shape[0]
    local = ids - low
    inside = (local >= 0) & (local < count)
    ones = inside.astype(jnp.int32)
    rank = [jnp.zeros_like(ones[0:1])]
    for e in range(entries):
        rank.append(rank[-1] + ones[e : e + 1])
    row = lax.broadcasted_iota(jnp.int32, (16, ids.shape[1]), 0)
    out = jnp.where(row == entries, rank[-1], 0)
    for e in range(entries):
        here = (row == rank[e]) & (ones[e : e + 1] == 1)
        out = out + jnp.where(here, local[e : e + 1], 0)
    return out


def up_kernel(dims, pos_ref, x_hbm, d_hbm, ids, leaf_pick, local_pick, leaf_hbm, local_hbm,
              w_hbm, terms_hbm, spread, list_low, acc,
              pair, big, at, b, wt, xt, dt, terms, lb, nb, coeff, skel, tiles, lv, lst, xs, ls, ms):
    count, leaf, rank, dim, cols = dims
    entries = ids.shape[0]
    part = count // CHUNKS
    seg = lambda c: pl.ds(c * part * leaf, part * leaf)
    own = lambda c: pl.ds(c * part, part)
    get_x = [copy(x_hbm.at[:, seg(c)], xt.at[:, seg(c)], xs.at[c]) for c in range(CHUNKS)]
    get_d = copy(d_hbm, dt, ms.at[0])
    pos = pos_ref[0]
    table = ids[...]
    put_list = put_class(table, pos * count, count, lv, lst, ms.at[4])
    list_low[...] = class_list(table, (pos - 1) * count, count)
    acc[...] = jnp.zeros_like(acc)

    def prepare(l):
        left, right = feature_pair(xt[:, lanes(l, leaf)])
        return left, right.T

    def keep(l, got):
        at[l], b[l] = got

    total = 0
    for c in range(CHUNKS):
        get_x[c].wait()
        if c == 0:
            put_list.wait()
        if c == 1:
            get_leaf = [copy(leaf_hbm.at[own(k)], lb.at[own(k)], ls.at[k]) for k in range(CHUNKS)]
            get_local = copy(local_hbm, nb, ms.at[1])
        total = grouped(part, 8, prepare, keep, c * part, scan_leaf(count, entries, lst, pair), total)
    end_list(count, pair, total)
    get_d.wait()
    for c in range(CHUNKS):
        wt[:, seg(c)] = dt[:, seg(c)].astype(bf16)
    puts = [copy(wt, w_hbm, ms.at[2])]
    base = count - 1

    def leaf_step(l):
        c = dot(wt[:, lanes(l, leaf)], lb[l])
        sel = selector(leaf_pick[pl.ds(l, 1), :], leaf)
        return c.astype(bf16), dot(at[l], sel).astype(bf16)

    def leaf_keep(l, got):
        coeff[:, lanes(base + l, rank)], skel[:, lanes(base + l, rank)] = got

    for c in range(CHUNKS):
        get_leaf[c].wait()
        grouped(part, 8, leaf_step, leaf_keep, c * part)
    get_local.wait()
    depth = count.bit_length() - 1
    for d in range(depth, 0, -1):
        up = 2 ** (d - 1) - 1

        def climb(j):
            both = lanes(2 * j + 1, rank, 2)
            sel = selector(local_pick[pl.ds(j, 1), :], 2 * rank)
            return dot(coeff[:, both], nb[j]).astype(bf16), dot(skel[:, both], sel).astype(bf16)

        def climb_keep(j, got):
            coeff[:, lanes(j, rank)], skel[:, lanes(j, rank)] = got

        grouped(2 ** (d - 1), 16, climb, climb_keep, up)
    root_c, root_s = coeff[:, :rank], skel[:dim, :rank]
    for s in range(spread.shape[0]):
        spread[s, :cols, :] = root_c
        spread[s, cols:, :] = root_s

    last = count - 2

    def index(j):
        return min(j, last) if isinstance(j, int) else jnp.minimum(j, last)

    def first(j, slot):
        both = skel[:, lanes(2 * index(j) + 1, rank, 2)]
        tiles[slot] = gauss(swap_form(both[:, rank:], dim).T, both[:, :rank])

    def second(j, slot):
        c2 = coeff[:, lanes(2 * index(j) + 1, rank, 2)]
        g = tiles[slot]
        return jnp.concatenate([dot(c2[:, rank:], g), dot(c2[:, :rank], g, 1, 1)], 1)

    for u in range(PAIRS):
        first(u, u)

    def body(t, carry):
        for phase in range(2):
            k = (2 * t + phase) * PAIRS
            got = []
            for u in range(PAIRS):
                first(k + PAIRS + u, (1 - phase) * PAIRS + u)
                got.append(second(k + u, phase * PAIRS + u))
            for u in range(PAIRS):
                terms[:, lanes(2 * index(k + u), rank, 2)] = got[u]
        return carry

    lax.fori_loop(0, count // (2 * PAIRS), body, 0)
    puts.append(copy(terms, terms_hbm, ms.at[3]))
    near_pairs(count, total, pair, at, b, wt, acc, big)
    for p in puts:
        p.wait()


def put_class(table, low, count, lv, lst, sem):
    lv[...] = jnp.zeros_like(lv)
    lv[:, :count] = class_list(table, low, count)
    return copy(lv, lst, sem)


def upward(pos, xt, dt, ids, leaf_pick, local_pick, leaf_basis, local_basis, subtrees):
    count, leaf, rank = leaf_basis.shape
    dim, cols = xt.shape[0], dt.shape[0]
    entries = ids.shape[0]
    return pl.pallas_call(
        functools.partial(up_kernel, (count, leaf, rank, dim, cols)),
        grid_spec=pltpu.PrefetchScalarGridSpec(
            num_scalar_prefetch=1,
            grid=(1,),
            in_specs=[HBM, HBM, VM, VM, VM, HBM, HBM],
            out_specs=[HBM, HBM, VM, VM, VM],
            scratch_shapes=near_scratch(count, entries, leaf, dim, cols)
            + [
                pltpu.VMEM(dt.shape, f32),
                pltpu.VMEM((cols, (2 * count - 2) * rank), f32),
                pltpu.VMEM(leaf_basis.shape, bf16),
                pltpu.VMEM(local_basis.shape, bf16),
                pltpu.VMEM((cols, (2 * count - 1) * rank), bf16),
                pltpu.VMEM((FEAT, (2 * count - 1) * rank), bf16),
                pltpu.VMEM((2 * PAIRS, rank, rank), bf16),
                pltpu.VMEM((16, 128), jnp.int32),
                pltpu.SMEM((16, 128), jnp.int32),
                pltpu.SemaphoreType.DMA((CHUNKS,)),
                pltpu.SemaphoreType.DMA((CHUNKS,)),
                pltpu.SemaphoreType.DMA((5,)),
            ],
        ),
        out_shape=[
            jax.ShapeDtypeStruct((cols, count * leaf), bf16),
            jax.ShapeDtypeStruct((cols, (2 * count - 2) * rank), f32),
            jax.ShapeDtypeStruct((subtrees, cols + dim, rank), bf16),
            jax.ShapeDtypeStruct((16, count), jnp.int32),
            jax.ShapeDtypeStruct((count + 1, cols, leaf), f32),
        ],
        compiler_params=pltpu.CompilerParams(vmem_limit_bytes=60 << 20),
        name="upward",
    )(pos, xt, dt, ids, leaf_pick, local_pick, leaf_basis, local_basis)


def scan_leaf(count, entries, lst, pair):
    def scan(i, pos):
        for e in range(entries):
            pair[pos + e] = i * count + lst[e, i]
        return pos + lst[entries, i]

    return scan


def end_list(count, pair, total):
    for u in range(3 * GROUP):
        pair[total + u] = count * count


def near_pairs(count, total, pair, at, b, w, acc, tiles):
    h = GROUP
    leaf = b.shape[1]
    shift = count.bit_length() - 1

    def first(k, slot):
        code = pair[k]
        tiles[slot] = gauss(b[code & (count - 1)], at[(code >> shift) & (count - 1)])

    def second(k, slot):
        code = pair[k]
        return code >> shift, dot(w[:, lanes(code & (count - 1), leaf)], tiles[slot])

    for u in range(h):
        first(u, u)

    def body(t, carry):
        for phase in range(2):
            k = (2 * t + phase) * h
            got = []
            for u in range(h):
                first(k + h + u, (1 - phase) * h + u)
                got.append(second(k + u, phase * h + u))
            for i, o in got:
                acc[i] += o
        return carry

    blocks = (total + h - 1) // h
    lax.fori_loop(0, (blocks + 1) // 2, body, 0)


def near_scratch(count, entries, leaf, dim, cols):
    return [
        pltpu.SMEM((count * entries + entries + 4 * GROUP,), jnp.int32),
        pltpu.VMEM((2 * GROUP, leaf, leaf), bf16),
        pltpu.VMEM((count, FEAT, leaf), bf16),
        pltpu.VMEM((count, leaf, FEAT), bf16),
        pltpu.VMEM((cols, count * leaf), bf16),
        pltpu.VMEM((dim, count * leaf), bf16),
    ]


def two_sided(count, leaf, target_hbm, source_hbm, x, y, at, b, xs):
    part = count // CHUNKS
    seg = lambda c: pl.ds(c * part * leaf, part * leaf)
    gets = []
    for c in range(CHUNKS):
        gets.append(copy(source_hbm.at[:, seg(c)], y.at[:, seg(c)], xs.at[1, c]))
        gets.append(copy(target_hbm.at[:, seg(c)], x.at[:, seg(c)], xs.at[0, c]))

    def finish(also):
        def prepare(l):
            return feature_pair(x[:, lanes(l, leaf)])[0], feature_pair(y[:, lanes(l, leaf)])[1].T

        def keep(l, got):
            at[l], b[l] = got

        total = 0
        for c in range(CHUNKS):
            gets[2 * c].wait()
            gets[2 * c + 1].wait()
            total = grouped(part, 8, prepare, keep, c * part, also, total)
        return total

    return finish


def near_back_kernel(pos_ref, ids, low_hbm, x_hbm, w_hbm, out,
                     pair, tiles, at, b, w, x, y, acc, lv, lst, xs, sems):
    count, _, leaf = at.shape
    entries = ids.shape[0]
    finish = two_sided(count, leaf, low_hbm, x_hbm, x, y, at, b, xs)
    get_w = copy(w_hbm, w, sems.at[0])
    pos = pos_ref[0]
    low = jnp.where(pos == 0, -(1 << 24), pos * count)
    put_list = put_class(ids[...], low, count, lv, lst, sems.at[1])
    acc[...] = jnp.zeros_like(acc)
    put_list.wait()
    total = finish(scan_leaf(count, entries, lst, pair))
    end_list(count, pair, total)
    get_w.wait()
    near_pairs(count, total, pair, at, b, w, acc, tiles)

    def store(l, got):
        out[:, lanes(l, leaf)] = got.astype(out.dtype)

    grouped(count, 8, lambda l: acc[l], store)


def near_back(pos, ids_low, x_low, x, w, count, leaf):
    dim, cols = x.shape[0], w.shape[0]
    entries = ids_low.shape[0]
    return pl.pallas_call(
        near_back_kernel,
        grid_spec=pltpu.PrefetchScalarGridSpec(
            num_scalar_prefetch=1,
            grid=(1,),
            in_specs=[VM, ANY, HBM, HBM],
            out_specs=VM,
            scratch_shapes=near_scratch(count, entries, leaf, dim, cols)
            + [
                pltpu.VMEM((dim, count * leaf), bf16),
                pltpu.VMEM((count + 1, cols, leaf), f32),
                pltpu.VMEM((16, 128), jnp.int32),
                pltpu.SMEM((16, 128), jnp.int32),
                pltpu.SemaphoreType.DMA((2, CHUNKS)),
                pltpu.SemaphoreType.DMA((2,)),
            ],
        ),
        out_shape=jax.ShapeDtypeStruct((cols, count * leaf), bf16),
        compiler_params=pltpu.CompilerParams(vmem_limit_bytes=52 << 20),
        name="near_back",
    )(pos, ids_low, x_low, x, w)


def down_kernel(dims, pos_ref, lst, ridge, gathered, top_pick, low_hbm, x_hbm, wlow_hbm, own_hbm,
                top_hbm, terms_hbm, local_hbm, leaf_hbm, d_hbm, after, out,
                pair, tiles, at, b, w, x, y, acc, tb, terms, nb, lb, dt, tcoeff, tskel, value, xs, sems):
    count, leaf, rank, dim, cols, subtrees, entries = dims
    finish_features = two_sided(count, leaf, x_hbm, low_hbm, x, y, at, b, xs)
    get_w = copy(wlow_hbm, w, sems.at[0])
    get_acc = copy(own_hbm, acc, sems.at[1])
    pairs = ((top_hbm, tb), (terms_hbm, terms), (local_hbm, nb), (leaf_hbm, lb), (d_hbm, dt))
    total = finish_features(scan_leaf(count, entries, lst, pair))
    end_list(count, pair, total)
    gets = [copy(src, dst, sems.at[k + 2]) for k, (src, dst) in enumerate(pairs)]
    get_w.wait()
    get_acc.wait()
    near_pairs(count, total, pair, at, b, w, acc, tiles)

    pos = pos_ref[0]
    depth = subtrees.bit_length() - 1
    for s in range(subtrees):
        tcoeff[:, lanes(subtrees - 1 + s, rank)] = gathered[s, :cols]
        tskel[:, lanes(subtrees - 1 + s, rank)] = gathered[s, cols:]
    for g in gets:
        g.wait()
    for d in range(depth - 1, 0, -1):

        def climb(j):
            both = lanes(2 * j + 1, rank, 2)
            sel = selector(top_pick[pl.ds(j, 1), :], 2 * rank)
            return dot(tcoeff[:, both], tb[j]).astype(bf16), dot(tskel[:, both], sel).astype(bf16)

        def climb_keep(j, got):
            tcoeff[:, lanes(j, rank)], tskel[:, lanes(j, rank)] = got

        grouped(2**d, 8, climb, climb_keep, 2**d - 1)

    def half(v):
        return (v.astype(f32) * 0.5).astype(bf16)

    top_terms = {}
    for d in range(depth, 0, -1):
        mine = pos >> (depth - d)
        other = mine ^ 1
        own_left = feature_pair(half(tskel[:, lanes(2**d - 1 + mine, rank)]))[0]
        sib_right = feature_pair(half(tskel[:, lanes(2**d - 1 + other, rank)]))[1]
        g = gauss(sib_right.T, own_left)
        top_terms[d] = dot(tcoeff[:, lanes(2**d - 1 + other, rank)], g)
    v = jnp.zeros((cols, rank), bf16)
    for d in range(1, depth + 1):
        parent = pos >> (depth - d + 1)
        down = dot(v, tb[2 ** (d - 1) - 1 + parent], 1, 1)
        right = ((pos >> (depth - d)) & 1) == 1
        v = (top_terms[d] + jnp.where(right, down[:, rank:], down[:, :rank])).astype(bf16)
    value[:, lanes(0, rank)] = v
    local_depth = count.bit_length() - 1
    for d in range(1, local_depth + 1):

        def descend(j):
            down = dot(value[:, lanes(j, rank)], nb[j], 1, 1)
            return (terms[:, lanes(2 * j, rank, 2)] + down).astype(bf16)

        def descend_keep(j, got):
            value[:, lanes(2 * j + 1, rank, 2)] = got

        grouped(2 ** (d - 1), 8, descend, descend_keep, 2 ** (d - 1) - 1)
    row = lax.broadcasted_iota(jnp.int32, (cols, leaf), 0)
    scale = jnp.zeros((cols, leaf), f32)
    for r in range(cols):
        scale = jnp.where(row == r, ridge[r], scale)

    def finish(l):
        far = dot(value[:, lanes(count - 1 + l, rank)], lb[l], 1, 1)
        return scale * dt[:, lanes(l, leaf)] + far + acc[l]

    def finish_keep(l, got):
        out[:, lanes(l, leaf)] = got

    grouped(count, 8, finish, finish_keep)


def downward(pos, lst, ridge, gathered, top_pick, x_low, x, w_low, n_own, top_basis, terms, local_basis, leaf_basis,
             dt, after, entries):
    count, leaf, rank = leaf_basis.shape
    dim, cols = x.shape[0], dt.shape[0]
    subtrees = gathered.shape[0]
    big = (top_basis, terms, local_basis, leaf_basis, dt)
    return pl.pallas_call(
        functools.partial(down_kernel, (count, leaf, rank, dim, cols, subtrees, entries)),
        grid_spec=pltpu.PrefetchScalarGridSpec(
            num_scalar_prefetch=3,
            grid=(1,),
            in_specs=[VM] * 2 + [ANY, HBM, ANY] + [HBM] * 7,
            out_specs=VM,
            scratch_shapes=near_scratch(count, entries, leaf, dim, cols)
            + [pltpu.VMEM((dim, count * leaf), bf16), pltpu.VMEM((count + 1, cols, leaf), f32)]
            + [pltpu.VMEM(a.shape, a.dtype) for a in big]
            + [
                pltpu.VMEM((cols, (2 * subtrees - 1) * rank), bf16),
                pltpu.VMEM((dim, (2 * subtrees - 1) * rank), bf16),
                pltpu.VMEM((cols, (2 * count - 1) * rank), bf16),
                pltpu.SemaphoreType.DMA((2, CHUNKS)),
                pltpu.SemaphoreType.DMA((7,)),
            ],
        ),
        out_shape=jax.ShapeDtypeStruct(dt.shape, f32),
        compiler_params=pltpu.CompilerParams(vmem_limit_bytes=52 << 20),
        name="downward",
    )(pos, lst, ridge, gathered, top_pick, x_low, x, w_low, n_own, *big, after)


def shards(points, direction, ridge, leaf_basis, local_basis, top_basis, leaf_pick, local_pick, top_pick, near_list):
    count, leaf, rank = leaf_basis.shape
    entries = near_list.shape[1]
    chips = lax.axis_size("chip")
    subtrees = lax.axis_size("leaf") * chips
    pos = (lax.axis_index("leaf") * chips + lax.axis_index("chip"))[None]
    upper = [(i, i + 1) for i in range(subtrees - 1)]
    lower = [(i + 1, i) for i in range(subtrees - 1)]

    xt, dt, ids = points.T, direction.T, near_list.T
    ids_low = lax.ppermute(ids, AXES, upper)
    x_sent, ids_low = lax.optimization_barrier((xt, ids_low))
    x_low = lax.ppermute(x_sent, AXES, upper)
    w, terms, spread, list_low, n_own = upward(
        pos, xt, dt, ids, leaf_pick, local_pick, leaf_basis, local_basis, subtrees
    )
    gathered = lax.all_to_all(spread, AXES, 0, 0)
    w_low = lax.ppermute(w, AXES, upper)
    back = near_back(pos, ids_low, x_low, xt, w, count, leaf)
    returned = lax.ppermute(back, AXES, lower)
    out = downward(
        pos, list_low, ridge, gathered, top_pick, x_low, xt, w_low, n_own, top_basis, terms, local_basis, leaf_basis,
        dt, back, entries,
    )
    return (out + returned.astype(f32)).T


def solution(mesh):
    split = P(AXES, None)
    split3 = P(AXES, None, None)
    return jax.shard_map(
        shards,
        mesh=mesh,
        in_specs=(split, split, P(), split3, split3, P(), split, split, P(), split),
        out_specs=split,
        check_vma=False,
    )
```

```python
import functools
import math

import jax
import jax.numpy as jnp
from jax import lax
from jax.experimental import pallas as pl
from jax.experimental.pallas import tpu as pltpu
from jax.sharding import PartitionSpec as P

f32 = jnp.float32
bf16 = jnp.bfloat16
AXES = ("leaf", "chip")
SCALE = math.log2(math.e) / 32.0
FEAT = 128
GROUP = 16


def dot(a, b, ca=1, cb=0):
    return lax.dot_general(a, b, (((ca,), (cb,)), ((), ())), preferred_element_type=f32)


def copy(src, dst, sem):
    c = pltpu.make_async_copy(src, dst, sem)
    c.start()
    return c


def near_cost(pairs, leaf, cols, data):
    return pl.CostEstimate(
        flops=pairs * 2 * leaf * leaf * (2 * FEAT + leaf), transcendentals=pairs * leaf * leaf, bytes_accessed=data
    )


VM = pl.BlockSpec(memory_space=pltpu.VMEM)
HBM = pl.BlockSpec(memory_space=pltpu.HBM)
ANY = pl.BlockSpec(memory_space=pl.ANY)


def square_rows(xf):
    n = jnp.sum(xf * xf, axis=0, keepdims=True)
    hi = n.astype(bf16).astype(f32)
    rest = n - hi
    mid = rest.astype(bf16).astype(f32)
    low = rest - mid
    row = lax.broadcasted_iota(jnp.int32, (16, xf.shape[1]), 0)
    zero = jnp.zeros((), f32)
    neg = jnp.where(row == 0, -hi, jnp.where(row == 1, -mid, jnp.where(row == 2, -low, zero)))
    ones = jnp.where(row < 3, jnp.ones((), f32), zero)
    return neg.astype(bf16), ones.astype(bf16)


def feature_pair(x):
    dim, width = x.shape
    xf = x.astype(f32)
    neg, ones = square_rows(xf)
    pad = jnp.zeros((FEAT - dim - 32, width), bf16)
    left = jnp.concatenate([(xf + xf).astype(bf16), ones, neg, pad], 0)
    right = jnp.concatenate([x, neg, ones, pad], 0)
    return left, right


def swap_form(left, dim):
    half = (left[:dim].astype(f32) * 0.5).astype(bf16)
    return jnp.concatenate([half, left[dim + 16 : dim + 32], left[dim : dim + 16], left[dim + 32 :]], 0)


def selector(pick_row, width):
    rows = lax.broadcasted_iota(jnp.int32, (width, pick_row.shape[1]), 0)
    return jnp.where(rows == pick_row, jnp.ones((), f32), jnp.zeros((), f32)).astype(bf16)


def gauss(right_rows, left_cols):
    s = dot(right_rows, left_cols)
    return jnp.exp2(s * SCALE).astype(bf16)


def grouped(count, group, compute, store, start=0, also=None, carry=0):
    group = min(group, count)

    def body(t, carry):
        got = [compute(start + t * group + u) for u in range(group)]
        for u in range(group):
            store(start + t * group + u, got[u])
            if also is not None:
                carry = also(start + t * group + u, carry)
        return carry

    if count == group:
        return body(0, carry)
    return lax.fori_loop(0, count // group, body, carry)


def lanes(start, width, number=1):
    if isinstance(start, int):
        return pl.ds(start * width, number * width)
    return pl.ds(pl.multiple_of(start * width, width), number * width)


CHUNKS = 4
PAIRS = 16


def class_list(ids, low, count):
    entries = ids.shape[0]
    local = ids - low
    inside = (local >= 0) & (local < count)
    ones = inside.astype(jnp.int32)
    rank = [jnp.zeros_like(ones[0:1])]
    for e in range(entries):
        rank.append(rank[-1] + ones[e : e + 1])
    row = lax.broadcasted_iota(jnp.int32, (16, ids.shape[1]), 0)
    out = jnp.where(row == entries, rank[-1], 0)
    for e in range(entries):
        here = (row == rank[e]) & (ones[e : e + 1] == 1)
        out = out + jnp.where(here, local[e : e + 1], 0)
    return out


def pack_kernel(pos_ref, d_hbm, ids, out, dt, sems):
    cols, width = dt.shape
    count = ids.shape[1]
    part = width // CHUNKS
    gets = [copy(d_hbm.at[:, pl.ds(c * part, part)], dt.at[:, pl.ds(c * part, part)], sems.at[c]) for c in range(CHUNKS)]
    out[:, pl.ds(width, 128)] = jnp.zeros((cols, 128), bf16)
    out[:, pl.ds(width, count)] = class_list(ids[...], (pos_ref[0] + 1) * count, count).astype(f32).astype(bf16)
    for c in range(CHUNKS):
        gets[c].wait()
        s = pl.ds(c * part, part)
        out[:, s] = dt[:, s].astype(bf16)


def pack(pos, dt, ids):
    cols, width = dt.shape
    return pl.pallas_call(
        pack_kernel,
        grid_spec=pltpu.PrefetchScalarGridSpec(
            num_scalar_prefetch=1,
            grid=(1,),
            in_specs=[HBM, VM],
            out_specs=VM,
            scratch_shapes=[pltpu.VMEM(dt.shape, f32), pltpu.SemaphoreType.DMA((CHUNKS,))],
        ),
        out_shape=jax.ShapeDtypeStruct((cols, width + 128), bf16),
        compiler_params=pltpu.CompilerParams(vmem_limit_bytes=60 << 20),
        name="pack",
    )(pos, dt, ids)


def up_kernel(dims, pos_ref, x_hbm, w_hbm, ids, leaf_pick, local_pick, leaf_hbm, local_hbm,
              terms_hbm, spread, list_low, acc,
              pair, big, at, b, wt, xt, terms, lb, nb, coeff, skel, tiles, lv, lst, xs, ls, ms):
    count, leaf, rank, dim, cols = dims
    entries = ids.shape[0]
    part = count // CHUNKS
    seg = lambda c: pl.ds(c * part * leaf, part * leaf)
    own = lambda c: pl.ds(c * part, part)
    get_x = [copy(x_hbm.at[:, seg(c)], xt.at[:, seg(c)], xs.at[c]) for c in range(CHUNKS)]
    get_w = copy(w_hbm, wt, ms.at[0])
    pos = pos_ref[0]
    table = ids[...]
    put_list = put_class(table, pos * count, count, lv, lst, ms.at[3])
    list_low[...] = class_list(table, (pos - 1) * count, count)
    acc[...] = jnp.zeros_like(acc)

    def prepare(l):
        left, right = feature_pair(xt[:, lanes(l, leaf)])
        return left, right.T

    def keep(l, got):
        at[l], b[l] = got

    total = 0
    for c in range(CHUNKS):
        get_x[c].wait()
        if c == 0:
            put_list.wait()
        if c == 1:
            get_leaf = [copy(leaf_hbm.at[own(k)], lb.at[own(k)], ls.at[k]) for k in range(CHUNKS)]
            get_local = copy(local_hbm, nb, ms.at[1])
        total = grouped(part, 16, prepare, keep, c * part, scan_leaf(count, entries, lst, pair), total)
    end_list(count, pair, total)
    get_w.wait()
    base = count - 1

    def leaf_step(l):
        c = dot(wt[:, lanes(l, leaf)], lb[l])
        sel = selector(leaf_pick[pl.ds(l, 1), :], leaf)
        return c.astype(bf16), dot(at[l], sel).astype(bf16)

    def leaf_keep(l, got):
        coeff[:, lanes(base + l, rank)], skel[:, lanes(base + l, rank)] = got

    for c in range(CHUNKS):
        get_leaf[c].wait()
        grouped(part, 16, leaf_step, leaf_keep, c * part)
    get_local.wait()
    depth = count.bit_length() - 1
    for d in range(depth, 0, -1):
        up = 2 ** (d - 1) - 1

        def climb(j):
            both = lanes(2 * j + 1, rank, 2)
            sel = selector(local_pick[pl.ds(j, 1), :], 2 * rank)
            return dot(coeff[:, both], nb[j]).astype(bf16), dot(skel[:, both], sel).astype(bf16)

        def climb_keep(j, got):
            coeff[:, lanes(j, rank)], skel[:, lanes(j, rank)] = got

        grouped(2 ** (d - 1), 32, climb, climb_keep, up)
    root_c, root_s = coeff[:, :rank], skel[:dim, :rank]
    for s in range(spread.shape[0]):
        spread[s, :cols, :] = root_c
        spread[s, cols:, :] = root_s

    last = count - 2

    def index(j):
        return min(j, last) if isinstance(j, int) else jnp.minimum(j, last)

    def first(j, slot):
        both = skel[:, lanes(2 * index(j) + 1, rank, 2)]
        tiles[slot] = gauss(swap_form(both[:, rank:], dim).T, both[:, :rank])

    def second(j, slot):
        c2 = coeff[:, lanes(2 * index(j) + 1, rank, 2)]
        g = tiles[slot]
        return jnp.concatenate([dot(c2[:, rank:], g), dot(c2[:, :rank], g, 1, 1)], 1)

    for u in range(PAIRS):
        first(u, u)

    def body(t, carry):
        for phase in range(2):
            k = (2 * t + phase) * PAIRS
            got = []
            for u in range(PAIRS):
                first(k + PAIRS + u, (1 - phase) * PAIRS + u)
                got.append(second(k + u, phase * PAIRS + u))
            for u in range(PAIRS):
                terms[:, lanes(2 * index(k + u), rank, 2)] = got[u]
        return carry

    lax.fori_loop(0, count // (2 * PAIRS), body, 0)
    put_terms = copy(terms, terms_hbm, ms.at[2])
    near_pairs(count, total, pair, at, b, wt, acc, big)
    put_terms.wait()


def put_class(table, low, count, lv, lst, sem):
    lv[...] = jnp.zeros_like(lv)
    lv[:, :count] = class_list(table, low, count)
    return copy(lv, lst, sem)


def upward(pos, xt, w, ids, leaf_pick, local_pick, leaf_basis, local_basis, subtrees):
    count, leaf, rank = leaf_basis.shape
    dim, cols = xt.shape[0], w.shape[0]
    entries = ids.shape[0]
    return pl.pallas_call(
        functools.partial(up_kernel, (count, leaf, rank, dim, cols)),
        grid_spec=pltpu.PrefetchScalarGridSpec(
            num_scalar_prefetch=1,
            grid=(1,),
            in_specs=[HBM, HBM, VM, VM, VM, HBM, HBM],
            out_specs=[HBM, VM, VM, VM],
            scratch_shapes=near_scratch(count, entries, leaf, dim, cols)
            + [
                pltpu.VMEM((cols, (2 * count - 2) * rank), f32),
                pltpu.VMEM(leaf_basis.shape, bf16),
                pltpu.VMEM(local_basis.shape, bf16),
                pltpu.VMEM((cols, (2 * count - 1) * rank), bf16),
                pltpu.VMEM((FEAT, (2 * count - 1) * rank), bf16),
                pltpu.VMEM((2 * PAIRS, rank, rank), bf16),
                pltpu.VMEM((16, 128), jnp.int32),
                pltpu.SMEM((16, 128), jnp.int32),
                pltpu.SemaphoreType.DMA((CHUNKS,)),
                pltpu.SemaphoreType.DMA((CHUNKS,)),
                pltpu.SemaphoreType.DMA((4,)),
            ],
        ),
        out_shape=[
            jax.ShapeDtypeStruct((cols, (2 * count - 2) * rank), f32),
            jax.ShapeDtypeStruct((subtrees, cols + dim, rank), bf16),
            jax.ShapeDtypeStruct((16, count), jnp.int32),
            jax.ShapeDtypeStruct((count + 1, cols, leaf), f32),
        ],
        compiler_params=pltpu.CompilerParams(vmem_limit_bytes=60 << 20),
        cost_estimate=near_cost(12 * count, leaf, cols, 16 << 20),
        name="upward",
    )(pos, xt, w, ids, leaf_pick, local_pick, leaf_basis, local_basis)


def scan_leaf(count, entries, lst, pair):
    def scan(i, pos):
        for e in range(entries):
            pair[pos + e] = i * count + lst[e, i]
        return pos + lst[entries, i]

    return scan


def end_list(count, pair, total):
    for u in range(3 * GROUP):
        pair[total + u] = count * count


def near_pairs(count, total, pair, at, b, w, acc, tiles):
    h = GROUP
    leaf = b.shape[1]
    shift = count.bit_length() - 1

    def first(k, slot):
        code = pair[k]
        tiles[slot] = gauss(b[code & (count - 1)], at[(code >> shift) & (count - 1)])

    def second(k, slot):
        code = pair[k]
        return code >> shift, dot(w[:, lanes(code & (count - 1), leaf)], tiles[slot])

    for u in range(h):
        first(u, u)

    def body(t, carry):
        for phase in range(2):
            k = (2 * t + phase) * h
            got = []
            for u in range(h):
                first(k + h + u, (1 - phase) * h + u)
                got.append(second(k + u, phase * h + u))
            for i, o in got:
                acc[i] += o
        return carry

    blocks = (total + h - 1) // h
    lax.fori_loop(0, (blocks + 1) // 2, body, 0)


def near_scratch(count, entries, leaf, dim, cols):
    return [
        pltpu.SMEM((count * entries + entries + 4 * GROUP,), jnp.int32),
        pltpu.VMEM((2 * GROUP, leaf, leaf), bf16),
        pltpu.VMEM((count, FEAT, leaf), bf16),
        pltpu.VMEM((count, leaf, FEAT), bf16),
        pltpu.VMEM((cols, count * leaf + 128), bf16),
        pltpu.VMEM((dim, count * leaf), bf16),
    ]


def two_sided(count, leaf, target_hbm, source_hbm, x, y, at, b, xs):
    part = count // CHUNKS
    seg = lambda c: pl.ds(c * part * leaf, part * leaf)
    gets = []
    for c in range(CHUNKS):
        gets.append(copy(source_hbm.at[:, seg(c)], y.at[:, seg(c)], xs.at[1, c]))
        gets.append(copy(target_hbm.at[:, seg(c)], x.at[:, seg(c)], xs.at[0, c]))

    def finish(also):
        def prepare(l):
            return feature_pair(x[:, lanes(l, leaf)])[0], feature_pair(y[:, lanes(l, leaf)])[1].T

        def keep(l, got):
            at[l], b[l] = got

        total = 0
        for c in range(CHUNKS):
            gets[2 * c].wait()
            gets[2 * c + 1].wait()
            total = grouped(part, 16, prepare, keep, c * part, also, total)
        return total

    return finish


def near_back_kernel(entries, low_hbm, x_hbm, wlow_hbm, w_hbm, out,
                     pair, tiles, at, b, w, x, y, acc, lf, lv, lst, xs, sems):
    count, _, leaf = at.shape
    get_list = copy(wlow_hbm.at[:, pl.ds(count * leaf, 128)], lf, sems.at[0])
    finish = two_sided(count, leaf, low_hbm, x_hbm, x, y, at, b, xs)
    get_w = copy(w_hbm, w, sems.at[1])
    get_list.wait()
    lv[...] = lf[...].astype(f32).astype(jnp.int32)
    put_list = copy(lv, lst, sems.at[2])
    acc[...] = jnp.zeros_like(acc)
    put_list.wait()
    total = finish(scan_leaf(count, entries, lst, pair))
    end_list(count, pair, total)
    get_w.wait()
    near_pairs(count, total, pair, at, b, w, acc, tiles)

    def store(l, got):
        out[:, lanes(l, leaf)] = got.astype(out.dtype)

    grouped(count, 8, lambda l: acc[l], store)


def near_back(x_low, x, w_low, w, after, count, entries, leaf):
    dim, cols = x.shape[0], w.shape[0]

    def kernel(low_hbm, x_hbm, wlow_hbm, w_hbm, after_hbm, *rest):
        near_back_kernel(entries, low_hbm, x_hbm, wlow_hbm, w_hbm, *rest)

    return pl.pallas_call(
        kernel,
        grid_spec=pltpu.PrefetchScalarGridSpec(
            num_scalar_prefetch=0,
            grid=(1,),
            in_specs=[ANY, HBM, ANY, HBM, HBM],
            out_specs=VM,
            scratch_shapes=near_scratch(count, entries, leaf, dim, cols)
            + [
                pltpu.VMEM((dim, count * leaf), bf16),
                pltpu.VMEM((count + 1, cols, leaf), f32),
                pltpu.VMEM((cols, 128), bf16),
                pltpu.VMEM((cols, 128), jnp.int32),
                pltpu.SMEM((cols, 128), jnp.int32),
                pltpu.SemaphoreType.DMA((2, CHUNKS)),
                pltpu.SemaphoreType.DMA((3,)),
            ],
        ),
        out_shape=jax.ShapeDtypeStruct((cols, count * leaf), bf16),
        compiler_params=pltpu.CompilerParams(vmem_limit_bytes=52 << 20),
        cost_estimate=near_cost(4 * count, leaf, cols, 6 << 20),
        name="near_back",
    )(x_low, x, w_low, w, after)


def down_kernel(dims, pos_ref, lst, ridge, gathered, top_pick, low_hbm, x_hbm, wlow_hbm, own_hbm,
                top_hbm, terms_hbm, local_hbm, leaf_hbm, d_hbm, after, out,
                pair, tiles, at, b, w, x, y, acc, tb, terms, nb, lb, dt, tcoeff, tskel, value, xs, sems):
    count, leaf, rank, dim, cols, subtrees, entries = dims
    finish_features = two_sided(count, leaf, x_hbm, low_hbm, x, y, at, b, xs)
    get_w = copy(wlow_hbm, w, sems.at[0])
    get_acc = copy(own_hbm, acc, sems.at[1])
    pairs = ((top_hbm, tb), (terms_hbm, terms), (local_hbm, nb), (leaf_hbm, lb), (d_hbm, dt))
    total = finish_features(scan_leaf(count, entries, lst, pair))
    end_list(count, pair, total)
    gets = [copy(src, dst, sems.at[k + 2]) for k, (src, dst) in enumerate(pairs)]
    get_w.wait()
    get_acc.wait()
    near_pairs(count, total, pair, at, b, w, acc, tiles)

    pos = pos_ref[0]
    depth = subtrees.bit_length() - 1
    for s in range(subtrees):
        tcoeff[:, lanes(subtrees - 1 + s, rank)] = gathered[s, :cols]
        tskel[:, lanes(subtrees - 1 + s, rank)] = gathered[s, cols:]
    for g in gets:
        g.wait()
    for d in range(depth - 1, 0, -1):

        def climb(j):
            both = lanes(2 * j + 1, rank, 2)
            sel = selector(top_pick[pl.ds(j, 1), :], 2 * rank)
            return dot(tcoeff[:, both], tb[j]).astype(bf16), dot(tskel[:, both], sel).astype(bf16)

        def climb_keep(j, got):
            tcoeff[:, lanes(j, rank)], tskel[:, lanes(j, rank)] = got

        grouped(2**d, 16, climb, climb_keep, 2**d - 1)

    def half(v):
        return (v.astype(f32) * 0.5).astype(bf16)

    top_terms = {}
    for d in range(depth, 0, -1):
        mine = pos >> (depth - d)
        other = mine ^ 1
        own_left = feature_pair(half(tskel[:, lanes(2**d - 1 + mine, rank)]))[0]
        sib_right = feature_pair(half(tskel[:, lanes(2**d - 1 + other, rank)]))[1]
        g = gauss(sib_right.T, own_left)
        top_terms[d] = dot(tcoeff[:, lanes(2**d - 1 + other, rank)], g)
    v = jnp.zeros((cols, rank), bf16)
    for d in range(1, depth + 1):
        parent = pos >> (depth - d + 1)
        down = dot(v, tb[2 ** (d - 1) - 1 + parent], 1, 1)
        right = ((pos >> (depth - d)) & 1) == 1
        v = (top_terms[d] + jnp.where(right, down[:, rank:], down[:, :rank])).astype(bf16)
    value[:, lanes(0, rank)] = v
    local_depth = count.bit_length() - 1
    for d in range(1, local_depth + 1):

        def descend(j):
            down = dot(value[:, lanes(j, rank)], nb[j], 1, 1)
            return (terms[:, lanes(2 * j, rank, 2)] + down).astype(bf16)

        def descend_keep(j, got):
            value[:, lanes(2 * j + 1, rank, 2)] = got

        grouped(2 ** (d - 1), 32, descend, descend_keep, 2 ** (d - 1) - 1)
    row = lax.broadcasted_iota(jnp.int32, (cols, leaf), 0)
    scale = jnp.zeros((cols, leaf), f32)
    for r in range(cols):
        scale = jnp.where(row == r, ridge[r], scale)

    def finish(l):
        far = dot(value[:, lanes(count - 1 + l, rank)], lb[l], 1, 1)
        return scale * dt[:, lanes(l, leaf)] + far + acc[l]

    def finish_keep(l, got):
        out[:, lanes(l, leaf)] = got

    grouped(count, 16, finish, finish_keep)


def downward(pos, lst, ridge, gathered, top_pick, x_low, x, w_low, n_own, top_basis, terms, local_basis, leaf_basis,
             dt, after, entries):
    count, leaf, rank = leaf_basis.shape
    dim, cols = x.shape[0], dt.shape[0]
    subtrees = gathered.shape[0]
    big = (top_basis, terms, local_basis, leaf_basis, dt)
    return pl.pallas_call(
        functools.partial(down_kernel, (count, leaf, rank, dim, cols, subtrees, entries)),
        grid_spec=pltpu.PrefetchScalarGridSpec(
            num_scalar_prefetch=3,
            grid=(1,),
            in_specs=[VM] * 2 + [ANY, HBM, ANY] + [HBM] * 7,
            out_specs=VM,
            scratch_shapes=near_scratch(count, entries, leaf, dim, cols)
            + [pltpu.VMEM((dim, count * leaf), bf16), pltpu.VMEM((count + 1, cols, leaf), f32)]
            + [pltpu.VMEM(a.shape, a.dtype) for a in big]
            + [
                pltpu.VMEM((cols, (2 * subtrees - 1) * rank), bf16),
                pltpu.VMEM((dim, (2 * subtrees - 1) * rank), bf16),
                pltpu.VMEM((cols, (2 * count - 1) * rank), bf16),
                pltpu.SemaphoreType.DMA((2, CHUNKS)),
                pltpu.SemaphoreType.DMA((7,)),
            ],
        ),
        out_shape=jax.ShapeDtypeStruct(dt.shape, f32),
        compiler_params=pltpu.CompilerParams(vmem_limit_bytes=52 << 20),
        cost_estimate=near_cost(8 * count, leaf, cols, 20 << 20),
        name="downward",
    )(pos, lst, ridge, gathered, top_pick, x_low, x, w_low, n_own, *big, after)


def shards(points, direction, ridge, leaf_basis, local_basis, top_basis, leaf_pick, local_pick, top_pick, near_list):
    count, leaf, rank = leaf_basis.shape
    entries = near_list.shape[1]
    chips = lax.axis_size("chip")
    subtrees = lax.axis_size("leaf") * chips
    pos = (lax.axis_index("leaf") * chips + lax.axis_index("chip"))[None]
    upper = [(i, i + 1) for i in range(subtrees - 1)]
    lower = [(i + 1, i) for i in range(subtrees - 1)]

    xt, dt, ids = points.T, direction.T, near_list.T
    x_low = lax.ppermute(xt, AXES, upper)
    w = pack(pos, dt, ids)
    w_low = lax.ppermute(w, AXES, upper)
    terms, spread, list_low, n_own = upward(
        pos, xt, w, ids, leaf_pick, local_pick, leaf_basis, local_basis, subtrees
    )
    gathered = lax.all_to_all(spread, AXES, 0, 0)
    back = near_back(x_low, xt, w_low, w, n_own, count, entries, leaf)
    returned = lax.ppermute(back, AXES, lower)
    out = downward(
        pos, list_low, ridge, gathered, top_pick, x_low, xt, w_low, n_own, top_basis, terms, local_basis, leaf_basis,
        dt, back, entries,
    )
    return (out + returned.astype(f32)).T


def solution(mesh):
    split = P(AXES, None)
    split3 = P(AXES, None, None)
    return jax.shard_map(
        shards,
        mesh=mesh,
        in_specs=(split, split, P(), split3, split3, P(), split, split, P(), split),
        out_specs=split,
        check_vma=False,
    )
```

```python
import functools
import math

import jax
import jax.numpy as jnp
from jax import lax
from jax.experimental import pallas as pl
from jax.experimental.pallas import tpu as pltpu
from jax.sharding import PartitionSpec as P

f32 = jnp.float32
bf16 = jnp.bfloat16
AXES = ("leaf", "chip")
SCALE = math.log2(math.e) / 32.0
FEAT = 128
GROUP = 16
EARLY = 4.5


def dot(a, b, ca=1, cb=0):
    return lax.dot_general(a, b, (((ca,), (cb,)), ((), ())), preferred_element_type=f32)


def copy(src, dst, sem):
    c = pltpu.make_async_copy(src, dst, sem)
    c.start()
    return c


def near_cost(pairs, leaf, cols, data):
    return pl.CostEstimate(
        flops=pairs * 2 * leaf * leaf * (2 * FEAT + leaf), transcendentals=pairs * leaf * leaf, bytes_accessed=data
    )


VM = pl.BlockSpec(memory_space=pltpu.VMEM)
HBM = pl.BlockSpec(memory_space=pltpu.HBM)
ANY = pl.BlockSpec(memory_space=pl.ANY)


def square_rows(xf):
    n = jnp.sum(xf * xf, axis=0, keepdims=True)
    hi = n.astype(bf16).astype(f32)
    rest = n - hi
    mid = rest.astype(bf16).astype(f32)
    low = rest - mid
    row = lax.broadcasted_iota(jnp.int32, (16, xf.shape[1]), 0)
    zero = jnp.zeros((), f32)
    neg = jnp.where(row == 0, -hi, jnp.where(row == 1, -mid, jnp.where(row == 2, -low, zero)))
    ones = jnp.where(row < 3, jnp.ones((), f32), zero)
    return neg.astype(bf16), ones.astype(bf16)


def feature_pair(x):
    dim, width = x.shape
    xf = x.astype(f32)
    neg, ones = square_rows(xf)
    pad = jnp.zeros((FEAT - dim - 32, width), bf16)
    left = jnp.concatenate([(xf + xf).astype(bf16), ones, neg, pad], 0)
    right = jnp.concatenate([x, neg, ones, pad], 0)
    return left, right


def swap_form(left, dim):
    half = (left[:dim].astype(f32) * 0.5).astype(bf16)
    return jnp.concatenate([half, left[dim + 16 : dim + 32], left[dim : dim + 16], left[dim + 32 :]], 0)


def selector(pick_row, width):
    rows = lax.broadcasted_iota(jnp.int32, (width, pick_row.shape[1]), 0)
    return jnp.where(rows == pick_row, jnp.ones((), f32), jnp.zeros((), f32)).astype(bf16)


def gauss(right_rows, left_cols):
    s = dot(right_rows, left_cols)
    return jnp.exp2(s * SCALE).astype(bf16)


def grouped(count, group, compute, store, start=0, also=None, carry=0):
    group = min(group, count)

    def body(t, carry):
        got = [compute(start + t * group + u) for u in range(group)]
        for u in range(group):
            store(start + t * group + u, got[u])
            if also is not None:
                carry = also(start + t * group + u, carry)
        return carry

    if count == group:
        return body(0, carry)
    return lax.fori_loop(0, count // group, body, carry)


def lanes(start, width, number=1):
    if isinstance(start, int):
        return pl.ds(start * width, number * width)
    return pl.ds(pl.multiple_of(start * width, width), number * width)


CHUNKS = 4
PAIRS = 16


def class_list(ids, low, count):
    entries = ids.shape[0]
    local = ids - low
    inside = (local >= 0) & (local < count)
    ones = inside.astype(jnp.int32)
    rank = [jnp.zeros_like(ones[0:1])]
    for e in range(entries):
        rank.append(rank[-1] + ones[e : e + 1])
    row = lax.broadcasted_iota(jnp.int32, (16, ids.shape[1]), 0)
    out = jnp.where(row == entries, rank[-1], 0)
    for e in range(entries):
        here = (row == rank[e]) & (ones[e : e + 1] == 1)
        out = out + jnp.where(here, local[e : e + 1], 0)
    return out


def pack_kernel(pos_ref, d_hbm, ids, out, dt, sems):
    cols, width = dt.shape
    count = ids.shape[1]
    part = width // CHUNKS
    gets = [copy(d_hbm.at[:, pl.ds(c * part, part)], dt.at[:, pl.ds(c * part, part)], sems.at[c]) for c in range(CHUNKS)]
    out[:, pl.ds(width, 128)] = jnp.zeros((cols, 128), bf16)
    out[:, pl.ds(width, count)] = class_list(ids[...], (pos_ref[0] + 1) * count, count).astype(f32).astype(bf16)
    for c in range(CHUNKS):
        gets[c].wait()
        s = pl.ds(c * part, part)
        out[:, s] = dt[:, s].astype(bf16)


def pack(pos, dt, ids):
    cols, width = dt.shape
    return pl.pallas_call(
        pack_kernel,
        grid_spec=pltpu.PrefetchScalarGridSpec(
            num_scalar_prefetch=1,
            grid=(1,),
            in_specs=[HBM, VM],
            out_specs=VM,
            scratch_shapes=[pltpu.VMEM(dt.shape, f32), pltpu.SemaphoreType.DMA((CHUNKS,))],
        ),
        out_shape=jax.ShapeDtypeStruct((cols, width + 128), bf16),
        compiler_params=pltpu.CompilerParams(vmem_limit_bytes=60 << 20),
        name="pack",
    )(pos, dt, ids)


def up_kernel(dims, pos_ref, x_hbm, w_hbm, ids, leaf_pick, local_pick, leaf_hbm, local_hbm,
              terms_hbm, spread, list_low, acc, pair,
              big, at, b, wt, xt, terms, lb, nb, coeff, skel, tiles, lv, lst, xs, ls, ms):
    count, leaf, rank, dim, cols = dims
    entries = ids.shape[0]
    part = count // CHUNKS
    seg = lambda c: pl.ds(c * part * leaf, part * leaf)
    own = lambda c: pl.ds(c * part, part)
    get_x = [copy(x_hbm.at[:, seg(c)], xt.at[:, seg(c)], xs.at[c]) for c in range(CHUNKS)]
    get_w = copy(w_hbm, wt, ms.at[0])
    pos = pos_ref[0]
    table = ids[...]
    put_list = put_class(table, pos * count, count, lv, lst, ms.at[3])
    list_low[...] = class_list(table, (pos - 1) * count, count)
    acc[...] = jnp.zeros_like(acc)

    def prepare(l):
        left, right = feature_pair(xt[:, lanes(l, leaf)])
        return left, right.T

    def keep(l, got):
        at[l], b[l] = got

    total = 0
    for c in range(CHUNKS):
        get_x[c].wait()
        if c == 0:
            put_list.wait()
        if c == 1:
            get_leaf = [copy(leaf_hbm.at[own(k)], lb.at[own(k)], ls.at[k]) for k in range(CHUNKS)]
            get_local = copy(local_hbm, nb, ms.at[1])
        total = grouped(part, 16, prepare, keep, c * part, scan_leaf(count, entries, lst, pair), total)
    end_list(count, pair, total)
    get_w.wait()
    base = count - 1

    def leaf_step(l):
        c = dot(wt[:, lanes(l, leaf)], lb[l])
        sel = selector(leaf_pick[pl.ds(l, 1), :], leaf)
        return c.astype(bf16), dot(at[l], sel).astype(bf16)

    def leaf_keep(l, got):
        coeff[:, lanes(base + l, rank)], skel[:, lanes(base + l, rank)] = got

    for c in range(CHUNKS):
        get_leaf[c].wait()
        grouped(part, 16, leaf_step, leaf_keep, c * part)
    get_local.wait()
    depth = count.bit_length() - 1
    for d in range(depth, 0, -1):
        up = 2 ** (d - 1) - 1

        def climb(j):
            both = lanes(2 * j + 1, rank, 2)
            sel = selector(local_pick[pl.ds(j, 1), :], 2 * rank)
            return dot(coeff[:, both], nb[j]).astype(bf16), dot(skel[:, both], sel).astype(bf16)

        def climb_keep(j, got):
            coeff[:, lanes(j, rank)], skel[:, lanes(j, rank)] = got

        grouped(2 ** (d - 1), 32, climb, climb_keep, up)
    root_c, root_s = coeff[:, :rank], skel[:dim, :rank]
    for s in range(spread.shape[0]):
        spread[s, :cols, :] = root_c
        spread[s, cols:, :] = root_s

    last = count - 2

    def index(j):
        return min(j, last) if isinstance(j, int) else jnp.minimum(j, last)

    def first(j, slot):
        both = skel[:, lanes(2 * index(j) + 1, rank, 2)]
        tiles[slot] = gauss(swap_form(both[:, rank:], dim).T, both[:, :rank])

    def second(j, slot):
        c2 = coeff[:, lanes(2 * index(j) + 1, rank, 2)]
        g = tiles[slot]
        return jnp.concatenate([dot(c2[:, rank:], g), dot(c2[:, :rank], g, 1, 1)], 1)

    for u in range(PAIRS):
        first(u, u)

    def body(t, carry):
        for phase in range(2):
            k = (2 * t + phase) * PAIRS
            got = []
            for u in range(PAIRS):
                first(k + PAIRS + u, (1 - phase) * PAIRS + u)
                got.append(second(k + u, phase * PAIRS + u))
            for u in range(PAIRS):
                terms[:, lanes(2 * index(k + u), rank, 2)] = got[u]
        return carry

    lax.fori_loop(0, count // (2 * PAIRS), body, 0)
    put_terms = copy(terms, terms_hbm, ms.at[2])
    pair[pair.shape[0] - 1] = total
    near_pairs(count, jnp.minimum(total, early_pairs(count)), pair, at, b, wt, acc, big)
    put_terms.wait()


def put_class(table, low, count, lv, lst, sem):
    lv[...] = jnp.zeros_like(lv)
    lv[:, :count] = class_list(table, low, count)
    return copy(lv, lst, sem)


def upward(pos, xt, w, ids, leaf_pick, local_pick, leaf_basis, local_basis, subtrees):
    count, leaf, rank = leaf_basis.shape
    dim, cols = xt.shape[0], w.shape[0]
    entries = ids.shape[0]
    return pl.pallas_call(
        functools.partial(up_kernel, (count, leaf, rank, dim, cols)),
        grid_spec=pltpu.PrefetchScalarGridSpec(
            num_scalar_prefetch=1,
            grid=(1,),
            in_specs=[HBM, HBM, VM, VM, VM, HBM, HBM],
            out_specs=[HBM, VM, VM, VM, pl.BlockSpec(memory_space=pltpu.SMEM)],
            scratch_shapes=near_scratch(count, entries, leaf, dim, cols)[1:]
            + [
                pltpu.VMEM((cols, (2 * count - 2) * rank), f32),
                pltpu.VMEM(leaf_basis.shape, bf16),
                pltpu.VMEM(local_basis.shape, bf16),
                pltpu.VMEM((cols, (2 * count - 1) * rank), bf16),
                pltpu.VMEM((FEAT, (2 * count - 1) * rank), bf16),
                pltpu.VMEM((2 * PAIRS, rank, rank), bf16),
                pltpu.VMEM((16, 128), jnp.int32),
                pltpu.SMEM((16, 128), jnp.int32),
                pltpu.SemaphoreType.DMA((CHUNKS,)),
                pltpu.SemaphoreType.DMA((CHUNKS,)),
                pltpu.SemaphoreType.DMA((4,)),
            ],
        ),
        out_shape=[
            jax.ShapeDtypeStruct((cols, (2 * count - 2) * rank), f32),
            jax.ShapeDtypeStruct((subtrees, cols + dim, rank), bf16),
            jax.ShapeDtypeStruct((16, count), jnp.int32),
            jax.ShapeDtypeStruct((count + 1, cols, leaf), f32),
            jax.ShapeDtypeStruct((pair_slots(count, entries) + 1,), jnp.int32),
        ],
        compiler_params=pltpu.CompilerParams(vmem_limit_bytes=60 << 20),
        cost_estimate=near_cost(12 * count, leaf, cols, 16 << 20),
        name="upward",
    )(pos, xt, w, ids, leaf_pick, local_pick, leaf_basis, local_basis)


def scan_leaf(count, entries, lst, pair):
    def scan(i, pos):
        for e in range(entries):
            pair[pos + e] = i * count + lst[e, i]
        return pos + lst[entries, i]

    return scan


def end_list(count, pair, total):
    for u in range(3 * GROUP):
        pair[total + u] = count * count


def early_pairs(count):
    return int(EARLY * count) // (2 * GROUP) * 2 * GROUP


def near_pairs(count, total, pair, at, b, w, acc, tiles, begin=0):
    h = GROUP
    leaf = b.shape[1]
    shift = count.bit_length() - 1

    def first(k, slot):
        code = pair[begin + k]
        tiles[slot] = gauss(b[code & (count - 1)], at[(code >> shift) & (count - 1)])

    def second(k, slot):
        code = pair[begin + k]
        return code >> shift, dot(w[:, lanes(code & (count - 1), leaf)], tiles[slot])

    for u in range(h):
        first(u, u)

    def body(t, carry):
        for phase in range(2):
            k = (2 * t + phase) * h
            got = []
            for u in range(h):
                first(k + h + u, (1 - phase) * h + u)
                got.append(second(k + u, phase * h + u))
            for i, o in got:
                acc[i] += o
        return carry

    blocks = (total - begin + h - 1) // h
    lax.fori_loop(0, (blocks + 1) // 2, body, 0)


def pair_slots(count, entries):
    return count * entries + entries + 4 * GROUP


def near_scratch(count, entries, leaf, dim, cols):
    return [
        pltpu.SMEM((pair_slots(count, entries),), jnp.int32),
        pltpu.VMEM((2 * GROUP, leaf, leaf), bf16),
        pltpu.VMEM((count, FEAT, leaf), bf16),
        pltpu.VMEM((count, leaf, FEAT), bf16),
        pltpu.VMEM((cols, count * leaf + 128), bf16),
        pltpu.VMEM((dim, count * leaf), bf16),
    ]


def two_sided(count, leaf, target_hbm, source_hbm, x, y, at, b, xs):
    part = count // CHUNKS
    seg = lambda c: pl.ds(c * part * leaf, part * leaf)
    gets = []
    for c in range(CHUNKS):
        gets.append(copy(source_hbm.at[:, seg(c)], y.at[:, seg(c)], xs.at[1, c]))
        gets.append(copy(target_hbm.at[:, seg(c)], x.at[:, seg(c)], xs.at[0, c]))

    def finish(also):
        def prepare(l):
            return feature_pair(x[:, lanes(l, leaf)])[0], feature_pair(y[:, lanes(l, leaf)])[1].T

        def keep(l, got):
            at[l], b[l] = got

        total = 0
        for c in range(CHUNKS):
            gets[2 * c].wait()
            gets[2 * c + 1].wait()
            total = grouped(part, 16, prepare, keep, c * part, also, total)
        return total

    return finish


def near_back_kernel(entries, left_over, low_hbm, x_hbm, wlow_hbm, w_hbm, own_hbm, out, own,
                     pair, tiles, at, b, w, x, y, acc, lf, lv, lst, xs, sems):
    count, _, leaf = at.shape
    get_list = copy(wlow_hbm.at[:, pl.ds(count * leaf, 128)], lf, sems.at[0])
    finish = two_sided(count, leaf, low_hbm, x_hbm, x, y, at, b, xs)
    get_w = copy(w_hbm, w, sems.at[1])
    get_own = copy(own_hbm, own, sems.at[3])
    get_list.wait()
    lv[...] = lf[...].astype(f32).astype(jnp.int32)
    put_list = copy(lv, lst, sems.at[2])
    acc[...] = jnp.zeros_like(acc)
    put_list.wait()
    total = finish(scan_leaf(count, entries, lst, pair))
    end_list(count, pair, total)
    get_w.wait()
    near_pairs(count, total, pair, at, b, w, acc, tiles)

    def store(l, got):
        out[:, lanes(l, leaf)] = got.astype(out.dtype)

    grouped(count, 8, lambda l: acc[l], store)
    get_own.wait()
    all_own = left_over[left_over.shape[0] - 1]

    @pl.when(all_own > early_pairs(count))
    def _():
        def keep(l, got):
            at[l] = got

        grouped(count, 16, lambda l: feature_pair(y[:, lanes(l, leaf)])[0], keep)
        near_pairs(count, all_own, left_over, at, b, w, own, tiles, early_pairs(count))


def near_back(left_over, x_low, x, w_low, w, n_own, count, entries, leaf):
    dim, cols = x.shape[0], w.shape[0]
    return pl.pallas_call(
        functools.partial(near_back_kernel, entries),
        grid_spec=pltpu.PrefetchScalarGridSpec(
            num_scalar_prefetch=1,
            grid=(1,),
            in_specs=[ANY, HBM, ANY, HBM, HBM],
            out_specs=[VM, VM],
            scratch_shapes=near_scratch(count, entries, leaf, dim, cols)
            + [
                pltpu.VMEM((dim, count * leaf), bf16),
                pltpu.VMEM((count + 1, cols, leaf), f32),
                pltpu.VMEM((cols, 128), bf16),
                pltpu.VMEM((cols, 128), jnp.int32),
                pltpu.SMEM((cols, 128), jnp.int32),
                pltpu.SemaphoreType.DMA((2, CHUNKS)),
                pltpu.SemaphoreType.DMA((4,)),
            ],
        ),
        out_shape=[
            jax.ShapeDtypeStruct((cols, count * leaf), bf16),
            jax.ShapeDtypeStruct((count + 1, cols, leaf), f32),
        ],
        compiler_params=pltpu.CompilerParams(vmem_limit_bytes=52 << 20),
        cost_estimate=near_cost(4 * count, leaf, cols, 6 << 20),
        name="near_back",
    )(left_over, x_low, x, w_low, w, n_own)


def down_kernel(dims, pos_ref, lst, ridge, gathered, top_pick, low_hbm, x_hbm, wlow_hbm, own_hbm,
                top_hbm, terms_hbm, local_hbm, leaf_hbm, d_hbm, after, out,
                pair, tiles, at, b, w, x, y, acc, tb, terms, nb, lb, dt, tcoeff, tskel, value, xs, sems):
    count, leaf, rank, dim, cols, subtrees, entries = dims
    finish_features = two_sided(count, leaf, x_hbm, low_hbm, x, y, at, b, xs)
    get_w = copy(wlow_hbm, w, sems.at[0])
    get_acc = copy(own_hbm, acc, sems.at[1])
    pairs = ((top_hbm, tb), (terms_hbm, terms), (local_hbm, nb), (leaf_hbm, lb), (d_hbm, dt))
    total = finish_features(scan_leaf(count, entries, lst, pair))
    end_list(count, pair, total)
    gets = [copy(src, dst, sems.at[k + 2]) for k, (src, dst) in enumerate(pairs)]
    get_w.wait()
    get_acc.wait()
    near_pairs(count, total, pair, at, b, w, acc, tiles)

    pos = pos_ref[0]
    depth = subtrees.bit_length() - 1
    for s in range(subtrees):
        tcoeff[:, lanes(subtrees - 1 + s, rank)] = gathered[s, :cols]
        tskel[:, lanes(subtrees - 1 + s, rank)] = gathered[s, cols:]
    for g in gets:
        g.wait()
    for d in range(depth - 1, 0, -1):

        def climb(j):
            both = lanes(2 * j + 1, rank, 2)
            sel = selector(top_pick[pl.ds(j, 1), :], 2 * rank)
            return dot(tcoeff[:, both], tb[j]).astype(bf16), dot(tskel[:, both], sel).astype(bf16)

        def climb_keep(j, got):
            tcoeff[:, lanes(j, rank)], tskel[:, lanes(j, rank)] = got

        grouped(2**d, 16, climb, climb_keep, 2**d - 1)

    def half(v):
        return (v.astype(f32) * 0.5).astype(bf16)

    top_terms = {}
    for d in range(depth, 0, -1):
        mine = pos >> (depth - d)
        other = mine ^ 1
        own_left = feature_pair(half(tskel[:, lanes(2**d - 1 + mine, rank)]))[0]
        sib_right = feature_pair(half(tskel[:, lanes(2**d - 1 + other, rank)]))[1]
        g = gauss(sib_right.T, own_left)
        top_terms[d] = dot(tcoeff[:, lanes(2**d - 1 + other, rank)], g)
    v = jnp.zeros((cols, rank), bf16)
    for d in range(1, depth + 1):
        parent = pos >> (depth - d + 1)
        down = dot(v, tb[2 ** (d - 1) - 1 + parent], 1, 1)
        right = ((pos >> (depth - d)) & 1) == 1
        v = (top_terms[d] + jnp.where(right, down[:, rank:], down[:, :rank])).astype(bf16)
    value[:, lanes(0, rank)] = v
    local_depth = count.bit_length() - 1
    for d in range(1, local_depth + 1):

        def descend(j):
            down = dot(value[:, lanes(j, rank)], nb[j], 1, 1)
            return (terms[:, lanes(2 * j, rank, 2)] + down).astype(bf16)

        def descend_keep(j, got):
            value[:, lanes(2 * j + 1, rank, 2)] = got

        grouped(2 ** (d - 1), 32, descend, descend_keep, 2 ** (d - 1) - 1)
    row = lax.broadcasted_iota(jnp.int32, (cols, leaf), 0)
    scale = jnp.zeros((cols, leaf), f32)
    for r in range(cols):
        scale = jnp.where(row == r, ridge[r], scale)

    def finish(l):
        far = dot(value[:, lanes(count - 1 + l, rank)], lb[l], 1, 1)
        return scale * dt[:, lanes(l, leaf)] + far + acc[l]

    def finish_keep(l, got):
        out[:, lanes(l, leaf)] = got

    grouped(count, 16, finish, finish_keep)


def downward(pos, lst, ridge, gathered, top_pick, x_low, x, w_low, n_own, top_basis, terms, local_basis, leaf_basis,
             dt, after, entries):
    count, leaf, rank = leaf_basis.shape
    dim, cols = x.shape[0], dt.shape[0]
    subtrees = gathered.shape[0]
    big = (top_basis, terms, local_basis, leaf_basis, dt)
    return pl.pallas_call(
        functools.partial(down_kernel, (count, leaf, rank, dim, cols, subtrees, entries)),
        grid_spec=pltpu.PrefetchScalarGridSpec(
            num_scalar_prefetch=3,
            grid=(1,),
            in_specs=[VM] * 2 + [ANY, HBM, ANY] + [HBM] * 7,
            out_specs=VM,
            scratch_shapes=near_scratch(count, entries, leaf, dim, cols)
            + [pltpu.VMEM((dim, count * leaf), bf16), pltpu.VMEM((count + 1, cols, leaf), f32)]
            + [pltpu.VMEM(a.shape, a.dtype) for a in big]
            + [
                pltpu.VMEM((cols, (2 * subtrees - 1) * rank), bf16),
                pltpu.VMEM((dim, (2 * subtrees - 1) * rank), bf16),
                pltpu.VMEM((cols, (2 * count - 1) * rank), bf16),
                pltpu.SemaphoreType.DMA((2, CHUNKS)),
                pltpu.SemaphoreType.DMA((7,)),
            ],
        ),
        out_shape=jax.ShapeDtypeStruct(dt.shape, f32),
        compiler_params=pltpu.CompilerParams(vmem_limit_bytes=52 << 20),
        cost_estimate=near_cost(8 * count, leaf, cols, 20 << 20),
        name="downward",
    )(pos, lst, ridge, gathered, top_pick, x_low, x, w_low, n_own, *big, after)


def shards(points, direction, ridge, leaf_basis, local_basis, top_basis, leaf_pick, local_pick, top_pick, near_list):
    count, leaf, rank = leaf_basis.shape
    entries = near_list.shape[1]
    chips = lax.axis_size("chip")
    subtrees = lax.axis_size("leaf") * chips
    pos = (lax.axis_index("leaf") * chips + lax.axis_index("chip"))[None]
    upper = [(i, i + 1) for i in range(subtrees - 1)]
    lower = [(i + 1, i) for i in range(subtrees - 1)]

    xt, dt, ids = points.T, direction.T, near_list.T
    x_low = lax.ppermute(xt, AXES, upper)
    w = pack(pos, dt, ids)
    w_low = lax.ppermute(w, AXES, upper)
    terms, spread, list_low, n_own, own_list = upward(
        pos, xt, w, ids, leaf_pick, local_pick, leaf_basis, local_basis, subtrees
    )
    gathered = lax.all_to_all(spread, AXES, 0, 0)
    back, n_own = near_back(own_list, x_low, xt, w_low, w, n_own, count, entries, leaf)
    returned = lax.ppermute(back, AXES, lower)
    out = downward(
        pos, list_low, ridge, gathered, top_pick, x_low, xt, w_low, n_own, top_basis, terms, local_basis, leaf_basis,
        dt, back, entries,
    )
    return (out + returned.astype(f32)).T


def solution(mesh):
    split = P(AXES, None)
    split3 = P(AXES, None, None)
    return jax.shard_map(
        shards,
        mesh=mesh,
        in_specs=(split, split, P(), split3, split3, P(), split, split, P(), split),
        out_specs=split,
        check_vma=False,
    )
```

```python
import functools
import math

import jax
import jax.numpy as jnp
from jax import lax
from jax.experimental import pallas as pl
from jax.experimental.pallas import tpu as pltpu
from jax.sharding import PartitionSpec as P

f32 = jnp.float32
bf16 = jnp.bfloat16
AXES = ("leaf", "chip")
SCALE = math.log2(math.e) / 32.0
FEAT = 128
GROUP = 16
EARLY = 5.5


def dot(a, b, ca=1, cb=0):
    return lax.dot_general(a, b, (((ca,), (cb,)), ((), ())), preferred_element_type=f32)


def copy(src, dst, sem):
    c = pltpu.make_async_copy(src, dst, sem)
    c.start()
    return c


def near_cost(pairs, leaf, cols, data):
    return pl.CostEstimate(
        flops=pairs * 2 * leaf * leaf * (2 * FEAT + leaf), transcendentals=pairs * leaf * leaf, bytes_accessed=data
    )


VM = pl.BlockSpec(memory_space=pltpu.VMEM)
HBM = pl.BlockSpec(memory_space=pltpu.HBM)
ANY = pl.BlockSpec(memory_space=pl.ANY)


def square_rows(xf):
    n = jnp.sum(xf * xf, axis=0, keepdims=True)
    hi = n.astype(bf16).astype(f32)
    rest = n - hi
    mid = rest.astype(bf16).astype(f32)
    low = rest - mid
    row = lax.broadcasted_iota(jnp.int32, (16, xf.shape[1]), 0)
    zero = jnp.zeros((), f32)
    neg = jnp.where(row == 0, -hi, jnp.where(row == 1, -mid, jnp.where(row == 2, -low, zero)))
    ones = jnp.where(row < 3, jnp.ones((), f32), zero)
    return neg.astype(bf16), ones.astype(bf16)


def feature_pair(x):
    dim, width = x.shape
    xf = x.astype(f32)
    neg, ones = square_rows(xf)
    pad = jnp.zeros((FEAT - dim - 32, width), bf16)
    left = jnp.concatenate([(xf + xf).astype(bf16), ones, neg, pad], 0)
    right = jnp.concatenate([x, neg, ones, pad], 0)
    return left, right


def swap_form(left, dim):
    half = (left[:dim].astype(f32) * 0.5).astype(bf16)
    return jnp.concatenate([half, left[dim + 16 : dim + 32], left[dim : dim + 16], left[dim + 32 :]], 0)


def selector(pick_row, width):
    rows = lax.broadcasted_iota(jnp.int32, (width, pick_row.shape[1]), 0)
    return jnp.where(rows == pick_row, jnp.ones((), f32), jnp.zeros((), f32)).astype(bf16)


def gauss(right_rows, left_cols):
    s = dot(right_rows, left_cols)
    return jnp.exp2(s * SCALE).astype(bf16)


def grouped(count, group, compute, store, start=0, also=None, carry=0):
    group = min(group, count)

    def body(t, carry):
        got = [compute(start + t * group + u) for u in range(group)]
        for u in range(group):
            store(start + t * group + u, got[u])
            if also is not None:
                carry = also(start + t * group + u, carry)
        return carry

    if count == group:
        return body(0, carry)
    return lax.fori_loop(0, count // group, body, carry)


def lanes(start, width, number=1):
    if isinstance(start, int):
        return pl.ds(start * width, number * width)
    return pl.ds(pl.multiple_of(start * width, width), number * width)


CHUNKS = 4
PAIRS = 16


def class_list(ids, low, count):
    entries = ids.shape[0]
    local = ids - low
    inside = (local >= 0) & (local < count)
    ones = inside.astype(jnp.int32)
    rank = [jnp.zeros_like(ones[0:1])]
    for e in range(entries):
        rank.append(rank[-1] + ones[e : e + 1])
    row = lax.broadcasted_iota(jnp.int32, (16, ids.shape[1]), 0)
    out = jnp.where(row == entries, rank[-1], 0)
    for e in range(entries):
        here = (row == rank[e]) & (ones[e : e + 1] == 1)
        out = out + jnp.where(here, local[e : e + 1], 0)
    return out


def pack_kernel(pos_ref, d_hbm, ids, out, dt, sems):
    cols, width = dt.shape
    count = ids.shape[1]
    part = width // CHUNKS
    gets = [copy(d_hbm.at[:, pl.ds(c * part, part)], dt.at[:, pl.ds(c * part, part)], sems.at[c]) for c in range(CHUNKS)]
    out[:, pl.ds(width, 128)] = jnp.zeros((cols, 128), bf16)
    out[:, pl.ds(width, count)] = class_list(ids[...], (pos_ref[0] + 1) * count, count).astype(f32).astype(bf16)
    for c in range(CHUNKS):
        gets[c].wait()
        s = pl.ds(c * part, part)
        out[:, s] = dt[:, s].astype(bf16)


def pack(pos, dt, ids):
    cols, width = dt.shape
    return pl.pallas_call(
        pack_kernel,
        grid_spec=pltpu.PrefetchScalarGridSpec(
            num_scalar_prefetch=1,
            grid=(1,),
            in_specs=[HBM, VM],
            out_specs=VM,
            scratch_shapes=[pltpu.VMEM(dt.shape, f32), pltpu.SemaphoreType.DMA((CHUNKS,))],
        ),
        out_shape=jax.ShapeDtypeStruct((cols, width + 128), bf16),
        compiler_params=pltpu.CompilerParams(vmem_limit_bytes=60 << 20),
        name="pack",
    )(pos, dt, ids)


def up_kernel(dims, pos_ref, x_hbm, w_hbm, ids, leaf_pick, local_pick, leaf_hbm, local_hbm,
              terms_hbm, spread, list_low, acc, pair,
              big, at, b, wt, xt, terms, lb, nb, coeff, skel, tiles, lv, lst, xs, ls, ms):
    count, leaf, rank, dim, cols = dims
    entries = ids.shape[0]
    part = count // CHUNKS
    seg = lambda c: pl.ds(c * part * leaf, part * leaf)
    own = lambda c: pl.ds(c * part, part)
    get_x = [copy(x_hbm.at[:, seg(c)], xt.at[:, seg(c)], xs.at[c]) for c in range(CHUNKS)]
    get_w = copy(w_hbm, wt, ms.at[0])
    pos = pos_ref[0]
    table = ids[...]
    put_list = put_class(table, pos * count, count, lv, lst, ms.at[3])
    list_low[...] = class_list(table, (pos - 1) * count, count)
    acc[...] = jnp.zeros_like(acc)

    def prepare(l):
        left, right = feature_pair(xt[:, lanes(l, leaf)])
        return left, right.T

    def keep(l, got):
        at[l], b[l] = got

    total = 0
    for c in range(CHUNKS):
        get_x[c].wait()
        if c == 0:
            put_list.wait()
        if c == 1:
            get_leaf = [copy(leaf_hbm.at[own(k)], lb.at[own(k)], ls.at[k]) for k in range(CHUNKS)]
            get_local = copy(local_hbm, nb, ms.at[1])
        total = grouped(part, 16, prepare, keep, c * part, scan_leaf(count, entries, lst, pair), total)
    end_list(count, pair, total)
    get_w.wait()
    base = count - 1

    def leaf_step(l):
        c = dot(wt[:, lanes(l, leaf)], lb[l])
        sel = selector(leaf_pick[pl.ds(l, 1), :], leaf)
        return c.astype(bf16), dot(at[l], sel).astype(bf16)

    def leaf_keep(l, got):
        coeff[:, lanes(base + l, rank)], skel[:, lanes(base + l, rank)] = got

    for c in range(CHUNKS):
        get_leaf[c].wait()
        grouped(part, 16, leaf_step, leaf_keep, c * part)
    get_local.wait()
    depth = count.bit_length() - 1
    for d in range(depth, 0, -1):
        up = 2 ** (d - 1) - 1

        def climb(j):
            both = lanes(2 * j + 1, rank, 2)
            sel = selector(local_pick[pl.ds(j, 1), :], 2 * rank)
            return dot(coeff[:, both], nb[j]).astype(bf16), dot(skel[:, both], sel).astype(bf16)

        def climb_keep(j, got):
            coeff[:, lanes(j, rank)], skel[:, lanes(j, rank)] = got

        grouped(2 ** (d - 1), 32, climb, climb_keep, up)
    root_c, root_s = coeff[:, :rank], skel[:dim, :rank]
    for s in range(spread.shape[0]):
        spread[s, :cols, :] = root_c
        spread[s, cols:, :] = root_s

    last = count - 2

    def index(j):
        return min(j, last) if isinstance(j, int) else jnp.minimum(j, last)

    def first(j, slot):
        both = skel[:, lanes(2 * index(j) + 1, rank, 2)]
        tiles[slot] = gauss(swap_form(both[:, rank:], dim).T, both[:, :rank])

    def second(j, slot):
        c2 = coeff[:, lanes(2 * index(j) + 1, rank, 2)]
        g = tiles[slot]
        return jnp.concatenate([dot(c2[:, rank:], g), dot(c2[:, :rank], g, 1, 1)], 1)

    for u in range(PAIRS):
        first(u, u)

    def body(t, carry):
        for phase in range(2):
            k = (2 * t + phase) * PAIRS
            got = []
            for u in range(PAIRS):
                first(k + PAIRS + u, (1 - phase) * PAIRS + u)
                got.append(second(k + u, phase * PAIRS + u))
            for u in range(PAIRS):
                terms[:, lanes(2 * index(k + u), rank, 2)] = got[u]
        return carry

    lax.fori_loop(0, count // (2 * PAIRS), body, 0)
    put_terms = copy(terms, terms_hbm, ms.at[2])
    pair[pair.shape[0] - 1] = total
    near_pairs(count, jnp.minimum(total, early_pairs(count)), pair, at, b, wt, acc, big)
    put_terms.wait()


def put_class(table, low, count, lv, lst, sem):
    lv[...] = jnp.zeros_like(lv)
    lv[:, :count] = class_list(table, low, count)
    return copy(lv, lst, sem)


def upward(pos, xt, w, ids, leaf_pick, local_pick, leaf_basis, local_basis, subtrees):
    count, leaf, rank = leaf_basis.shape
    dim, cols = xt.shape[0], w.shape[0]
    entries = ids.shape[0]
    return pl.pallas_call(
        functools.partial(up_kernel, (count, leaf, rank, dim, cols)),
        grid_spec=pltpu.PrefetchScalarGridSpec(
            num_scalar_prefetch=1,
            grid=(1,),
            in_specs=[HBM, HBM, VM, VM, VM, HBM, HBM],
            out_specs=[HBM, VM, VM, VM, pl.BlockSpec(memory_space=pltpu.SMEM)],
            scratch_shapes=near_scratch(count, entries, leaf, dim, cols)[1:]
            + [
                pltpu.VMEM((cols, (2 * count - 2) * rank), f32),
                pltpu.VMEM(leaf_basis.shape, bf16),
                pltpu.VMEM(local_basis.shape, bf16),
                pltpu.VMEM((cols, (2 * count - 1) * rank), bf16),
                pltpu.VMEM((FEAT, (2 * count - 1) * rank), bf16),
                pltpu.VMEM((2 * PAIRS, rank, rank), bf16),
                pltpu.VMEM((16, 128), jnp.int32),
                pltpu.SMEM((16, 128), jnp.int32),
                pltpu.SemaphoreType.DMA((CHUNKS,)),
                pltpu.SemaphoreType.DMA((CHUNKS,)),
                pltpu.SemaphoreType.DMA((4,)),
            ],
        ),
        out_shape=[
            jax.ShapeDtypeStruct((cols, (2 * count - 2) * rank), f32),
            jax.ShapeDtypeStruct((subtrees, cols + dim, rank), bf16),
            jax.ShapeDtypeStruct((16, count), jnp.int32),
            jax.ShapeDtypeStruct((count + 1, cols, leaf), f32),
            jax.ShapeDtypeStruct((pair_slots(count, entries) + 1,), jnp.int32),
        ],
        compiler_params=pltpu.CompilerParams(vmem_limit_bytes=60 << 20),
        cost_estimate=near_cost(12 * count, leaf, cols, 16 << 20),
        name="upward",
    )(pos, xt, w, ids, leaf_pick, local_pick, leaf_basis, local_basis)


def scan_leaf(count, entries, lst, pair):
    def scan(i, pos):
        for e in range(entries):
            pair[pos + e] = i * count + lst[e, i]
        return pos + lst[entries, i]

    return scan


def end_list(count, pair, total):
    for u in range(3 * GROUP):
        pair[total + u] = count * count


def early_pairs(count):
    return int(EARLY * count) // (2 * GROUP) * 2 * GROUP


def near_pairs(count, total, pair, at, b, w, acc, tiles, begin=0):
    h = GROUP
    leaf = b.shape[1]
    shift = count.bit_length() - 1

    def first(k, slot):
        code = pair[begin + k]
        tiles[slot] = gauss(b[code & (count - 1)], at[(code >> shift) & (count - 1)])

    def second(k, slot):
        code = pair[begin + k]
        return code >> shift, dot(w[:, lanes(code & (count - 1), leaf)], tiles[slot])

    for u in range(h):
        first(u, u)

    def body(t, carry):
        for phase in range(2):
            k = (2 * t + phase) * h
            got = []
            for u in range(h):
                first(k + h + u, (1 - phase) * h + u)
                got.append(second(k + u, phase * h + u))
            for i, o in got:
                acc[i] += o
        return carry

    blocks = (total - begin + h - 1) // h
    lax.fori_loop(0, (blocks + 1) // 2, body, 0)


def pair_slots(count, entries):
    return count * entries + entries + 4 * GROUP


def near_scratch(count, entries, leaf, dim, cols):
    return [
        pltpu.SMEM((pair_slots(count, entries),), jnp.int32),
        pltpu.VMEM((2 * GROUP, leaf, leaf), bf16),
        pltpu.VMEM((count, FEAT, leaf), bf16),
        pltpu.VMEM((count, leaf, FEAT), bf16),
        pltpu.VMEM((cols, count * leaf + 128), bf16),
        pltpu.VMEM((dim, count * leaf), bf16),
    ]


def two_sided(count, leaf, target_hbm, source_hbm, x, y, at, b, xs):
    part = count // CHUNKS
    seg = lambda c: pl.ds(c * part * leaf, part * leaf)
    gets = []
    for c in range(CHUNKS):
        gets.append(copy(source_hbm.at[:, seg(c)], y.at[:, seg(c)], xs.at[1, c]))
        gets.append(copy(target_hbm.at[:, seg(c)], x.at[:, seg(c)], xs.at[0, c]))

    def finish(also):
        def prepare(l):
            return feature_pair(x[:, lanes(l, leaf)])[0], feature_pair(y[:, lanes(l, leaf)])[1].T

        def keep(l, got):
            at[l], b[l] = got

        total = 0
        for c in range(CHUNKS):
            gets[2 * c].wait()
            gets[2 * c + 1].wait()
            total = grouped(part, 16, prepare, keep, c * part, also, total)
        return total

    return finish


def near_back_kernel(entries, left_over, low_hbm, x_hbm, wlow_hbm, w_hbm, own_hbm, out, own,
                     pair, tiles, at, b, w, x, y, acc, lf, lv, lst, xs, sems):
    count, _, leaf = at.shape
    get_list = copy(wlow_hbm.at[:, pl.ds(count * leaf, 128)], lf, sems.at[0])
    finish = two_sided(count, leaf, low_hbm, x_hbm, x, y, at, b, xs)
    get_w = copy(w_hbm, w, sems.at[1])
    get_own = copy(own_hbm, own, sems.at[3])
    get_list.wait()
    lv[...] = lf[...].astype(f32).astype(jnp.int32)
    put_list = copy(lv, lst, sems.at[2])
    acc[...] = jnp.zeros_like(acc)
    put_list.wait()
    total = finish(scan_leaf(count, entries, lst, pair))
    end_list(count, pair, total)
    get_w.wait()
    near_pairs(count, total, pair, at, b, w, acc, tiles)

    def store(l, got):
        out[:, lanes(l, leaf)] = got.astype(out.dtype)

    grouped(count, 8, lambda l: acc[l], store)
    get_own.wait()
    all_own = left_over[left_over.shape[0] - 1]

    @pl.when(all_own > early_pairs(count))
    def _():
        def keep(l, got):
            at[l] = got

        grouped(count, 16, lambda l: feature_pair(y[:, lanes(l, leaf)])[0], keep)
        near_pairs(count, all_own, left_over, at, b, w, own, tiles, early_pairs(count))


def near_back(left_over, x_low, x, w_low, w, n_own, count, entries, leaf):
    dim, cols = x.shape[0], w.shape[0]
    return pl.pallas_call(
        functools.partial(near_back_kernel, entries),
        grid_spec=pltpu.PrefetchScalarGridSpec(
            num_scalar_prefetch=1,
            grid=(1,),
            in_specs=[ANY, HBM, ANY, HBM, HBM],
            out_specs=[VM, VM],
            scratch_shapes=near_scratch(count, entries, leaf, dim, cols)
            + [
                pltpu.VMEM((dim, count * leaf), bf16),
                pltpu.VMEM((count + 1, cols, leaf), f32),
                pltpu.VMEM((cols, 128), bf16),
                pltpu.VMEM((cols, 128), jnp.int32),
                pltpu.SMEM((cols, 128), jnp.int32),
                pltpu.SemaphoreType.DMA((2, CHUNKS)),
                pltpu.SemaphoreType.DMA((4,)),
            ],
        ),
        out_shape=[
            jax.ShapeDtypeStruct((cols, count * leaf), bf16),
            jax.ShapeDtypeStruct((count + 1, cols, leaf), f32),
        ],
        compiler_params=pltpu.CompilerParams(vmem_limit_bytes=52 << 20),
        cost_estimate=near_cost(4 * count, leaf, cols, 6 << 20),
        name="near_back",
    )(left_over, x_low, x, w_low, w, n_own)


def down_kernel(dims, pos_ref, lst, ridge, gathered, top_pick, low_hbm, x_hbm, wlow_hbm, own_hbm,
                top_hbm, terms_hbm, local_hbm, leaf_hbm, d_hbm, after, out,
                pair, tiles, at, b, w, x, y, acc, tb, terms, nb, lb, dt, tcoeff, tskel, value, xs, sems):
    count, leaf, rank, dim, cols, subtrees, entries = dims
    finish_features = two_sided(count, leaf, x_hbm, low_hbm, x, y, at, b, xs)
    get_w = copy(wlow_hbm, w, sems.at[0])
    get_acc = copy(own_hbm, acc, sems.at[1])
    pairs = ((top_hbm, tb), (terms_hbm, terms), (local_hbm, nb), (leaf_hbm, lb), (d_hbm, dt))
    total = finish_features(scan_leaf(count, entries, lst, pair))
    end_list(count, pair, total)
    gets = [copy(src, dst, sems.at[k + 2]) for k, (src, dst) in enumerate(pairs)]
    get_w.wait()
    get_acc.wait()
    near_pairs(count, total, pair, at, b, w, acc, tiles)

    pos = pos_ref[0]
    depth = subtrees.bit_length() - 1
    for s in range(subtrees):
        tcoeff[:, lanes(subtrees - 1 + s, rank)] = gathered[s, :cols]
        tskel[:, lanes(subtrees - 1 + s, rank)] = gathered[s, cols:]
    for g in gets:
        g.wait()
    for d in range(depth - 1, 0, -1):

        def climb(j):
            both = lanes(2 * j + 1, rank, 2)
            sel = selector(top_pick[pl.ds(j, 1), :], 2 * rank)
            return dot(tcoeff[:, both], tb[j]).astype(bf16), dot(tskel[:, both], sel).astype(bf16)

        def climb_keep(j, got):
            tcoeff[:, lanes(j, rank)], tskel[:, lanes(j, rank)] = got

        grouped(2**d, 16, climb, climb_keep, 2**d - 1)

    def half(v):
        return (v.astype(f32) * 0.5).astype(bf16)

    top_terms = {}
    for d in range(depth, 0, -1):
        mine = pos >> (depth - d)
        other = mine ^ 1
        own_left = feature_pair(half(tskel[:, lanes(2**d - 1 + mine, rank)]))[0]
        sib_right = feature_pair(half(tskel[:, lanes(2**d - 1 + other, rank)]))[1]
        g = gauss(sib_right.T, own_left)
        top_terms[d] = dot(tcoeff[:, lanes(2**d - 1 + other, rank)], g)
    v = jnp.zeros((cols, rank), bf16)
    for d in range(1, depth + 1):
        parent = pos >> (depth - d + 1)
        down = dot(v, tb[2 ** (d - 1) - 1 + parent], 1, 1)
        right = ((pos >> (depth - d)) & 1) == 1
        v = (top_terms[d] + jnp.where(right, down[:, rank:], down[:, :rank])).astype(bf16)
    value[:, lanes(0, rank)] = v
    local_depth = count.bit_length() - 1
    for d in range(1, local_depth + 1):

        def descend(j):
            down = dot(value[:, lanes(j, rank)], nb[j], 1, 1)
            return (terms[:, lanes(2 * j, rank, 2)] + down).astype(bf16)

        def descend_keep(j, got):
            value[:, lanes(2 * j + 1, rank, 2)] = got

        grouped(2 ** (d - 1), 32, descend, descend_keep, 2 ** (d - 1) - 1)
    row = lax.broadcasted_iota(jnp.int32, (cols, leaf), 0)
    scale = jnp.zeros((cols, leaf), f32)
    for r in range(cols):
        scale = jnp.where(row == r, ridge[r], scale)

    def finish(l):
        far = dot(value[:, lanes(count - 1 + l, rank)], lb[l], 1, 1)
        return scale * dt[:, lanes(l, leaf)] + far + acc[l]

    def finish_keep(l, got):
        out[:, lanes(l, leaf)] = got

    grouped(count, 16, finish, finish_keep)


def downward(pos, lst, ridge, gathered, top_pick, x_low, x, w_low, n_own, top_basis, terms, local_basis, leaf_basis,
             dt, after, entries):
    count, leaf, rank = leaf_basis.shape
    dim, cols = x.shape[0], dt.shape[0]
    subtrees = gathered.shape[0]
    big = (top_basis, terms, local_basis, leaf_basis, dt)
    return pl.pallas_call(
        functools.partial(down_kernel, (count, leaf, rank, dim, cols, subtrees, entries)),
        grid_spec=pltpu.PrefetchScalarGridSpec(
            num_scalar_prefetch=3,
            grid=(1,),
            in_specs=[VM] * 2 + [ANY, HBM, ANY] + [HBM] * 7,
            out_specs=VM,
            scratch_shapes=near_scratch(count, entries, leaf, dim, cols)
            + [pltpu.VMEM((dim, count * leaf), bf16), pltpu.VMEM((count + 1, cols, leaf), f32)]
            + [pltpu.VMEM(a.shape, a.dtype) for a in big]
            + [
                pltpu.VMEM((cols, (2 * subtrees - 1) * rank), bf16),
                pltpu.VMEM((dim, (2 * subtrees - 1) * rank), bf16),
                pltpu.VMEM((cols, (2 * count - 1) * rank), bf16),
                pltpu.SemaphoreType.DMA((2, CHUNKS)),
                pltpu.SemaphoreType.DMA((7,)),
            ],
        ),
        out_shape=jax.ShapeDtypeStruct(dt.shape, f32),
        compiler_params=pltpu.CompilerParams(vmem_limit_bytes=52 << 20),
        cost_estimate=near_cost(8 * count, leaf, cols, 20 << 20),
        name="downward",
    )(pos, lst, ridge, gathered, top_pick, x_low, x, w_low, n_own, *big, after)


def shards(points, direction, ridge, leaf_basis, local_basis, top_basis, leaf_pick, local_pick, top_pick, near_list):
    count, leaf, rank = leaf_basis.shape
    entries = near_list.shape[1]
    chips = lax.axis_size("chip")
    subtrees = lax.axis_size("leaf") * chips
    pos = (lax.axis_index("leaf") * chips + lax.axis_index("chip"))[None]
    upper = [(i, i + 1) for i in range(subtrees - 1)]
    lower = [(i + 1, i) for i in range(subtrees - 1)]

    xt, dt, ids = points.T, direction.T, near_list.T
    x_low = lax.ppermute(xt, AXES, upper)
    w = pack(pos, dt, ids)
    w_low = lax.ppermute(w, AXES, upper)
    terms, spread, list_low, n_own, own_list = upward(
        pos, xt, w, ids, leaf_pick, local_pick, leaf_basis, local_basis, subtrees
    )
    gathered = lax.all_to_all(spread, AXES, 0, 0)
    back, n_own = near_back(own_list, x_low, xt, w_low, w, n_own, count, entries, leaf)
    returned = lax.ppermute(back, AXES, lower)
    out = downward(
        pos, list_low, ridge, gathered, top_pick, x_low, xt, w_low, n_own, top_basis, terms, local_basis, leaf_basis,
        dt, back, entries,
    )
    return (out + returned.astype(f32)).T


def solution(mesh):
    split = P(AXES, None)
    split3 = P(AXES, None, None)
    return jax.shard_map(
        shards,
        mesh=mesh,
        in_specs=(split, split, P(), split3, split3, P(), split, split, P(), split),
        out_specs=split,
        check_vma=False,
    )
```

```python
import functools
import math

import jax
import jax.numpy as jnp
from jax import lax
from jax.experimental import pallas as pl
from jax.experimental.pallas import tpu as pltpu
from jax.sharding import PartitionSpec as P

f32 = jnp.float32
bf16 = jnp.bfloat16
AXES = ("leaf", "chip")
SCALE = math.log2(math.e) / 32.0
FEAT = 128
GROUP = 16
EARLY = 5.0


def dot(a, b, ca=1, cb=0):
    return lax.dot_general(a, b, (((ca,), (cb,)), ((), ())), preferred_element_type=f32)


def copy(src, dst, sem):
    c = pltpu.make_async_copy(src, dst, sem)
    c.start()
    return c


def near_cost(pairs, leaf, cols, data):
    return pl.CostEstimate(
        flops=pairs * 2 * leaf * leaf * (2 * FEAT + leaf), transcendentals=pairs * leaf * leaf, bytes_accessed=data
    )


VM = pl.BlockSpec(memory_space=pltpu.VMEM)
HBM = pl.BlockSpec(memory_space=pltpu.HBM)
ANY = pl.BlockSpec(memory_space=pl.ANY)


def square_rows(xf):
    n = jnp.sum(xf * xf, axis=0, keepdims=True)
    hi = n.astype(bf16).astype(f32)
    rest = n - hi
    mid = rest.astype(bf16).astype(f32)
    low = rest - mid
    row = lax.broadcasted_iota(jnp.int32, (16, xf.shape[1]), 0)
    zero = jnp.zeros((), f32)
    neg = jnp.where(row == 0, -hi, jnp.where(row == 1, -mid, jnp.where(row == 2, -low, zero)))
    ones = jnp.where(row < 3, jnp.ones((), f32), zero)
    return neg.astype(bf16), ones.astype(bf16)


def feature_pair(x):
    dim, width = x.shape
    xf = x.astype(f32)
    neg, ones = square_rows(xf)
    pad = jnp.zeros((FEAT - dim - 32, width), bf16)
    left = jnp.concatenate([(xf + xf).astype(bf16), ones, neg, pad], 0)
    right = jnp.concatenate([x, neg, ones, pad], 0)
    return left, right


def swap_form(left, dim):
    half = (left[:dim].astype(f32) * 0.5).astype(bf16)
    return jnp.concatenate([half, left[dim + 16 : dim + 32], left[dim : dim + 16], left[dim + 32 :]], 0)


def selector(pick_row, width):
    rows = lax.broadcasted_iota(jnp.int32, (width, pick_row.shape[1]), 0)
    return jnp.where(rows == pick_row, jnp.ones((), f32), jnp.zeros((), f32)).astype(bf16)


def gauss(right_rows, left_cols):
    s = dot(right_rows, left_cols)
    return jnp.exp2(s * SCALE).astype(bf16)


def grouped(count, group, compute, store, start=0, also=None, carry=0):
    group = min(group, count)

    def body(t, carry):
        got = [compute(start + t * group + u) for u in range(group)]
        for u in range(group):
            store(start + t * group + u, got[u])
            if also is not None:
                carry = also(start + t * group + u, carry)
        return carry

    if count == group:
        return body(0, carry)
    return lax.fori_loop(0, count // group, body, carry)


def lanes(start, width, number=1):
    if isinstance(start, int):
        return pl.ds(start * width, number * width)
    return pl.ds(pl.multiple_of(start * width, width), number * width)


CHUNKS = 4
PAIRS = 16


def class_list(ids, low, count):
    entries = ids.shape[0]
    local = ids - low
    inside = (local >= 0) & (local < count)
    ones = inside.astype(jnp.int32)
    rank = [jnp.zeros_like(ones[0:1])]
    for e in range(entries):
        rank.append(rank[-1] + ones[e : e + 1])
    row = lax.broadcasted_iota(jnp.int32, (16, ids.shape[1]), 0)
    out = jnp.where(row == entries, rank[-1], 0)
    for e in range(entries):
        here = (row == rank[e]) & (ones[e : e + 1] == 1)
        out = out + jnp.where(here, local[e : e + 1], 0)
    return out


def pack_kernel(pos_ref, d_hbm, ids, out, dt, sems):
    cols, width = dt.shape
    count = ids.shape[1]
    part = width // CHUNKS
    gets = [copy(d_hbm.at[:, pl.ds(c * part, part)], dt.at[:, pl.ds(c * part, part)], sems.at[c]) for c in range(CHUNKS)]
    out[:, pl.ds(width, 128)] = jnp.zeros((cols, 128), bf16)
    out[:, pl.ds(width, count)] = class_list(ids[...], (pos_ref[0] + 1) * count, count).astype(f32).astype(bf16)
    for c in range(CHUNKS):
        gets[c].wait()
        s = pl.ds(c * part, part)
        out[:, s] = dt[:, s].astype(bf16)


def pack(pos, dt, ids):
    cols, width = dt.shape
    return pl.pallas_call(
        pack_kernel,
        grid_spec=pltpu.PrefetchScalarGridSpec(
            num_scalar_prefetch=1,
            grid=(1,),
            in_specs=[HBM, VM],
            out_specs=VM,
            scratch_shapes=[pltpu.VMEM(dt.shape, f32), pltpu.SemaphoreType.DMA((CHUNKS,))],
        ),
        out_shape=jax.ShapeDtypeStruct((cols, width + 128), bf16),
        compiler_params=pltpu.CompilerParams(vmem_limit_bytes=60 << 20),
        name="pack",
    )(pos, dt, ids)


def up_kernel(dims, pos_ref, x_hbm, w_hbm, ids, leaf_pick, local_pick, leaf_hbm, local_hbm,
              terms_hbm, spread, list_low, acc, pair,
              big, at, b, wt, xt, terms, lb, nb, coeff, skel, tiles, lv, lst, xs, ls, ms):
    count, leaf, rank, dim, cols = dims
    entries = ids.shape[0]
    part = count // CHUNKS
    seg = lambda c: pl.ds(c * part * leaf, part * leaf)
    own = lambda c: pl.ds(c * part, part)
    get_x = [copy(x_hbm.at[:, seg(c)], xt.at[:, seg(c)], xs.at[c]) for c in range(CHUNKS)]
    get_w = copy(w_hbm, wt, ms.at[0])
    pos = pos_ref[0]
    table = ids[...]
    put_list = put_class(table, pos * count, count, lv, lst, ms.at[3])
    list_low[...] = class_list(table, (pos - 1) * count, count)
    acc[...] = jnp.zeros_like(acc)

    def prepare(l):
        left, right = feature_pair(xt[:, lanes(l, leaf)])
        return left, right.T

    def keep(l, got):
        at[l], b[l] = got

    total = 0
    for c in range(CHUNKS):
        get_x[c].wait()
        if c == 0:
            put_list.wait()
        if c == 1:
            get_leaf = [copy(leaf_hbm.at[own(k)], lb.at[own(k)], ls.at[k]) for k in range(CHUNKS)]
            get_local = copy(local_hbm, nb, ms.at[1])
        total = grouped(part, 16, prepare, keep, c * part, scan_leaf(count, entries, lst, pair), total)
    end_list(count, pair, total)
    get_w.wait()
    base = count - 1

    def leaf_step(l):
        c = dot(wt[:, lanes(l, leaf)], lb[l])
        sel = selector(leaf_pick[pl.ds(l, 1), :], leaf)
        return c.astype(bf16), dot(at[l], sel).astype(bf16)

    def leaf_keep(l, got):
        coeff[:, lanes(base + l, rank)], skel[:, lanes(base + l, rank)] = got

    for c in range(CHUNKS):
        get_leaf[c].wait()
        grouped(part, 16, leaf_step, leaf_keep, c * part)
    get_local.wait()
    depth = count.bit_length() - 1
    for d in range(depth, 0, -1):
        up = 2 ** (d - 1) - 1

        def climb(j):
            both = lanes(2 * j + 1, rank, 2)
            sel = selector(local_pick[pl.ds(j, 1), :], 2 * rank)
            return dot(coeff[:, both], nb[j]).astype(bf16), dot(skel[:, both], sel).astype(bf16)

        def climb_keep(j, got):
            coeff[:, lanes(j, rank)], skel[:, lanes(j, rank)] = got

        grouped(2 ** (d - 1), 32, climb, climb_keep, up)
    root_c, root_s = coeff[:, :rank], skel[:dim, :rank]
    for s in range(spread.shape[0]):
        spread[s, :cols, :] = root_c
        spread[s, cols:, :] = root_s

    last = count - 2

    def index(j):
        return min(j, last) if isinstance(j, int) else jnp.minimum(j, last)

    def first(j, slot):
        both = skel[:, lanes(2 * index(j) + 1, rank, 2)]
        tiles[slot] = gauss(swap_form(both[:, rank:], dim).T, both[:, :rank])

    def second(j, slot):
        c2 = coeff[:, lanes(2 * index(j) + 1, rank, 2)]
        g = tiles[slot]
        return jnp.concatenate([dot(c2[:, rank:], g), dot(c2[:, :rank], g, 1, 1)], 1)

    for u in range(PAIRS):
        first(u, u)

    def body(t, carry):
        for phase in range(2):
            k = (2 * t + phase) * PAIRS
            got = []
            for u in range(PAIRS):
                first(k + PAIRS + u, (1 - phase) * PAIRS + u)
                got.append(second(k + u, phase * PAIRS + u))
            for u in range(PAIRS):
                terms[:, lanes(2 * index(k + u), rank, 2)] = got[u]
        return carry

    lax.fori_loop(0, count // (2 * PAIRS), body, 0)
    put_terms = copy(terms, terms_hbm, ms.at[2])
    pair[pair.shape[0] - 1] = total
    near_pairs(count, jnp.minimum(total, early_pairs(count)), pair, at, b, wt, acc, big)
    put_terms.wait()


def put_class(table, low, count, lv, lst, sem):
    lv[...] = jnp.zeros_like(lv)
    lv[:, :count] = class_list(table, low, count)
    return copy(lv, lst, sem)


def upward(pos, xt, w, ids, leaf_pick, local_pick, leaf_basis, local_basis, subtrees):
    count, leaf, rank = leaf_basis.shape
    dim, cols = xt.shape[0], w.shape[0]
    entries = ids.shape[0]
    return pl.pallas_call(
        functools.partial(up_kernel, (count, leaf, rank, dim, cols)),
        grid_spec=pltpu.PrefetchScalarGridSpec(
            num_scalar_prefetch=1,
            grid=(1,),
            in_specs=[HBM, HBM, VM, VM, VM, HBM, HBM],
            out_specs=[HBM, VM, VM, VM, pl.BlockSpec(memory_space=pltpu.SMEM)],
            scratch_shapes=near_scratch(count, entries, leaf, dim, cols)[1:]
            + [
                pltpu.VMEM((cols, (2 * count - 2) * rank), f32),
                pltpu.VMEM(leaf_basis.shape, bf16),
                pltpu.VMEM(local_basis.shape, bf16),
                pltpu.VMEM((cols, (2 * count - 1) * rank), bf16),
                pltpu.VMEM((FEAT, (2 * count - 1) * rank), bf16),
                pltpu.VMEM((2 * PAIRS, rank, rank), bf16),
                pltpu.VMEM((16, 128), jnp.int32),
                pltpu.SMEM((16, 128), jnp.int32),
                pltpu.SemaphoreType.DMA((CHUNKS,)),
                pltpu.SemaphoreType.DMA((CHUNKS,)),
                pltpu.SemaphoreType.DMA((4,)),
            ],
        ),
        out_shape=[
            jax.ShapeDtypeStruct((cols, (2 * count - 2) * rank), f32),
            jax.ShapeDtypeStruct((subtrees, cols + dim, rank), bf16),
            jax.ShapeDtypeStruct((16, count), jnp.int32),
            jax.ShapeDtypeStruct((count + 1, cols, leaf), f32),
            jax.ShapeDtypeStruct((pair_slots(count, entries) + 1,), jnp.int32),
        ],
        compiler_params=pltpu.CompilerParams(vmem_limit_bytes=60 << 20),
        cost_estimate=near_cost(12 * count, leaf, cols, 16 << 20),
        name="upward",
    )(pos, xt, w, ids, leaf_pick, local_pick, leaf_basis, local_basis)


def scan_leaf(count, entries, lst, pair):
    def scan(i, pos):
        for e in range(entries):
            pair[pos + e] = i * count + lst[e, i]
        return pos + lst[entries, i]

    return scan


def end_list(count, pair, total):
    for u in range(3 * GROUP):
        pair[total + u] = count * count


def early_pairs(count):
    return int(EARLY * count) // (2 * GROUP) * 2 * GROUP


def near_pairs(count, total, pair, at, b, w, acc, tiles, begin=0):
    h = GROUP
    leaf = b.shape[1]
    shift = count.bit_length() - 1

    def first(k, slot):
        code = pair[begin + k]
        tiles[slot] = gauss(b[code & (count - 1)], at[(code >> shift) & (count - 1)])

    def second(k, slot):
        code = pair[begin + k]
        return code >> shift, dot(w[:, lanes(code & (count - 1), leaf)], tiles[slot])

    for u in range(h):
        first(u, u)

    def body(t, carry):
        for phase in range(2):
            k = (2 * t + phase) * h
            got = []
            for u in range(h):
                first(k + h + u, (1 - phase) * h + u)
                got.append(second(k + u, phase * h + u))
            for i, o in got:
                acc[i] += o
        return carry

    blocks = (total - begin + h - 1) // h
    lax.fori_loop(0, (blocks + 1) // 2, body, 0)


def pair_slots(count, entries):
    return count * entries + entries + 4 * GROUP


def near_scratch(count, entries, leaf, dim, cols):
    return [
        pltpu.SMEM((pair_slots(count, entries),), jnp.int32),
        pltpu.VMEM((2 * GROUP, leaf, leaf), bf16),
        pltpu.VMEM((count, FEAT, leaf), bf16),
        pltpu.VMEM((count, leaf, FEAT), bf16),
        pltpu.VMEM((cols, count * leaf + 128), bf16),
        pltpu.VMEM((dim, count * leaf), bf16),
    ]


def two_sided(count, leaf, target_hbm, source_hbm, x, y, at, b, xs):
    part = count // CHUNKS
    seg = lambda c: pl.ds(c * part * leaf, part * leaf)
    gets = []
    for c in range(CHUNKS):
        gets.append(copy(source_hbm.at[:, seg(c)], y.at[:, seg(c)], xs.at[1, c]))
        gets.append(copy(target_hbm.at[:, seg(c)], x.at[:, seg(c)], xs.at[0, c]))

    def finish(also):
        def prepare(l):
            return feature_pair(x[:, lanes(l, leaf)])[0], feature_pair(y[:, lanes(l, leaf)])[1].T

        def keep(l, got):
            at[l], b[l] = got

        total = 0
        for c in range(CHUNKS):
            gets[2 * c].wait()
            gets[2 * c + 1].wait()
            total = grouped(part, 16, prepare, keep, c * part, also, total)
        return total

    return finish


def near_back_kernel(entries, left_over, low_hbm, x_hbm, wlow_hbm, w_hbm, own_hbm, out, own,
                     pair, tiles, at, b, w, x, y, acc, lf, lv, lst, xs, sems):
    count, _, leaf = at.shape
    get_list = copy(wlow_hbm.at[:, pl.ds(count * leaf, 128)], lf, sems.at[0])
    finish = two_sided(count, leaf, low_hbm, x_hbm, x, y, at, b, xs)
    get_w = copy(w_hbm, w, sems.at[1])
    get_own = copy(own_hbm, own, sems.at[3])
    get_list.wait()
    lv[...] = lf[...].astype(f32).astype(jnp.int32)
    put_list = copy(lv, lst, sems.at[2])
    acc[...] = jnp.zeros_like(acc)
    put_list.wait()
    total = finish(scan_leaf(count, entries, lst, pair))
    end_list(count, pair, total)
    get_w.wait()
    near_pairs(count, total, pair, at, b, w, acc, tiles)

    def store(l, got):
        out[:, lanes(l, leaf)] = got.astype(out.dtype)

    grouped(count, 8, lambda l: acc[l], store)
    get_own.wait()
    all_own = left_over[left_over.shape[0] - 1]

    @pl.when(all_own > early_pairs(count))
    def _():
        def keep(l, got):
            at[l] = got

        grouped(count, 16, lambda l: feature_pair(y[:, lanes(l, leaf)])[0], keep)
        near_pairs(count, all_own, left_over, at, b, w, own, tiles, early_pairs(count))


def near_back(left_over, x_low, x, w_low, w, n_own, count, entries, leaf):
    dim, cols = x.shape[0], w.shape[0]
    return pl.pallas_call(
        functools.partial(near_back_kernel, entries),
        grid_spec=pltpu.PrefetchScalarGridSpec(
            num_scalar_prefetch=1,
            grid=(1,),
            in_specs=[ANY, HBM, ANY, HBM, HBM],
            out_specs=[VM, VM],
            scratch_shapes=near_scratch(count, entries, leaf, dim, cols)
            + [
                pltpu.VMEM((dim, count * leaf), bf16),
                pltpu.VMEM((count + 1, cols, leaf), f32),
                pltpu.VMEM((cols, 128), bf16),
                pltpu.VMEM((cols, 128), jnp.int32),
                pltpu.SMEM((cols, 128), jnp.int32),
                pltpu.SemaphoreType.DMA((2, CHUNKS)),
                pltpu.SemaphoreType.DMA((4,)),
            ],
        ),
        out_shape=[
            jax.ShapeDtypeStruct((cols, count * leaf), bf16),
            jax.ShapeDtypeStruct((count + 1, cols, leaf), f32),
        ],
        compiler_params=pltpu.CompilerParams(vmem_limit_bytes=52 << 20),
        cost_estimate=near_cost(4 * count, leaf, cols, 6 << 20),
        name="near_back",
    )(left_over, x_low, x, w_low, w, n_own)


def down_kernel(dims, pos_ref, lst, ridge, gathered, top_pick, low_hbm, x_hbm, wlow_hbm, own_hbm,
                top_hbm, terms_hbm, local_hbm, leaf_hbm, d_hbm, after, out,
                pair, tiles, at, b, w, x, y, acc, tb, terms, nb, lb, dt, tcoeff, tskel, value, xs, sems):
    count, leaf, rank, dim, cols, subtrees, entries = dims
    finish_features = two_sided(count, leaf, x_hbm, low_hbm, x, y, at, b, xs)
    get_w = copy(wlow_hbm, w, sems.at[0])
    get_acc = copy(own_hbm, acc, sems.at[1])
    pairs = ((top_hbm, tb), (terms_hbm, terms), (local_hbm, nb), (leaf_hbm, lb), (d_hbm, dt))
    total = finish_features(scan_leaf(count, entries, lst, pair))
    end_list(count, pair, total)
    gets = [copy(src, dst, sems.at[k + 2]) for k, (src, dst) in enumerate(pairs)]
    get_w.wait()
    get_acc.wait()
    near_pairs(count, total, pair, at, b, w, acc, tiles)

    pos = pos_ref[0]
    depth = subtrees.bit_length() - 1
    for s in range(subtrees):
        tcoeff[:, lanes(subtrees - 1 + s, rank)] = gathered[s, :cols]
        tskel[:, lanes(subtrees - 1 + s, rank)] = gathered[s, cols:]
    for g in gets:
        g.wait()
    for d in range(depth - 1, 0, -1):

        def climb(j):
            both = lanes(2 * j + 1, rank, 2)
            sel = selector(top_pick[pl.ds(j, 1), :], 2 * rank)
            return dot(tcoeff[:, both], tb[j]).astype(bf16), dot(tskel[:, both], sel).astype(bf16)

        def climb_keep(j, got):
            tcoeff[:, lanes(j, rank)], tskel[:, lanes(j, rank)] = got

        grouped(2**d, 16, climb, climb_keep, 2**d - 1)

    def half(v):
        return (v.astype(f32) * 0.5).astype(bf16)

    top_terms = {}
    for d in range(depth, 0, -1):
        mine = pos >> (depth - d)
        other = mine ^ 1
        own_left = feature_pair(half(tskel[:, lanes(2**d - 1 + mine, rank)]))[0]
        sib_right = feature_pair(half(tskel[:, lanes(2**d - 1 + other, rank)]))[1]
        g = gauss(sib_right.T, own_left)
        top_terms[d] = dot(tcoeff[:, lanes(2**d - 1 + other, rank)], g)
    v = jnp.zeros((cols, rank), bf16)
    for d in range(1, depth + 1):
        parent = pos >> (depth - d + 1)
        down = dot(v, tb[2 ** (d - 1) - 1 + parent], 1, 1)
        right = ((pos >> (depth - d)) & 1) == 1
        v = (top_terms[d] + jnp.where(right, down[:, rank:], down[:, :rank])).astype(bf16)
    value[:, lanes(0, rank)] = v
    local_depth = count.bit_length() - 1
    for d in range(1, local_depth + 1):

        def descend(j):
            down = dot(value[:, lanes(j, rank)], nb[j], 1, 1)
            return (terms[:, lanes(2 * j, rank, 2)] + down).astype(bf16)

        def descend_keep(j, got):
            value[:, lanes(2 * j + 1, rank, 2)] = got

        grouped(2 ** (d - 1), 32, descend, descend_keep, 2 ** (d - 1) - 1)
    row = lax.broadcasted_iota(jnp.int32, (cols, leaf), 0)
    scale = jnp.zeros((cols, leaf), f32)
    for r in range(cols):
        scale = jnp.where(row == r, ridge[r], scale)

    def finish(l):
        far = dot(value[:, lanes(count - 1 + l, rank)], lb[l], 1, 1)
        return scale * dt[:, lanes(l, leaf)] + far + acc[l]

    def finish_keep(l, got):
        out[:, lanes(l, leaf)] = got

    grouped(count, 16, finish, finish_keep)


def downward(pos, lst, ridge, gathered, top_pick, x_low, x, w_low, n_own, top_basis, terms, local_basis, leaf_basis,
             dt, after, entries):
    count, leaf, rank = leaf_basis.shape
    dim, cols = x.shape[0], dt.shape[0]
    subtrees = gathered.shape[0]
    big = (top_basis, terms, local_basis, leaf_basis, dt)
    return pl.pallas_call(
        functools.partial(down_kernel, (count, leaf, rank, dim, cols, subtrees, entries)),
        grid_spec=pltpu.PrefetchScalarGridSpec(
            num_scalar_prefetch=3,
            grid=(1,),
            in_specs=[VM] * 2 + [ANY, HBM, ANY] + [HBM] * 7,
            out_specs=VM,
            scratch_shapes=near_scratch(count, entries, leaf, dim, cols)
            + [pltpu.VMEM((dim, count * leaf), bf16), pltpu.VMEM((count + 1, cols, leaf), f32)]
            + [pltpu.VMEM(a.shape, a.dtype) for a in big]
            + [
                pltpu.VMEM((cols, (2 * subtrees - 1) * rank), bf16),
                pltpu.VMEM((dim, (2 * subtrees - 1) * rank), bf16),
                pltpu.VMEM((cols, (2 * count - 1) * rank), bf16),
                pltpu.SemaphoreType.DMA((2, CHUNKS)),
                pltpu.SemaphoreType.DMA((7,)),
            ],
        ),
        out_shape=jax.ShapeDtypeStruct(dt.shape, f32),
        compiler_params=pltpu.CompilerParams(vmem_limit_bytes=52 << 20),
        cost_estimate=near_cost(8 * count, leaf, cols, 20 << 20),
        name="downward",
    )(pos, lst, ridge, gathered, top_pick, x_low, x, w_low, n_own, *big, after)


def shards(points, direction, ridge, leaf_basis, local_basis, top_basis, leaf_pick, local_pick, top_pick, near_list):
    count, leaf, rank = leaf_basis.shape
    entries = near_list.shape[1]
    chips = lax.axis_size("chip")
    subtrees = lax.axis_size("leaf") * chips
    pos = (lax.axis_index("leaf") * chips + lax.axis_index("chip"))[None]
    upper = [(i, i + 1) for i in range(subtrees - 1)]
    lower = [(i + 1, i) for i in range(subtrees - 1)]

    xt, dt, ids = points.T, direction.T, near_list.T
    x_low = lax.ppermute(xt, AXES, upper)
    w = pack(pos, dt, ids)
    w_low = lax.ppermute(w, AXES, upper)
    terms, spread, list_low, n_own, own_list = upward(
        pos, xt, w, ids, leaf_pick, local_pick, leaf_basis, local_basis, subtrees
    )
    gathered = lax.all_to_all(spread, AXES, 0, 0)
    back, n_own = near_back(own_list, x_low, xt, w_low, w, n_own, count, entries, leaf)
    returned = lax.ppermute(back, AXES, lower)
    out = downward(
        pos, list_low, ridge, gathered, top_pick, x_low, xt, w_low, n_own, top_basis, terms, local_basis, leaf_basis,
        dt, back, entries,
    )
    return (out + returned.astype(f32)).T


def solution(mesh):
    split = P(AXES, None)
    split3 = P(AXES, None, None)
    return jax.shard_map(
        shards,
        mesh=mesh,
        in_specs=(split, split, P(), split3, split3, P(), split, split, P(), split),
        out_specs=split,
        check_vma=False,
    )
```
